32 devices in a mesh: lat: 2 (over core), lon: 16 (over z, y, x).
Axes of the slice: x: 2, y: 2, z: 4, core: 2. Of those that a mesh axis runs over, the one named last changes fastest.
Arguments:
- stream: bfloat16 [32, 256, 256], P('lat', 'lon'), may hold values from -6 to 6
- gains: float32 [2, 2, 256], replicated, may hold values from 0.5 to 1.5
- w_qkv: bfloat16 [2, 256, 768], replicated, may hold values from -8 to 8
- table: float32 [2, 4, 13, 7], replicated, may hold values from -4 to 4
- w_out: bfloat16 [2, 256, 256], replicated, may hold values from -0.375 to 0.375
- w_up: bfloat16 [2, 256, 768], replicated, may hold values from -0.375 to 0.375
- kernel: float32 [2, 3, 3, 768], replicated, may hold values from -2 to 2
- w_down: bfloat16 [2, 768, 256], replicated, may hold values from -0.21875 to 0.21875
Outputs:
- result: bfloat16 [32, 256, 256], P('lat', 'lon')
The draws below stay inside these ranges and needn't reach their ends.
All inputs are finite; a program needn't handle non-finite values.
Results may differ from the reference program's by a relative error of at most 0.013.
Values may be sent and summed in bfloat16 or wider, within the bound.
A program may use at most 64 MiB of HBM per device.

```python
import jax
import jax.numpy as jnp
from jax import lax

D = 256
HEADS = 4
FF = 768
WINDOW = 7
LAYERS = 2
CLAT = 16
NLAT = 32
NLON = 256
N_LAT = 2


def draw_w_qkv(key, part):
    spread = D ** (-0.5)
    base = jnp.clip(jax.random.normal(key, (LAYERS, D, 3 * D), jnp.float32) * spread, -4.0 * spread, 4.0 * spread)
    return jnp.clip(base, -8.0, 8.0).astype(jnp.bfloat16)


def block_levels(rng, shape, split, low, high):
    def one(position, blocks):
        draws = jax.random.uniform(jax.random.fold_in(jax.random.fold_in(rng, 6), position), (blocks,), jnp.float32, low / len(split), high / len(split))
        return jnp.repeat(jnp.exp(draws), shape[position] // blocks).reshape((-1,) + (1,) * (len(shape) - position - 1))

    loudness = one(*split[0])
    for cut in split[1:]:
        loudness = loudness * one(*cut)
    return loudness


def bell_draw(own_key, extent, scale, bound, split=(), kind=jnp.bfloat16):
    entries = scale * jax.random.normal(own_key, extent, jnp.float32)
    if split:
        entries = entries * block_levels(own_key, extent, split, -0.22, 0.18)
    return jnp.clip(entries, -bound, bound).astype(kind)


def setup_inputs(seed: int = 0) -> dict:
    streams_of = jax.random.split(jax.random.key(seed), 9)
    stream = bell_draw(streams_of[0], (NLAT, NLON, D), 1.0, 6.0, ((0, 2), (1, 16)))
    gains = jnp.clip(jax.random.uniform(streams_of[1], (LAYERS, 2, D), jnp.float32, 0.5, 1.5), 0.5, 1.5)
    w_qkv = draw_w_qkv(jax.random.fold_in(streams_of[8], 71), 0)
    table = bell_draw(streams_of[3], (LAYERS, HEADS, 2 * WINDOW - 1, WINDOW), 1.0, 4.0, (), jnp.float32)
    w_out = bell_draw(streams_of[4], (LAYERS, D, D), D ** -0.5, 0.375)
    w_up = bell_draw(streams_of[5], (LAYERS, D, FF), D ** -0.5, 0.375)
    kernel = bell_draw(streams_of[6], (LAYERS, 3, 3, FF), 9 ** -0.5, 2.0, (), jnp.float32)
    w_down = bell_draw(streams_of[7], (LAYERS, FF, D), FF ** -0.5, 0.21875)
    return {"stream": stream, "gains": gains, "w_qkv": w_qkv, "table": table, "w_out": w_out, "w_up": w_up, "kernel": kernel, "w_down": w_down}


def rms_normed(wide, gain):
    scale = lax.rsqrt(lax.optimization_barrier(jnp.mean(wide * wide, axis=-1, keepdims=True)) + 1e-06)
    return (wide * scale * gain).astype(jnp.bfloat16)

def make_tiles(source, n_rows, n_cols, side, row_span, col_span, heads, head_size):
    width = source.shape[2]
    source = jnp.pad(source, ((0, (n_rows + 2) * side - source.shape[0]), (0, (n_cols + 1) * side - source.shape[1]), (0, 0)))
    blocks = source.reshape(n_rows + 2, side, (n_cols + 1) * side, width)
    rowed = jnp.concatenate([blocks[:n_rows], blocks[1:n_rows + 1], blocks[2:, :row_span - 2 * side]], axis=1)
    blocks = rowed.reshape(n_rows, row_span, n_cols + 1, side, width)
    both = jnp.concatenate([blocks[:, :, :-1], blocks[:, :, 1:, :col_span - side]], axis=3)
    return both.reshape(n_rows, row_span, n_cols, col_span, heads, head_size)

def neighbour_attention(query, keys, values, first_row, total_rows, bias_table):
    reach = WINDOW // 2
    row_reach = WINDOW - 1
    extra = row_reach - reach
    side = 8
    col_span = side + 2 * reach
    row_span = side + 2 * row_reach
    q_rows, q_cols, width = query.shape
    heads = bias_table.shape[0]
    head_size = width // heads
    n_rows = (q_rows + side - 1) // side
    n_cols = (q_cols + side - 1) // side
    keys = jnp.pad(keys, ((extra, extra), (0, 0), (0, 0)))
    values = jnp.pad(values, ((extra, extra), (0, 0), (0, 0)))
    query = jnp.pad(query, ((0, n_rows * side - q_rows), (0, n_cols * side - q_cols), (0, 0)))
    query_tiles = query.reshape(n_rows, side, n_cols, side, heads, head_size).astype(jnp.float32)
    key_tiles = make_tiles(keys, n_rows, n_cols, side, row_span, col_span, heads, head_size).astype(jnp.float32)
    value_tiles = make_tiles(values, n_rows, n_cols, side, row_span, col_span, heads, head_size).astype(jnp.float32)
    scores = jnp.einsum('aibjhd,apbuhd->abhijpu', query_tiles, key_tiles)
    inner = jnp.arange(side, dtype=jnp.int32)
    outer_rows = jnp.arange(row_span, dtype=jnp.int32)
    outer_cols = jnp.arange(col_span, dtype=jnp.int32)
    row_hot = (outer_rows[None, :, None] - inner[:, None, None] == jnp.arange(2 * WINDOW - 1, dtype=jnp.int32)[None, None, :]).astype(jnp.float32)
    col_hot = (outer_cols[None, :, None] - inner[:, None, None] == jnp.arange(WINDOW, dtype=jnp.int32)[None, None, :]).astype(jnp.float32)
    bias = jnp.einsum('hrc,ipr,juc->hijpu', bias_table, row_hot, col_hot, precision=lax.Precision.HIGHEST)
    tile_rows = first_row + jnp.arange(n_rows, dtype=jnp.int32) * side
    query_rows = tile_rows[:, None] + inner[None, :]
    start = jnp.clip(query_rows - reach, 0, total_rows - WINDOW)
    key_rows = tile_rows[:, None, None] + outer_rows[None, None, :] - row_reach
    row_ok = (key_rows >= start[:, :, None]) & (key_rows < start[:, :, None] + WINDOW)
    offset = outer_cols[None, :] - reach - inner[:, None]
    col_ok = (offset >= -reach) & (offset <= reach)
    allowed = row_ok[:, None, None, :, None, :, None] & col_ok[None, None, None, None, :, None, :]
    scores = scores * head_size ** (-0.5) + bias[None, None]
    scores = jnp.where(allowed, scores, -1000000000.0)
    flat = scores.reshape(n_rows, n_cols, heads, side, side, row_span * col_span)
    peak = lax.optimization_barrier(jnp.max(flat, axis=-1, keepdims=True))
    raised = jnp.exp(flat - peak)
    weights = (raised / lax.optimization_barrier(jnp.sum(raised, axis=-1, keepdims=True))).astype(jnp.bfloat16)
    weights = weights.reshape(n_rows, n_cols, heads, side, side, row_span, col_span).astype(jnp.float32)
    output = jnp.einsum('abhijpu,apbuhd->aibjhd', weights, value_tiles)
    output = output.reshape(n_rows * side, n_cols * side, width)[:q_rows, :q_cols]
    return output.astype(jnp.bfloat16)

def depthwise(padded, weights):
    rows = padded.shape[0] - 2
    cols = padded.shape[1] - 2
    total = jnp.zeros((rows, cols, padded.shape[2]), jnp.float32)
    for first in range(3):
        for second in range(3):
            total = total + weights[first, second] * padded[first:first + rows, second:second + cols].astype(jnp.float32)
    return total

def reference(stream, gains, w_qkv, table, w_out, w_up, kernel, w_down):
    reach = WINDOW // 2
    current = stream
    for layer in range(LAYERS):
        wide = current.astype(jnp.float32)
        normed = rms_normed(wide, gains[layer, 0])
        mixed = jnp.dot(normed, w_qkv[layer], preferred_element_type=jnp.float32).astype(jnp.bfloat16)
        query = mixed[..., :D]
        paired = mixed[..., D:]
        paired = jnp.concatenate([paired[:, -reach:], paired, paired[:, :reach]], axis=1)
        paired = jnp.pad(paired, ((reach, reach), (0, 0), (0, 0)))
        bias_table = table[layer]

        def band(index):
            start = index * CLAT
            band_query = lax.dynamic_slice_in_dim(query, start, CLAT, 0)
            band_pair = lax.dynamic_slice_in_dim(paired, start, CLAT + 2 * reach, 0)
            return neighbour_attention(band_query, band_pair[..., :D], band_pair[..., D:], start, NLAT, bias_table)
        attended = lax.map(band, jnp.arange(N_LAT, dtype=jnp.int32)).reshape(NLAT, NLON, D)
        after = wide + jnp.dot(attended, w_out[layer], preferred_element_type=jnp.float32)
        normed = rms_normed(after, gains[layer, 1])
        lifted = jnp.dot(normed, w_up[layer], preferred_element_type=jnp.float32).astype(jnp.bfloat16)
        lifted = jnp.concatenate([lifted[:, -1:], lifted, lifted[:, :1]], axis=1)
        lifted = jnp.pad(lifted, ((1, 1), (0, 0), (0, 0)))
        hidden = jax.nn.gelu(depthwise(lifted, kernel[layer]), approximate=True).astype(jnp.bfloat16)
        current = (after + jnp.dot(hidden, w_down[layer], preferred_element_type=jnp.float32)).astype(jnp.bfloat16)
    return current
```

```python
import functools

import jax
import jax.numpy as jnp
from jax import lax
from jax.experimental import pallas as pl
from jax.experimental.pallas import tpu as pltpu
from jax.sharding import PartitionSpec as P

WINDOW = 7
REACH = 3
GROUP = 4
F32 = jnp.float32
BF16 = jnp.bfloat16

LEFT, RIGHT, TOP, BOTTOM, TOP_L, TOP_R, BOT_L, BOT_R = range(8)
STEPS = ((0, 1), (0, -1), (1, 0), (-1, 0), (1, 1), (1, -1), (-1, 1), (-1, -1))


def iota(shape, dim):
    return lax.broadcasted_iota(jnp.int32, shape, dim)


def hot(cond):
    return jnp.where(cond, 1.0, 0.0).astype(BF16)


def dot(a, b):
    return jnp.dot(a, b, preferred_element_type=F32)


def normed(wide, gain):
    scale = lax.rsqrt(jnp.mean(wide * wide, axis=-1, keepdims=True) + 1e-06)
    return (wide * scale * gain).astype(BF16)


def kernel(
    n_lat, n_lon, x_hbm, gains_hbm, table_hbm, conv_hbm, wqkv_hbm, wout_hbm, wup_hbm, wdown_hbm,
    out_ref, gains_ref, table, conv_ref, wqkv, wout, wup, wdown, kvb, near_l, near_r, xb, left, right, edge, lpad, pre, rows, spread,
    bias, row_bias, attn, in_sem, w_sem, send_sem, recv_sem,
):
    layers = wqkv.shape[0]
    tokens, width = x_hbm.shape
    cols = 16
    heads = table.shape[2]
    hid = wup.shape[2]
    lat = lax.axis_index("lat")
    lon = lax.axis_index("lon")
    has_up = lat > 0
    has_down = lat < n_lat - 1
    total_rows = n_lat * (tokens // cols)
    first_row = lat * (tokens // cols)

    loads = {}
    firsts = (("x", x_hbm, xb.at[0, pl.ds(64, 256)]), ("gains", gains_hbm, gains_ref), ("table", table_hbm, table), ("conv", conv_hbm, conv_ref))
    for k, (name, src, dst) in enumerate(firsts):
        loads[name] = pltpu.make_async_copy(src, dst, in_sem.at[k])
    loads["x"].start()
    loads["gains"].start()
    for n in range(layers):
        pairs = ((wqkv_hbm, wqkv), (wout_hbm, wout), (wup_hbm, wup), (wdown_hbm, wdown))
        for k, (src, dst) in enumerate(pairs):
            loads[n, k] = pltpu.make_async_copy(src.at[n], dst.at[n], w_sem.at[n, k])
            loads[n, k].start()
            if n == 0 and k == 0:
                loads["table"].start()
                loads["conv"].start()

    def target(step):
        return {"lat": lat + step[0], "lon": lax.rem(lon + step[1] + n_lon, n_lon)}

    def when_to(step, go):
        if step[0] == 0:
            go()
        else:
            pl.when(has_down if step[0] > 0 else has_up)(go)

    def when_from(step, go):
        when_to((-step[0], -step[1]), go)

    barrier = pltpu.get_barrier_semaphore()
    for step in STEPS:
        when_to(
            step,
            lambda step=step: pl.semaphore_signal(
                barrier, inc=1, device_id=target(step), device_id_type=pl.DeviceIdType.MESH
            ),
        )

    def remote(n, slot):
        own, lo, ro, ed = xb.at[n], left.at[n], right.at[n], edge.at[n]
        src, dst = (
            (ed.at[pl.ds(64, 64)], lo.at[pl.ds(16, 64)]),
            (ed.at[pl.ds(0, 64)], ro.at[pl.ds(16, 64)]),
            (own.at[pl.ds(256, 64)], own.at[pl.ds(0, 64)]),
            (own.at[pl.ds(64, 64)], own.at[pl.ds(320, 64)]),
            (ed.at[pl.ds(112, 16)], lo.at[pl.ds(0, 16)]),
            (ed.at[pl.ds(48, 16)], ro.at[pl.ds(0, 16)]),
            (ed.at[pl.ds(64, 16)], lo.at[pl.ds(80, 16)]),
            (ed.at[pl.ds(0, 16)], ro.at[pl.ds(80, 16)]),
        )[slot]
        return pltpu.make_async_remote_copy(
            src_ref=src,
            dst_ref=dst,
            send_sem=send_sem.at[n, slot],
            recv_sem=recv_sem.at[n, slot],
            device_id=target(STEPS[slot]),
            device_id_type=pl.DeviceIdType.MESH,
        )

    def send(n):
        for slot, step in enumerate(STEPS):
            when_to(step, lambda slot=slot: remote(n, slot).start())

    def receive(n):
        for slot, step in enumerate(STEPS):
            when_from(step, lambda slot=slot: remote(n, slot).wait_recv())

    @pl.when(jnp.logical_not(has_up))
    def _():
        for n in range(layers):
            xb[n, 0:64] = jnp.zeros((64, width), BF16)
            left[n, 0:16] = jnp.zeros((16, width), BF16)
            right[n, 0:16] = jnp.zeros((16, width), BF16)
        attn[320:352] = jnp.zeros((32, width), BF16)

    @pl.when(jnp.logical_not(has_down))
    def _():
        for n in range(layers):
            xb[n, 320:384] = jnp.zeros((64, width), BF16)
            left[n, 80:96] = jnp.zeros((16, width), BF16)
            right[n, 80:96] = jnp.zeros((16, width), BF16)
        attn[352:384] = jnp.zeros((32, width), BF16)

    lpad[0:16] = jnp.zeros((16, hid), F32)
    lpad[272:288] = jnp.zeros((16, hid), F32)

    m, t = iota((128, tokens), 0), iota((128, tokens), 1)
    pick_kv = hot(t == ((m & 63) >> 2) * cols + (m & 3) + jnp.where(m >= 64, cols - 4, 0))
    m, t = iota((128, 320), 0), iota((128, 320), 1)
    e = m & 31
    side = 4 * (4 * (m >> 4) + (m & 3) + 4)
    flank = jnp.where((m & 15) < 4, 128 + side + 3, jnp.where((m & 15) < 8, 224 + side, -1))
    above = jnp.where(e < 16, 48 + e, jnp.where(e == 16, 143, jnp.where(e == 17, 236, -1)))
    below = jnp.where(e < 16, 64 + e, jnp.where(e == 16, 211, jnp.where(e == 17, 304, -1)))
    pick_ring = hot(t == jnp.where(m < 64, flank, jnp.where(m < 96, above, below)))
    m, t = iota((32, 64), 0), iota((32, 64), 1)
    pick_side = hot(t == ((m & 15) >> 2) * 16 + (m & 3) + jnp.where(m < 16, 0, 4))
    t, k = iota((tokens, 64), 0), iota((tokens, 64), 1)
    place = hot(((k & 15) == (t >> 4)) & ((t & 15) == jnp.where(k < 32, 0, cols - 1)))
    head_of = iota((1, width), 1) >> 6
    head_hot = [hot(head_of == h) for h in range(heads)]

    def prepare(pick):
        for at in (0, 128):
            for b in range(WINDOW):
                spread[b, :, at : at + 128] = jnp.take_along_axis(
                    rows[b], pick[:, at : at + 128], axis=1
                )

    def chosen(row, offset):
        value = jnp.broadcast_to(spread[0, row : row + 1, :], offset.shape)
        for b in range(1, WINDOW):
            value = jnp.where(offset == b - REACH, spread[b, row : row + 1, :], value)
        return value

    def build_bias():
        for n in range(layers):
            for b in range(WINDOW):
                rows[b, heads * n : heads * (n + 1), 0 : 2 * WINDOW - 1] = table[n, b]
        x = iota((16, 256), 1)
        j = iota((16, 256), 0)
        own = x < 160
        on_left = x < 208
        y = jnp.where(on_left, x - 160, x - 208)
        p = jnp.where(own, x >> 4, (y >> 2) - 1)
        c = jnp.where(own, x & 15, jnp.where(on_left, (y & 3) - 4, (y & 3) + cols))
        col_ok = (c - j >= -REACH) & (c - j <= REACH)
        for i in range(GROUP):
            oks = []
            for group in (0, 1, 3):
                g = first_row + GROUP * group + i
                start = jnp.clip(g - REACH, 0, total_rows - WINDOW)
                r = first_row + GROUP * group - REACH + p
                oks.append(col_ok & (r >= start) & (r < start + WINDOW))
            prepare(jnp.clip(p[0:8] - i + REACH, 0, 2 * WINDOW - 2))
            for n in range(layers):
                for h in range(heads):
                    value = chosen(n * heads + h, c - j)
                    at = h * 80 + i * 16
                    for var in range(3):
                        bias[n, var, at : at + 16, :] = jnp.where(oks[var], value, -1000000000.0)
        e = iota((16, 256), 0)
        i, j = e & 3, jnp.where(e < 4, -1, cols)
        px, cx = p, c
        col_ok = (cx - j >= -REACH) & (cx - j <= REACH)
        oks = []
        for group in (0, 1, 3):
            g = first_row + GROUP * group + i
            start = jnp.clip(g - REACH, 0, total_rows - WINDOW)
            r = first_row + GROUP * group - REACH + px
            oks.append(col_ok & (r >= start) & (r < start + WINDOW))
        pick = jnp.clip(px - i + REACH, 0, 2 * WINDOW - 2)[0:8]
        for n in range(layers):
            for h in range(heads):
                value = jnp.zeros((8, 256), F32)
                for b in range(WINDOW):
                    source = jnp.broadcast_to(rows[b, n * heads + h : n * heads + h + 1, :], (8, 128))
                    got = [
                        jnp.take_along_axis(source, pick[:, at : at + 128], axis=1)
                        for at in (0, 128)
                    ]
                    value = jnp.where(
                        (cx - j)[0:8] == b - REACH, jnp.concatenate(got, axis=1), value
                    )
                at = h * 80 + 64
                for var in range(3):
                    bias[n, var, at : at + 8, :] = jnp.where(oks[var][0:8], value, -1000000000.0)
                    bias[n, var, at + 8 : at + 16, :] = jnp.zeros((8, 256), F32)
        x, e = iota((32, 256), 1), iota((32, 256), 0)
        j = jnp.where(e < 16, e, jnp.where(e == 16, -1, cols))
        own, on_left = x < 160, x < 208
        y = jnp.where(on_left, x - 160, x - 208)
        c = jnp.where(own, x & 15, jnp.where(on_left, (y & 3) - 4, (y & 3) + cols))
        for k, (here, first_own, first_near) in enumerate(((-1, -4, -4), (16, 10, 8))):
            away = jnp.where(own, first_own + (x >> 4), first_near + (y >> 2)) - here
            ok = (c - j >= -REACH) & (c - j <= REACH) & (away >= -REACH) & (away <= REACH)
            prepare(jnp.clip(away[0:8] + WINDOW - 1, 0, 2 * WINDOW - 2))
            for n in range(layers):
                for h in range(heads):
                    value = chosen(n * heads + h, c - j)
                    row_bias[n, k, h * 32 : h * 32 + 32, :] = jnp.where(ok, value, -1000000000.0)

    def attend(q, near, held, count):
        stacked = jnp.concatenate([q * head_hot[h] for h in range(heads)], axis=0)
        scores = lax.dot_general(
            stacked, near[:, :width], (((1,), (1,)), ((), ())), preferred_element_type=F32
        )
        scores = scores + held
        raised = jnp.exp(scores - jnp.max(scores, axis=-1, keepdims=True))
        weights = (raised * (1.0 / jnp.sum(raised, axis=-1, keepdims=True))).astype(BF16)
        mixed = dot(weights, near[:, width:])
        total = jnp.where(head_of == 0, mixed[0:count], 0.0)
        for h in range(1, heads):
            total = jnp.where(head_of == h, mixed[count * h : count * (h + 1)], total)
        return total.astype(BF16)

    def near_keys(own, side):
        parts = [kvb[own : own + 160, :], near_l[side : side + 48, :], near_r[side : side + 48, :]]
        return jnp.concatenate(parts, axis=0)

    scale = (width // heads) ** (-0.5)
    loads["x"].wait()
    for n in range(layers):
        current = xb[n, 64:320]
        edge[n] = dot(pick_kv, current).astype(BF16)
        if n == 0:
            count = 2 + jnp.where(has_up, 3, 0) + jnp.where(has_down, 3, 0)
            pl.semaphore_wait(barrier, count)
        send(n)
        if n == 0:
            loads["gains"].wait()
        gain = gains_ref[n, 0:1, :]
        wide = current.astype(F32)
        norm = normed(wide, gain)
        loads[n, 0].wait()
        kvb[64:320] = dot(norm, wqkv[n, :, width:]).astype(BF16)
        query = (dot(norm, wqkv[n, :, :width]).astype(BF16) * scale).astype(BF16)
        if n == 0:
            loads["table"].wait()
            build_bias()
            loads["conv"].wait()
        receive(n)
        around = jnp.concatenate([xb[n, 0:64], xb[n, 320:384], left[n], right[n]], axis=0)
        ring = dot(pick_ring, around)
        near = dot(normed(around.astype(F32), gain), wqkv[n, :, width:]).astype(BF16)
        kvb[0:64] = near[0:64]
        kvb[320:384] = near[64:128]
        near_l[...] = near[128:224]
        near_r[...] = near[224:320]
        ring_query = (dot(normed(ring, gain), wqkv[n, :, :width]).astype(BF16) * scale).astype(BF16)
        for group in range(4):
            at = 64 * group
            more = slice(16 * group, 16 * group + 16)
            q = jnp.concatenate([query[at : at + 64], ring_query[more]], axis=0)
            held = bias[n, (0, 1, 1, 2)[group]]
            got = attend(q, near_keys(at + 16, 16 * group), held, 80)
            attn[at : at + 64, :] = got[0:64]
            attn[256 + 16 * group : 272 + 16 * group, :] = got[64:80]

        @pl.when(has_up)
        def _():
            attn[320:352] = attend(ring_query[64:96], near_keys(0, 0), row_bias[n, 0], 32)

        @pl.when(has_down)
        def _():
            attn[352:384] = attend(ring_query[96:128], near_keys(224, 48), row_bias[n, 1], 32)

        loads[n, 1].wait()
        after = jnp.concatenate([wide, ring], axis=0) + dot(attn[...], wout[n])
        norm = normed(after, gains_ref[n, 1:2, :])
        after = after[0:tokens]
        loads[n, 2].wait()
        lift = dot(norm, wup[n]).astype(BF16)
        sides = dot(pick_side, lift[256:320])
        rims = lift[320:384].astype(F32)
        lpad[16:272] = lift[0:tokens].astype(F32)
        col = iota((tokens, 128), 0) & 15
        for ch in range(hid // 128):
            at = slice(128 * ch, 128 * ch + 128)
            above, here, below = lpad[0:256, at], lpad[16:272, at], lpad[32:288, at]

            def column(b):
                return (
                    conv_ref[0, b, n : n + 1, at] * above
                    + conv_ref[1, b, n : n + 1, at] * here
                    + conv_ref[2, b, n : n + 1, at] * below
                )

            pre[:, at] = (
                column(1)
                + jnp.where(col > 0, pltpu.roll(column(0), 1, 0), 0.0)
                + jnp.where(col < cols - 1, pltpu.roll(column(2), tokens - 1, 0), 0.0)
            )
        line = iota((16, hid), 0)

        def tap(a, b):
            return conv_ref[a, b, n : n + 1, :]

        def row_part(a, rim):
            middle = rim[0:16]
            back = jnp.where(line == 0, rim[16:17], pltpu.roll(middle, 1, 0))
            ahead = jnp.where(line == 15, rim[17:18], pltpu.roll(middle, 15, 0))
            return tap(a, 0) * back + tap(a, 1) * middle + tap(a, 2) * ahead

        def col_part(b, values):
            up = jnp.where(line == 0, 0.0, pltpu.roll(values, 1, 0))
            down = jnp.where(line == 15, 0.0, pltpu.roll(values, 15, 0))
            return tap(0, b) * up + tap(1, b) * values + tap(2, b) * down

        pieces = []
        for part in (col_part(0, sides[0:16]), col_part(2, sides[16:32])):
            high = part.astype(BF16)
            pieces += [high, (part - high.astype(F32)).astype(BF16)]
        pre[0:16] += row_part(0, rims[0:32])
        pre[240:256] += row_part(2, rims[32:64])
        whole = pre[...] + dot(place, jnp.concatenate(pieces, axis=0))
        hidden = jax.nn.gelu(whole, approximate=True).astype(BF16)
        loads[n, 3].wait()
        result = (after + dot(hidden, wdown[n])).astype(BF16)
        if n == layers - 1:
            out_ref[...] = result
        else:
            xb[n + 1, 64:320] = result

    for n in range(layers):
        for slot, step in enumerate(STEPS):
            when_to(step, lambda slot=slot: remote(n, slot).wait_send())


PITCH = 24
HALO = 8


def wide_kernel(
    n_lat, n_lon, x_hbm, gains_hbm, table_hbm, conv_hbm, wqkv_hbm, wout_hbm, wup_hbm, wdown_hbm,
    out_ref, gains_ref, table, conv_ref, wqkv, wout, wup, wdown, stage, edge, xf, kvb, qf, attn, af, lifted, hidden, rows,
    bias, place, gather, gather_far, in_sem, w_sem, send_sem, recv_sem,
):
    layers = wqkv.shape[0]
    tokens, width = x_hbm.shape
    cols = 16
    heads = table.shape[2]
    hid = wup.shape[2]
    chunks = hid // 128
    lat = lax.axis_index("lat")
    lon = lax.axis_index("lon")
    odd = lax.rem(lon, 2)
    near = lon + 1 - 2 * odd
    far = lax.rem(lon - 1 + 2 * odd + n_lon, n_lon)

    loads = {}
    firsts = (("x", x_hbm, stage.at[pl.ds(0, 256)]), ("gains", gains_hbm, gains_ref), ("table", table_hbm, table), ("conv", conv_hbm, conv_ref))
    for k, (name, src, dst) in enumerate(firsts):
        loads[name] = pltpu.make_async_copy(src, dst, in_sem.at[k])
        loads[name].start()
    for n in range(layers):
        pairs = ((wqkv_hbm, wqkv), (wout_hbm, wout), (wup_hbm, wup), (wdown_hbm, wdown))
        for k, (src, dst) in enumerate(pairs):
            loads[n, k] = pltpu.make_async_copy(src.at[n], dst.at[n], w_sem.at[n, k])
            loads[n, k].start()

    barrier = pltpu.get_barrier_semaphore()
    partners = ((lat, near), (1 - lat, near), (1 - lat, lon), (lat, far), (1 - lat, far))
    for row, col in partners:
        pl.semaphore_signal(
            barrier, inc=1, device_id={"lat": row, "lon": col}, device_id_type=pl.DeviceIdType.MESH
        )

    remotes = []
    pieces = (
        (edge.at[pl.ds(0, 128)], stage.at[pl.ds(384, 128)]),
        (edge.at[pl.ds(64, 64)], stage.at[pl.ds(512, 64)]),
        (stage.at[pl.ds(pl.multiple_of(128 * (1 - lat), 128), 128)], stage.at[pl.ds(256, 128)]),
        (edge.at[pl.ds(128, 128)], stage.at[pl.ds(576, 128)]),
        (edge.at[pl.ds(192, 64)], stage.at[pl.ds(704, 64)]),
    )
    for slot, (src, dst) in enumerate(pieces):
        remotes.append(
            pltpu.make_async_remote_copy(
                src_ref=src,
                dst_ref=dst,
                send_sem=send_sem.at[slot],
                recv_sem=recv_sem.at[slot],
                device_id={"lat": partners[slot][0], "lon": partners[slot][1]},
                device_id_type=pl.DeviceIdType.MESH,
            )
        )

    def flip(value, by):
        return value + by * (cols - 1 - 2 * value)

    m, t = iota((256, tokens), 0), iota((256, tokens), 1)
    u = (m & 7) + jnp.where(m < 128, 8, 0)
    v = (m & 127) >> 3
    pick = hot(t == flip(v, lat) * cols + flip(u, odd))
    loads["x"].wait()
    edge[...] = dot(pick, stage[0:256]).astype(BF16)
    pl.semaphore_wait(barrier, len(partners))
    for remote in remotes:
        remote.start()

    kvb[0, 768:832] = jnp.zeros((64, 2 * width), BF16)
    kvb[1, 672:832] = jnp.zeros((160, 2 * width), BF16)

    def index(shape, count):
        m, t = iota(shape, 0), iota(shape, 1)
        c = (m * 2731) >> 16
        return c, m - PITCH * c, t

    u, v, t = index((576, 640), 576)
    own = flip(v, lat) * cols + flip(u, odd)
    below = 256 + jnp.where(lat == 0, v - 16, 23 - v) * cols + flip(u, odd)
    side = 384 + v * 8 + 23 - u
    corner = 512 + (23 - v) * 8 + 23 - u
    source = jnp.where(u < 16, jnp.where(v < 16, own, below), jnp.where(v < 16, side, corner))
    gather[...] = hot(t == source)
    i, v, t = index((192, 256), 192)
    k = 7 - i
    gather_far[...] = hot(t == jnp.where(v < 16, v * 8 + k, 128 + (23 - v) * 8 + k))
    m, t = iota((256, 384), 0), iota((256, 384), 1)
    u, v = flip(m & 15, odd), flip(m >> 4, lat)
    place[...] = hot(t == u * PITCH + v)

    loads["table"].wait()
    for n in range(layers):
        for b in range(WINDOW):
            rows[heads * n : heads * (n + 1), 16 * b : 16 * b + 2 * WINDOW - 1] = table[n, b]
    lane, v = iota((PITCH, 256), 1), iota((PITCH, 256), 0)
    key_u = (lane * 2731) >> 16
    key_v = lane - PITCH * key_u
    start = jnp.maximum(v - REACH, 0)
    away = key_v - v
    row_ok = (key_v >= start) & (key_v < start + WINDOW)
    away = jnp.clip(away * (1 - 2 * lat) + WINDOW - 1, 0, 2 * WINDOW - 2)
    for q in range(GROUP):
        off = key_u - REACH - q
        ok = row_ok & (off >= -REACH) & (off <= REACH)
        at = jnp.clip(off * (1 - 2 * odd) + REACH, 0, WINDOW - 1) * 16 + away
        for n in range(layers):
            for h in range(heads):
                line = jnp.broadcast_to(rows[n * heads + h : n * heads + h + 1, :], (PITCH, 128))
                got = [jnp.take_along_axis(line, at[:, s : s + 128], axis=1) for s in (0, 128)]
                value = jnp.where(ok, jnp.concatenate(got, axis=1), -1000000000.0)
                bias[n, h, PITCH * q : PITCH * (q + 1), :] = value

    head_of = iota((1, width), 1) >> 6
    head_hot = [hot(head_of == h) for h in range(heads)]
    scale = (width // heads) ** (-0.5)

    def project(n, first, count, q_from, q_count):
        wide = xf[n, PITCH * first : PITCH * (first + count), :]
        norm = normed(wide, gains_ref[n, 0:1, :])
        kvb[n, PITCH * first : PITCH * (first + count), :] = dot(norm, wqkv[n, :, width:]).astype(BF16)
        query = dot(norm, wqkv[n, :, :width])
        at = PITCH * (q_from + 3 - first)
        qf[PITCH * q_from : PITCH * (q_from + q_count), :] = query[at : at + PITCH * q_count]

    def attend(n, j, w):
        count = PITCH * w
        q = (qf[PITCH * j : PITCH * (j + w), :] * scale).astype(BF16)
        stacked = jnp.concatenate([q * head_hot[h] for h in range(heads)], axis=0)
        keys = kvb[n, PITCH * j : PITCH * j + 256, :]
        scores = lax.dot_general(
            stacked, keys[:, :width], (((1,), (1,)), ((), ())), preferred_element_type=F32
        )
        weights, inverse = [], []
        for h in range(heads):
            held = scores[count * h : count * (h + 1)] + bias[n, h, 0:count, :]
            raised = jnp.exp(held - jnp.max(held, axis=-1, keepdims=True))
            inverse.append(1.0 / jnp.sum(raised, axis=-1, keepdims=True))
            weights.append(raised.astype(BF16))
        mixed = dot(jnp.concatenate(weights, axis=0), keys[:, width:])
        total = mixed[0:count] * inverse[0]
        for h in range(1, heads):
            total = jnp.where(head_of >= h, mixed[count * h : count * (h + 1)] * inverse[h], total)
        attn[PITCH * j : PITCH * (j + w), :] = total.astype(BF16)

    def tap(n, a, b, ch):
        return conv_ref[a + lat * (2 - 2 * a), b + odd * (2 - 2 * b), n : n + 1, 128 * ch : 128 * (ch + 1)]

    def feed(n, j0, count, tiles, o0, outs):
        for j, w in tiles:
            attend(n, j, w)
        size = PITCH * count
        here = slice(PITCH * j0, PITCH * j0 + size)
        wide = xf[n, PITCH * (j0 + 3) : PITCH * (j0 + 3) + size, :]
        after = wide + dot(attn[here], wout[n])
        af[here] = after
        scaled = lax.rsqrt(jnp.mean(after * after, axis=-1, keepdims=True) + 1e-06)
        line = iota((size, 1), 0)
        line = line - PITCH * ((line * 2731) >> 16)
        scaled = jnp.where(line == PITCH - 1, 0.0, scaled)
        norm = (after * scaled * gains_ref[n, 1:2, :]).astype(BF16)
        for ch in range(chunks):
            lifted[ch, 8 + PITCH * j0 : 8 + PITCH * j0 + size, :] = dot(norm, wup[n, :, 128 * ch : 128 * (ch + 1)])
        high = PITCH if n == 0 else 16
        for ch in range(chunks):
            taps = [[tap(n, a, b, ch) for b in range(3)] for a in range(3)]
            for part in range(0, outs, 4):
                pieces = []
                for j in range(o0 + part, o0 + part + 4):
                    total = None
                    for a in range(3):
                        for b in range(3):
                            at = 8 + PITCH * (j + b - 1) + a - 1
                            term = taps[a][b] * lifted[ch, at : at + high, :]
                            total = term if total is None else total + term
                    half = 0.5 * total
                    inner = total * (0.7978845608028654 + 0.035677408136300125 * (total * total))
                    pieces.append((half + half * jnp.tanh(inner)).astype(BF16))
                whole = jnp.concatenate(pieces, axis=0)
                hidden[high * part : high * (part + 4), 128 * ch : 128 * (ch + 1)] = whole
        down = dot(hidden[0 : high * outs], wdown[n])
        if n == 0:
            xf[1, PITCH * (o0 + 3) : PITCH * (o0 + 3 + outs), :] = af[PITCH * o0 : PITCH * (o0 + outs)] + down
        else:
            for k in range(outs):
                at = PITCH * (o0 + k)
                out = af[at : at + 16] + down[16 * k : 16 * (k + 1)]
                af[at : at + 16] = out

    for k in (0, 1, 2):
        remotes[k].wait_recv()
    loads["gains"].wait()
    loads["conv"].wait()
    xf[0, 192:768, :] = dot(gather[:, 0:576], stage[0:576])
    for k in range(4):
        loads[0, k].wait()
    project(0, 8, 24, 5, 21)
    feed(0, 8, 18, ((8, 4), (12, 4), (16, 4), (20, 4), (24, 2)), 9, 16)
    for k in range(4):
        loads[1, k].wait()
    project(1, 12, 16, 9, 13)
    feed(1, 12, 10, ((12, 4), (16, 4), (20, 2)), 13, 8)
    for k in (3, 4):
        remotes[k].wait_recv()
    xf[0, 0:192, :] = dot(gather_far[:, 0:192], stage[576:768])
    project(0, 0, 8, 0, 5)
    feed(0, 0, 8, ((0, 4), (4, 4)), 1, 8)
    project(1, 4, 8, 4, 5)
    feed(1, 4, 8, ((4, 4), (8, 4)), 5, 8)
    out_ref[...] = dot(place[...], af[PITCH * 5 : PITCH * 21].astype(BF16)).astype(BF16)
    for remote in remotes:
        remote.wait_send()


def wide_call(n_lat, n_lon, stream, gains, table, conv, w_qkv, w_out, w_up, w_down):
    layers = w_qkv.shape[0]
    width = stream.shape[1]
    hid = w_up.shape[2]
    vmem = pl.BlockSpec(memory_space=pltpu.VMEM)
    anywhere = pl.BlockSpec(memory_space=pltpu.HBM)
    heads = table.shape[2]
    return pl.pallas_call(
        functools.partial(wide_kernel, n_lat, n_lon),
        out_shape=pltpu.VMEM(stream.shape, BF16),
        in_specs=[anywhere] * 8,
        out_specs=vmem,
        scratch_shapes=[
            pltpu.VMEM(gains.shape, F32),
            pltpu.VMEM(table.shape, F32),
            pltpu.VMEM(conv.shape, F32),
            pltpu.VMEM(w_qkv.shape, BF16),
            pltpu.VMEM(w_out.shape, BF16),
            pltpu.VMEM(w_up.shape, BF16),
            pltpu.VMEM(w_down.shape, BF16),
            pltpu.VMEM((768, width), BF16),
            pltpu.VMEM((256, width), BF16),
            pltpu.VMEM((layers, 32 * PITCH, width), F32),
            pltpu.VMEM((layers, 832, 2 * width), BF16),
            pltpu.VMEM((26 * PITCH, width), F32),
            pltpu.VMEM((26 * PITCH, width), BF16),
            pltpu.VMEM((26 * PITCH, width), F32),
            pltpu.VMEM((hid // 128, 26 * PITCH + 16, 128), F32),
            pltpu.VMEM((16 * PITCH, hid), BF16),
            pltpu.VMEM((layers * heads, 128), F32),
            pltpu.VMEM((layers, heads, GROUP * PITCH, 256), F32),
            pltpu.VMEM((256, 384), BF16),
            pltpu.VMEM((576, 640), BF16),
            pltpu.VMEM((192, 256), BF16),
            pltpu.SemaphoreType.DMA((4,)),
            pltpu.SemaphoreType.DMA((layers, 4)),
            pltpu.SemaphoreType.DMA((5,)),
            pltpu.SemaphoreType.DMA((5,)),
        ],
        compiler_params=pltpu.CompilerParams(
            collective_id=0, has_side_effects=True, vmem_limit_bytes=58 * 1024 * 1024
        ),
    )(stream, gains, table, conv, w_qkv, w_out, w_up, w_down)


def on_device(n_lat, n_lon, stream, gains, w_qkv, table, w_out, w_up, conv, w_down):
    rows, cols, width = stream.shape
    layers, heads = table.shape[:2]
    table = table.transpose(0, 3, 1, 2)
    conv = conv.transpose(1, 2, 0, 3)
    hid = w_up.shape[2]
    vmem = pl.BlockSpec(memory_space=pltpu.VMEM)
    anywhere = pl.BlockSpec(memory_space=pltpu.HBM)
    if n_lat == 2 and n_lon % 2 == 0:
        result = wide_call(
            n_lat, n_lon, stream.reshape(rows * cols, width), gains, table, conv, w_qkv, w_out, w_up, w_down
        )
        return result.reshape(rows, cols, width)
    result = pl.pallas_call(
        functools.partial(kernel, n_lat, n_lon),
        out_shape=pltpu.VMEM((rows * cols, width), BF16),
        in_specs=[anywhere] * 8,
        out_specs=vmem,
        scratch_shapes=[
            pltpu.VMEM(gains.shape, F32),
            pltpu.VMEM(table.shape, F32),
            pltpu.VMEM(conv.shape, F32),
            pltpu.VMEM(w_qkv.shape, BF16),
            pltpu.VMEM(w_out.shape, BF16),
            pltpu.VMEM(w_up.shape, BF16),
            pltpu.VMEM(w_down.shape, BF16),
            pltpu.VMEM((384, 2 * width), BF16),
            pltpu.VMEM((96, 2 * width), BF16),
            pltpu.VMEM((96, 2 * width), BF16),
            pltpu.VMEM((layers, 384, width), BF16),
            pltpu.VMEM((layers, 96, width), BF16),
            pltpu.VMEM((layers, 96, width), BF16),
            pltpu.VMEM((layers, 128, width), BF16),
            pltpu.VMEM((288, hid), F32),
            pltpu.VMEM((256, hid), F32),
            pltpu.VMEM((WINDOW, layers * heads, 128), F32),
            pltpu.VMEM((WINDOW, layers * heads, 256), F32),
            pltpu.VMEM((layers, 3, 320, 256), F32),
            pltpu.VMEM((layers, 2, 128, 256), F32),
            pltpu.VMEM((384, width), BF16),
            pltpu.SemaphoreType.DMA((4,)),
            pltpu.SemaphoreType.DMA((layers, 4)),
            pltpu.SemaphoreType.DMA((layers, 8)),
            pltpu.SemaphoreType.DMA((layers, 8)),
        ],
        compiler_params=pltpu.CompilerParams(
            collective_id=0, has_side_effects=True, vmem_limit_bytes=58 * 1024 * 1024
        ),
    )(
        stream.reshape(rows * cols, width),
        gains,
        table,
        conv,
        w_qkv,
        w_out,
        w_up,
        w_down,
    )
    return result.reshape(rows, cols, width)


def solution(mesh):
    sizes = dict(mesh.shape)
    in_specs = (P("lat", "lon", None), P(), P(), P(), P(), P(), P(), P())
    return jax.shard_map(
        functools.partial(on_device, sizes["lat"], sizes["lon"]),
        mesh=mesh,
        in_specs=in_specs,
        out_specs=P("lat", "lon", None),
        check_vma=False,
    )
```

```python
import functools

import jax
import jax.numpy as jnp
from jax import lax
from jax.experimental import pallas as pl
from jax.experimental.pallas import tpu as pltpu
from jax.sharding import PartitionSpec as P

WINDOW = 7
REACH = 3
GROUP = 4
F32 = jnp.float32
BF16 = jnp.bfloat16

LEFT, RIGHT, TOP, BOTTOM, TOP_L, TOP_R, BOT_L, BOT_R = range(8)
STEPS = ((0, 1), (0, -1), (1, 0), (-1, 0), (1, 1), (1, -1), (-1, 1), (-1, -1))


def iota(shape, dim):
    return lax.broadcasted_iota(jnp.int32, shape, dim)


def hot(cond):
    return jnp.where(cond, 1.0, 0.0).astype(BF16)


def dot(a, b):
    return jnp.dot(a, b, preferred_element_type=F32)


def normed(wide, gain):
    scale = lax.rsqrt(jnp.mean(wide * wide, axis=-1, keepdims=True) + 1e-06)
    return (wide * scale * gain).astype(BF16)


def kernel(
    n_lat, n_lon, x_hbm, gains_hbm, table_hbm, conv_hbm, wqkv_hbm, wout_hbm, wup_hbm, wdown_hbm,
    out_ref, gains_ref, table, conv_ref, wqkv, wout, wup, wdown, kvb, near_l, near_r, xb, left, right, edge, lpad, pre, rows, spread,
    bias, row_bias, attn, in_sem, w_sem, send_sem, recv_sem,
):
    layers = wqkv.shape[0]
    tokens, width = x_hbm.shape
    cols = 16
    heads = table.shape[2]
    hid = wup.shape[2]
    lat = lax.axis_index("lat")
    lon = lax.axis_index("lon")
    has_up = lat > 0
    has_down = lat < n_lat - 1
    total_rows = n_lat * (tokens // cols)
    first_row = lat * (tokens // cols)

    loads = {}
    firsts = (("x", x_hbm, xb.at[0, pl.ds(64, 256)]), ("gains", gains_hbm, gains_ref), ("table", table_hbm, table), ("conv", conv_hbm, conv_ref))
    for k, (name, src, dst) in enumerate(firsts):
        loads[name] = pltpu.make_async_copy(src, dst, in_sem.at[k])
    loads["x"].start()
    loads["gains"].start()
    for n in range(layers):
        pairs = ((wqkv_hbm, wqkv), (wout_hbm, wout), (wup_hbm, wup), (wdown_hbm, wdown))
        for k, (src, dst) in enumerate(pairs):
            loads[n, k] = pltpu.make_async_copy(src.at[n], dst.at[n], w_sem.at[n, k])
            loads[n, k].start()
            if n == 0 and k == 0:
                loads["table"].start()
                loads["conv"].start()

    def target(step):
        return {"lat": lat + step[0], "lon": lax.rem(lon + step[1] + n_lon, n_lon)}

    def when_to(step, go):
        if step[0] == 0:
            go()
        else:
            pl.when(has_down if step[0] > 0 else has_up)(go)

    def when_from(step, go):
        when_to((-step[0], -step[1]), go)

    barrier = pltpu.get_barrier_semaphore()
    for step in STEPS:
        when_to(
            step,
            lambda step=step: pl.semaphore_signal(
                barrier, inc=1, device_id=target(step), device_id_type=pl.DeviceIdType.MESH
            ),
        )

    def remote(n, slot):
        own, lo, ro, ed = xb.at[n], left.at[n], right.at[n], edge.at[n]
        src, dst = (
            (ed.at[pl.ds(64, 64)], lo.at[pl.ds(16, 64)]),
            (ed.at[pl.ds(0, 64)], ro.at[pl.ds(16, 64)]),
            (own.at[pl.ds(256, 64)], own.at[pl.ds(0, 64)]),
            (own.at[pl.ds(64, 64)], own.at[pl.ds(320, 64)]),
            (ed.at[pl.ds(112, 16)], lo.at[pl.ds(0, 16)]),
            (ed.at[pl.ds(48, 16)], ro.at[pl.ds(0, 16)]),
            (ed.at[pl.ds(64, 16)], lo.at[pl.ds(80, 16)]),
            (ed.at[pl.ds(0, 16)], ro.at[pl.ds(80, 16)]),
        )[slot]
        return pltpu.make_async_remote_copy(
            src_ref=src,
            dst_ref=dst,
            send_sem=send_sem.at[n, slot],
            recv_sem=recv_sem.at[n, slot],
            device_id=target(STEPS[slot]),
            device_id_type=pl.DeviceIdType.MESH,
        )

    def send(n):
        for slot, step in enumerate(STEPS):
            when_to(step, lambda slot=slot: remote(n, slot).start())

    def receive(n):
        for slot, step in enumerate(STEPS):
            when_from(step, lambda slot=slot: remote(n, slot).wait_recv())

    @pl.when(jnp.logical_not(has_up))
    def _():
        for n in range(layers):
            xb[n, 0:64] = jnp.zeros((64, width), BF16)
            left[n, 0:16] = jnp.zeros((16, width), BF16)
            right[n, 0:16] = jnp.zeros((16, width), BF16)
        attn[320:352] = jnp.zeros((32, width), BF16)

    @pl.when(jnp.logical_not(has_down))
    def _():
        for n in range(layers):
            xb[n, 320:384] = jnp.zeros((64, width), BF16)
            left[n, 80:96] = jnp.zeros((16, width), BF16)
            right[n, 80:96] = jnp.zeros((16, width), BF16)
        attn[352:384] = jnp.zeros((32, width), BF16)

    lpad[0:16] = jnp.zeros((16, hid), F32)
    lpad[272:288] = jnp.zeros((16, hid), F32)

    m, t = iota((128, tokens), 0), iota((128, tokens), 1)
    pick_kv = hot(t == ((m & 63) >> 2) * cols + (m & 3) + jnp.where(m >= 64, cols - 4, 0))
    m, t = iota((128, 320), 0), iota((128, 320), 1)
    e = m & 31
    side = 4 * (4 * (m >> 4) + (m & 3) + 4)
    flank = jnp.where((m & 15) < 4, 128 + side + 3, jnp.where((m & 15) < 8, 224 + side, -1))
    above = jnp.where(e < 16, 48 + e, jnp.where(e == 16, 143, jnp.where(e == 17, 236, -1)))
    below = jnp.where(e < 16, 64 + e, jnp.where(e == 16, 211, jnp.where(e == 17, 304, -1)))
    pick_ring = hot(t == jnp.where(m < 64, flank, jnp.where(m < 96, above, below)))
    m, t = iota((32, 64), 0), iota((32, 64), 1)
    pick_side = hot(t == ((m & 15) >> 2) * 16 + (m & 3) + jnp.where(m < 16, 0, 4))
    t, k = iota((tokens, 64), 0), iota((tokens, 64), 1)
    place = hot(((k & 15) == (t >> 4)) & ((t & 15) == jnp.where(k < 32, 0, cols - 1)))
    head_of = iota((1, width), 1) >> 6
    head_hot = [hot(head_of == h) for h in range(heads)]

    def prepare(pick):
        for at in (0, 128):
            for b in range(WINDOW):
                spread[b, :, at : at + 128] = jnp.take_along_axis(
                    rows[b], pick[:, at : at + 128], axis=1
                )

    def chosen(row, offset):
        value = jnp.broadcast_to(spread[0, row : row + 1, :], offset.shape)
        for b in range(1, WINDOW):
            value = jnp.where(offset == b - REACH, spread[b, row : row + 1, :], value)
        return value

    def build_bias():
        for n in range(layers):
            for b in range(WINDOW):
                rows[b, heads * n : heads * (n + 1), 0 : 2 * WINDOW - 1] = table[n, b]
        x = iota((16, 256), 1)
        j = iota((16, 256), 0)
        own = x < 160
        on_left = x < 208
        y = jnp.where(on_left, x - 160, x - 208)
        p = jnp.where(own, x >> 4, (y >> 2) - 1)
        c = jnp.where(own, x & 15, jnp.where(on_left, (y & 3) - 4, (y & 3) + cols))
        col_ok = (c - j >= -REACH) & (c - j <= REACH)
        for i in range(GROUP):
            oks = []
            for group in (0, 1, 3):
                g = first_row + GROUP * group + i
                start = jnp.clip(g - REACH, 0, total_rows - WINDOW)
                r = first_row + GROUP * group - REACH + p
                oks.append(col_ok & (r >= start) & (r < start + WINDOW))
            prepare(jnp.clip(p[0:8] - i + REACH, 0, 2 * WINDOW - 2))
            for n in range(layers):
                for h in range(heads):
                    value = chosen(n * heads + h, c - j)
                    at = h * 80 + i * 16
                    for var in range(3):
                        bias[n, var, at : at + 16, :] = jnp.where(oks[var], value, -1000000000.0)
        e = iota((16, 256), 0)
        i, j = e & 3, jnp.where(e < 4, -1, cols)
        px, cx = p, c
        col_ok = (cx - j >= -REACH) & (cx - j <= REACH)
        oks = []
        for group in (0, 1, 3):
            g = first_row + GROUP * group + i
            start = jnp.clip(g - REACH, 0, total_rows - WINDOW)
            r = first_row + GROUP * group - REACH + px
            oks.append(col_ok & (r >= start) & (r < start + WINDOW))
        pick = jnp.clip(px - i + REACH, 0, 2 * WINDOW - 2)[0:8]
        for n in range(layers):
            for h in range(heads):
                value = jnp.zeros((8, 256), F32)
                for b in range(WINDOW):
                    source = jnp.broadcast_to(rows[b, n * heads + h : n * heads + h + 1, :], (8, 128))
                    got = [
                        jnp.take_along_axis(source, pick[:, at : at + 128], axis=1)
                        for at in (0, 128)
                    ]
                    value = jnp.where(
                        (cx - j)[0:8] == b - REACH, jnp.concatenate(got, axis=1), value
                    )
                at = h * 80 + 64
                for var in range(3):
                    bias[n, var, at : at + 8, :] = jnp.where(oks[var][0:8], value, -1000000000.0)
                    bias[n, var, at + 8 : at + 16, :] = jnp.zeros((8, 256), F32)
        x, e = iota((32, 256), 1), iota((32, 256), 0)
        j = jnp.where(e < 16, e, jnp.where(e == 16, -1, cols))
        own, on_left = x < 160, x < 208
        y = jnp.where(on_left, x - 160, x - 208)
        c = jnp.where(own, x & 15, jnp.where(on_left, (y & 3) - 4, (y & 3) + cols))
        for k, (here, first_own, first_near) in enumerate(((-1, -4, -4), (16, 10, 8))):
            away = jnp.where(own, first_own + (x >> 4), first_near + (y >> 2)) - here
            ok = (c - j >= -REACH) & (c - j <= REACH) & (away >= -REACH) & (away <= REACH)
            prepare(jnp.clip(away[0:8] + WINDOW - 1, 0, 2 * WINDOW - 2))
            for n in range(layers):
                for h in range(heads):
                    value = chosen(n * heads + h, c - j)
                    row_bias[n, k, h * 32 : h * 32 + 32, :] = jnp.where(ok, value, -1000000000.0)

    def attend(q, near, held, count):
        stacked = jnp.concatenate([q * head_hot[h] for h in range(heads)], axis=0)
        scores = lax.dot_general(
            stacked, near[:, :width], (((1,), (1,)), ((), ())), preferred_element_type=F32
        )
        scores = scores + held
        raised = jnp.exp(scores - jnp.max(scores, axis=-1, keepdims=True))
        weights = (raised * (1.0 / jnp.sum(raised, axis=-1, keepdims=True))).astype(BF16)
        mixed = dot(weights, near[:, width:])
        total = jnp.where(head_of == 0, mixed[0:count], 0.0)
        for h in range(1, heads):
            total = jnp.where(head_of == h, mixed[count * h : count * (h + 1)], total)
        return total.astype(BF16)

    def near_keys(own, side):
        parts = [kvb[own : own + 160, :], near_l[side : side + 48, :], near_r[side : side + 48, :]]
        return jnp.concatenate(parts, axis=0)

    scale = (width // heads) ** (-0.5)
    loads["x"].wait()
    for n in range(layers):
        current = xb[n, 64:320]
        edge[n] = dot(pick_kv, current).astype(BF16)
        if n == 0:
            count = 2 + jnp.where(has_up, 3, 0) + jnp.where(has_down, 3, 0)
            pl.semaphore_wait(barrier, count)
        send(n)
        if n == 0:
            loads["gains"].wait()
        gain = gains_ref[n, 0:1, :]
        wide = current.astype(F32)
        norm = normed(wide, gain)
        loads[n, 0].wait()
        kvb[64:320] = dot(norm, wqkv[n, :, width:]).astype(BF16)
        query = (dot(norm, wqkv[n, :, :width]).astype(BF16) * scale).astype(BF16)
        if n == 0:
            loads["table"].wait()
            build_bias()
            loads["conv"].wait()
        receive(n)
        around = jnp.concatenate([xb[n, 0:64], xb[n, 320:384], left[n], right[n]], axis=0)
        ring = dot(pick_ring, around)
        near = dot(normed(around.astype(F32), gain), wqkv[n, :, width:]).astype(BF16)
        kvb[0:64] = near[0:64]
        kvb[320:384] = near[64:128]
        near_l[...] = near[128:224]
        near_r[...] = near[224:320]
        ring_query = (dot(normed(ring, gain), wqkv[n, :, :width]).astype(BF16) * scale).astype(BF16)
        for group in range(4):
            at = 64 * group
            more = slice(16 * group, 16 * group + 16)
            q = jnp.concatenate([query[at : at + 64], ring_query[more]], axis=0)
            held = bias[n, (0, 1, 1, 2)[group]]
            got = attend(q, near_keys(at + 16, 16 * group), held, 80)
            attn[at : at + 64, :] = got[0:64]
            attn[256 + 16 * group : 272 + 16 * group, :] = got[64:80]

        @pl.when(has_up)
        def _():
            attn[320:352] = attend(ring_query[64:96], near_keys(0, 0), row_bias[n, 0], 32)

        @pl.when(has_down)
        def _():
            attn[352:384] = attend(ring_query[96:128], near_keys(224, 48), row_bias[n, 1], 32)

        loads[n, 1].wait()
        after = jnp.concatenate([wide, ring], axis=0) + dot(attn[...], wout[n])
        norm = normed(after, gains_ref[n, 1:2, :])
        after = after[0:tokens]
        loads[n, 2].wait()
        lift = dot(norm, wup[n]).astype(BF16)
        sides = dot(pick_side, lift[256:320])
        rims = lift[320:384].astype(F32)
        lpad[16:272] = lift[0:tokens].astype(F32)
        col = iota((tokens, 128), 0) & 15
        for ch in range(hid // 128):
            at = slice(128 * ch, 128 * ch + 128)
            above, here, below = lpad[0:256, at], lpad[16:272, at], lpad[32:288, at]

            def column(b):
                return (
                    conv_ref[0, b, n : n + 1, at] * above
                    + conv_ref[1, b, n : n + 1, at] * here
                    + conv_ref[2, b, n : n + 1, at] * below
                )

            pre[:, at] = (
                column(1)
                + jnp.where(col > 0, pltpu.roll(column(0), 1, 0), 0.0)
                + jnp.where(col < cols - 1, pltpu.roll(column(2), tokens - 1, 0), 0.0)
            )
        line = iota((16, hid), 0)

        def tap(a, b):
            return conv_ref[a, b, n : n + 1, :]

        def row_part(a, rim):
            middle = rim[0:16]
            back = jnp.where(line == 0, rim[16:17], pltpu.roll(middle, 1, 0))
            ahead = jnp.where(line == 15, rim[17:18], pltpu.roll(middle, 15, 0))
            return tap(a, 0) * back + tap(a, 1) * middle + tap(a, 2) * ahead

        def col_part(b, values):
            up = jnp.where(line == 0, 0.0, pltpu.roll(values, 1, 0))
            down = jnp.where(line == 15, 0.0, pltpu.roll(values, 15, 0))
            return tap(0, b) * up + tap(1, b) * values + tap(2, b) * down

        pieces = []
        for part in (col_part(0, sides[0:16]), col_part(2, sides[16:32])):
            high = part.astype(BF16)
            pieces += [high, (part - high.astype(F32)).astype(BF16)]
        pre[0:16] += row_part(0, rims[0:32])
        pre[240:256] += row_part(2, rims[32:64])
        whole = pre[...] + dot(place, jnp.concatenate(pieces, axis=0))
        hidden = jax.nn.gelu(whole, approximate=True).astype(BF16)
        loads[n, 3].wait()
        result = (after + dot(hidden, wdown[n])).astype(BF16)
        if n == layers - 1:
            out_ref[...] = result
        else:
            xb[n + 1, 64:320] = result

    for n in range(layers):
        for slot, step in enumerate(STEPS):
            when_to(step, lambda slot=slot: remote(n, slot).wait_send())


PITCH = 24
HALO = 8


def halved(a, b):
    half = a.shape[0] // 32 * 16
    return jnp.concatenate([dot(a[:half], b), dot(a[half:], b)], axis=0)


def wide_kernel(
    n_lat, n_lon, x_hbm, gains_hbm, table_hbm, conv_hbm, wqkv_hbm, wout_hbm, wup_hbm, wdown_hbm,
    out_ref, gains_ref, table, conv_ref, wqkv, wout, wup, wdown, stage, edge, xf, kvb, qf, attn, af, nf, lifted, lifted_b, hidden, rows,
    bias, place, gather, gather_far, in_sem, w_sem, send_sem, recv_sem, here_sem,
):
    layers = wqkv.shape[0]
    tokens, width = x_hbm.shape
    cols = 16
    heads = table.shape[2]
    hid = wup.shape[2]
    chunks = hid // 128
    lat = lax.axis_index("lat")
    lon = lax.axis_index("lon")
    odd = lax.rem(lon, 2)
    near = lon + 1 - 2 * odd
    far = lax.rem(lon - 1 + 2 * odd + n_lon, n_lon)

    loads = {}
    firsts = (("x", x_hbm, stage.at[pl.ds(0, 256)]), ("gains", gains_hbm, gains_ref), ("table", table_hbm, table), ("conv", conv_hbm, conv_ref))
    for k, (name, src, dst) in enumerate(firsts):
        loads[name] = pltpu.make_async_copy(src, dst, in_sem.at[k])
        loads[name].start()
    for n in range(layers):
        pairs = ((wqkv_hbm, wqkv), (wout_hbm, wout), (wup_hbm, wup), (wdown_hbm, wdown))
        for k, (src, dst) in enumerate(pairs):
            loads[n, k] = pltpu.make_async_copy(src.at[n], dst.at[n], w_sem.at[n, k])
            loads[n, k].start()

    barrier = pltpu.get_barrier_semaphore()
    partners = ((lat, near), (1 - lat, near), (1 - lat, lon), (lat, far), (1 - lat, far))
    first, last = lon == 0, lon == n_lon - 1

    def greet(semaphore, row, col):
        pl.semaphore_signal(
            semaphore, inc=1, device_id={"lat": row, "lon": col}, device_id_type=pl.DeviceIdType.MESH
        )

    for row, col in partners[:3]:
        greet(barrier, row, col)

    @pl.when(jnp.logical_not(last))
    def _():
        for row, col in partners[3:]:
            greet(barrier, row, col)

    @pl.when(last)
    def _():
        pl.semaphore_wait(barrier, len(partners))
        for row, col in partners[3:]:
            greet(here_sem, row, col)

    remotes = []
    pieces = (
        (edge.at[pl.ds(0, 128)], stage.at[pl.ds(384, 128)]),
        (edge.at[pl.ds(64, 64)], stage.at[pl.ds(512, 64)]),
        (stage.at[pl.ds(pl.multiple_of(128 * (1 - lat), 128), 128)], stage.at[pl.ds(256, 128)]),
        (edge.at[pl.ds(128, 128)], stage.at[pl.ds(576, 128)]),
        (edge.at[pl.ds(192, 64)], stage.at[pl.ds(704, 64)]),
    )
    for slot, (src, dst) in enumerate(pieces):
        remotes.append(
            pltpu.make_async_remote_copy(
                src_ref=src,
                dst_ref=dst,
                send_sem=send_sem.at[slot],
                recv_sem=recv_sem.at[slot],
                device_id={"lat": partners[slot][0], "lon": partners[slot][1]},
                device_id_type=pl.DeviceIdType.MESH,
            )
        )

    def flip(value, by):
        return value + by * (cols - 1 - 2 * value)

    m, t = iota((256, tokens), 0), iota((256, tokens), 1)
    u = (m & 7) + jnp.where(m < 128, 8, 0)
    v = (m & 127) >> 3
    pick = hot(t == flip(v, lat) * cols + flip(u, odd))
    loads["x"].wait()
    edge[...] = dot(pick, stage[0:256]).astype(BF16)
    @pl.when(jnp.logical_not(last))
    def _():
        pl.semaphore_wait(barrier, len(partners) - jnp.where(first, 2, 0))

    for remote in remotes[:3]:
        remote.start()

    @pl.when(last)
    def _():
        for remote in remotes[3:]:
            remote.start()

    def answer():
        @pl.when(first)
        def _():
            pl.semaphore_wait(here_sem, 2)
            for remote in remotes[3:]:
                remote.start()

    kvb[0, 768:832] = jnp.zeros((64, 2 * width), BF16)
    kvb[1, 672:832] = jnp.zeros((160, 2 * width), BF16)

    def index(shape, count):
        m, t = iota(shape, 0), iota(shape, 1)
        c = (m * 2731) >> 16
        return c, m - PITCH * c, t

    u, v, t = index((576, 640), 576)
    own = flip(v, lat) * cols + flip(u, odd)
    below = 256 + jnp.where(lat == 0, v - 16, 23 - v) * cols + flip(u, odd)
    side = 384 + v * 8 + 23 - u
    corner = 512 + (23 - v) * 8 + 23 - u
    source = jnp.where(u < 16, jnp.where(v < 16, own, below), jnp.where(v < 16, side, corner))
    gather[...] = hot(t == source)
    i, v, t = index((192, 256), 192)
    k = 7 - i
    gather_far[...] = hot(t == jnp.where(v < 16, v * 8 + k, 128 + (23 - v) * 8 + k))
    m, t = iota((256, 384), 0), iota((256, 384), 1)
    u, v = flip(m & 15, odd), flip(m >> 4, lat)
    place[...] = hot(t == u * PITCH + v)

    loads["table"].wait()
    for n in range(layers):
        for b in range(WINDOW):
            rows[heads * n : heads * (n + 1), 16 * b : 16 * b + 2 * WINDOW - 1] = table[n, b]
    lane, v = iota((PITCH, 256), 1), iota((PITCH, 256), 0)
    key_u = (lane * 2731) >> 16
    key_v = lane - PITCH * key_u
    start = jnp.maximum(v - REACH, 0)
    away = key_v - v
    row_ok = (key_v >= start) & (key_v < start + WINDOW)
    away = jnp.clip(away * (1 - 2 * lat) + WINDOW - 1, 0, 2 * WINDOW - 2)
    for q in range(GROUP):
        off = key_u - REACH - q
        ok = row_ok & (off >= -REACH) & (off <= REACH)
        at = jnp.clip(off * (1 - 2 * odd) + REACH, 0, WINDOW - 1) * 16 + away
        for n in range(layers):
            for h in range(heads):
                line = jnp.broadcast_to(rows[n * heads + h : n * heads + h + 1, :], (PITCH, 128))
                got = [jnp.take_along_axis(line, at[:, s : s + 128], axis=1) for s in (0, 128)]
                value = jnp.where(ok, jnp.concatenate(got, axis=1) * 1.4426950408889634, -1000000000.0)
                bias[n, h, PITCH * q : PITCH * (q + 1), :] = value

    head_of = iota((1, width), 1) >> 6
    head_hot = [hot(head_of == h) for h in range(heads)]
    half_hot = [hot((iota((1, 128), 1) >> 6) == k) for k in range(2)]
    log2e = 1.4426950408889634
    scale = (width // heads) ** (-0.5) * log2e

    def project(n, first, count, q_from, q_count):
        wide = xf[n, PITCH * first : PITCH * (first + count), :]
        norm = normed(wide, gains_ref[n, 0:1, :])
        kvb[n, PITCH * first : PITCH * (first + count), :] = halved(norm, wqkv[n, :, width:]).astype(BF16)
        query = halved(norm, wqkv[n, :, :width])
        at = PITCH * (q_from + 3 - first)
        qf[PITCH * q_from : PITCH * (q_from + q_count), :] = query[at : at + PITCH * q_count]

    def attend(n, tiles):
        def score(j, w):
            count = PITCH * w
            q = (qf[PITCH * j : PITCH * (j + w), :] * scale).astype(BF16)
            keys = kvb[n, PITCH * j : PITCH * j + 256, 0:width]
            scores = []
            for pair in range(heads // 2):
                stacked = jnp.concatenate([q * head_hot[2 * pair + k] for k in range(2)], axis=0)
                scores.append(
                    lax.dot_general(stacked, keys, (((1,), (1,)), ((), ())), preferred_element_type=F32)
                )
            return scores

        def soften(scores, w):
            count = PITCH * w
            weights = []
            for h in range(heads):
                held = scores[h // 2][count * (h % 2) : count * (h % 2 + 1)] + bias[n, h, 0:count, :]
                weights.append(jnp.exp2((held - jnp.max(held, axis=-1, keepdims=True)).astype(BF16)))
            return weights

        def gather_values(weights, j, w):
            for pair in range(heads // 2):
                values = []
                at = width + 128 * pair
                for k in range(2):
                    own = kvb[n, PITCH * j : PITCH * j + 256, at : at + 128] * half_hot[k]
                    values.append(jnp.concatenate([own, jnp.broadcast_to(half_hot[k], own.shape)], axis=1))
                both = jnp.concatenate(weights[2 * pair : 2 * pair + 2], axis=1)
                mixed = dot(both, jnp.concatenate(values, axis=0))
                total = mixed[:, 0:128] * (1.0 / mixed[:, 128:256])
                attn[PITCH * j : PITCH * (j + w), 128 * pair : 128 * (pair + 1)] = total.astype(BF16)

        ahead = [score(*tile) for tile in tiles[:2]]
        for k, (j, w) in enumerate(tiles):
            weights = soften(ahead[k], w)
            if k + 2 < len(tiles):
                ahead.append(score(*tiles[k + 2]))
            gather_values(weights, j, w)

    def tap(n, a, b, ch):
        return conv_ref[a + lat * (2 - 2 * a), b + odd * (2 - 2 * b), n : n + 1, 128 * ch : 128 * (ch + 1)]

    def feed(n, j0, count, tiles, o0, outs, then=None):
        attend(n, tiles)
        if then is not None:
            then()
        size = PITCH * count
        here = slice(PITCH * j0, PITCH * j0 + size)
        wide = xf[n, PITCH * (j0 + 3) : PITCH * (j0 + 3) + size, :]
        after = wide + halved(attn[here], wout[n])
        af[here] = after
        scaled = lax.rsqrt(jnp.mean(after * after, axis=-1, keepdims=True) + 1e-06)
        line = iota((size, 1), 0)
        line = line - PITCH * ((line * 2731) >> 16)
        scaled = jnp.where(line == PITCH - 1, 0.0, scaled)
        norm = after * scaled * gains_ref[n, 1:2, :]
        for k in range(2):
            nf[k, 8 + PITCH * j0 : 8 + PITCH * j0 + size, :] = norm[:, 128 * k : 128 * (k + 1)]
        high = PITCH if n == 0 else 16
        more = 1 if n == 0 and j0 == 0 else 0
        for a in range(3):
            halves = []
            for k in range(2):
                if n == 0:
                    at = 8 + PITCH * j0 + a - 1
                    halves.append(nf[k, at : at + size + PITCH * more, :].astype(BF16))
                else:
                    spots = [8 + PITCH * j + a - 1 for j in range(j0, j0 + count)]
                    halves.append(jnp.concatenate([nf[k, at : at + 16, :] for at in spots], axis=0).astype(BF16))
            moved = jnp.concatenate(halves, axis=1)
            for double in range(chunks // 2):
                both = dot(moved, wup[n, :, 256 * double : 256 * (double + 1)])
                for ch in (2 * double, 2 * double + 1):
                    lift = both[:, 128 * (ch % 2) : 128 * (ch % 2 + 1)]
                    if n == 0:
                        lift = lift.reshape(count + more, PITCH, 128)
                        base = lift[0:count, 0:16].reshape(16 * count, 128).astype(BF16)
                        over = lift[:, 16:PITCH]
                        pairs = jnp.concatenate([over[:-1], over[1:]], axis=1).reshape(-1, 128)
                        lifted_b[a, ch, 16 * j0 : 16 * (j0 + count + more - 1), :] = pairs.astype(BF16)
                    else:
                        base = lift.astype(BF16)
                    lifted[a, ch, 16 * j0 : 16 * (j0 + count), :] = base
        for ch in range(chunks):
            taps = [[tap(n, a, b, ch).astype(BF16) for b in range(3)] for a in range(3)]

            def convolved(source, j, wide):
                total = None
                for a in range(3):
                    for b in range(3):
                        at = 16 * (j + b - 1)
                        term = taps[a][b] * source[a, ch, at : at + 16 * wide, :]
                        total = term if total is None else total + term
                half = 0.5 * total
                inner = total * (0.7978845608028654 + 0.035677408136300125 * (total * total))
                return half + half * jnp.tanh(inner)

            for part in range(0, outs, 2):
                main = convolved(lifted, o0 + part, 2)
                if n == 0:
                    rest = convolved(lifted_b, o0 + part, 1).astype(F32)
                    main = main.astype(F32)
                    main = jnp.concatenate([main[0:16], rest[0:8], main[16:32], rest[8:16]], axis=0).astype(BF16)
                hidden[high * part : high * (part + 2), 128 * ch : 128 * (ch + 1)] = main
        down = halved(hidden[0 : high * outs], wdown[n])
        if n == 0:
            xf[1, PITCH * (o0 + 3) : PITCH * (o0 + 3 + outs), :] = af[PITCH * o0 : PITCH * (o0 + outs)] + down
        else:
            for k in range(outs):
                at = PITCH * (o0 + k)
                out = af[at : at + 16] + down[16 * k : 16 * (k + 1)]
                af[at : at + 16] = out

    for k in (0, 1, 2):
        remotes[k].wait_recv()

    @pl.when(jnp.logical_not(first | last))
    def _():
        for remote in remotes[3:]:
            remote.start()

    loads["gains"].wait()
    loads["conv"].wait()
    xf[0, 192:768, :] = halved(gather[:, 0:576], stage[0:576])
    for k in range(4):
        loads[0, k].wait()
    project(0, 8, 24, 5, 21)
    feed(0, 8, 18, ((8, 4), (12, 4), (16, 4), (20, 4), (24, 2)), 9, 16, answer)
    for k in range(4):
        loads[1, k].wait()
    project(1, 12, 16, 9, 13)
    feed(1, 12, 10, ((12, 4), (16, 4), (20, 2)), 13, 8)
    for k in (3, 4):
        remotes[k].wait_recv()
    xf[0, 0:192, :] = dot(gather_far[:, 0:192], stage[576:768])
    project(0, 0, 8, 0, 5)
    feed(0, 0, 8, ((0, 4), (4, 4)), 1, 8)
    project(1, 4, 8, 4, 5)
    feed(1, 4, 8, ((4, 4), (8, 4)), 5, 8)
    out_ref[...] = dot(place[...], af[PITCH * 5 : PITCH * 21].astype(BF16)).astype(BF16)
    for remote in remotes:
        remote.wait_send()


def wide_call(n_lat, n_lon, stream, gains, table, conv, w_qkv, w_out, w_up, w_down):
    layers = w_qkv.shape[0]
    width = stream.shape[1]
    hid = w_up.shape[2]
    vmem = pl.BlockSpec(memory_space=pltpu.VMEM)
    anywhere = pl.BlockSpec(memory_space=pltpu.HBM)
    heads = table.shape[2]
    return pl.pallas_call(
        functools.partial(wide_kernel, n_lat, n_lon),
        out_shape=pltpu.VMEM(stream.shape, BF16),
        in_specs=[anywhere] * 8,
        out_specs=vmem,
        scratch_shapes=[
            pltpu.VMEM(gains.shape, F32),
            pltpu.VMEM(table.shape, F32),
            pltpu.VMEM(conv.shape, F32),
            pltpu.VMEM(w_qkv.shape, BF16),
            pltpu.VMEM(w_out.shape, BF16),
            pltpu.VMEM(w_up.shape, BF16),
            pltpu.VMEM(w_down.shape, BF16),
            pltpu.VMEM((768, width), BF16),
            pltpu.VMEM((256, width), BF16),
            pltpu.VMEM((layers, 32 * PITCH, width), F32),
            pltpu.VMEM((layers, 832, 2 * width), BF16),
            pltpu.VMEM((26 * PITCH, width), F32),
            pltpu.VMEM((26 * PITCH, width), BF16),
            pltpu.VMEM((26 * PITCH, width), F32),
            pltpu.VMEM((2, 26 * PITCH + 16, 128), F32),
            pltpu.VMEM((3, hid // 128, 26 * 16, 128), BF16),
            pltpu.VMEM((3, hid // 128, 26 * 16, 128), BF16),
            pltpu.VMEM((16 * PITCH, hid), BF16),
            pltpu.VMEM((layers * heads, 128), F32),
            pltpu.VMEM((layers, heads, GROUP * PITCH, 256), F32),
            pltpu.VMEM((256, 384), BF16),
            pltpu.VMEM((576, 640), BF16),
            pltpu.VMEM((192, 256), BF16),
            pltpu.SemaphoreType.DMA((4,)),
            pltpu.SemaphoreType.DMA((layers, 4)),
            pltpu.SemaphoreType.DMA((5,)),
            pltpu.SemaphoreType.DMA((5,)),
            pltpu.SemaphoreType.REGULAR,
        ],
        compiler_params=pltpu.CompilerParams(
            collective_id=0, has_side_effects=True, vmem_limit_bytes=58 * 1024 * 1024
        ),
    )(stream, gains, table, conv, w_qkv, w_out, w_up, w_down)


def on_device(n_lat, n_lon, stream, gains, w_qkv, table, w_out, w_up, conv, w_down):
    rows, cols, width = stream.shape
    layers, heads = table.shape[:2]
    table = table.transpose(0, 3, 1, 2)
    conv = conv.transpose(1, 2, 0, 3)
    hid = w_up.shape[2]
    vmem = pl.BlockSpec(memory_space=pltpu.VMEM)
    anywhere = pl.BlockSpec(memory_space=pltpu.HBM)
    if n_lat == 2 and n_lon % 2 == 0 and n_lon > 2:
        result = wide_call(
            n_lat, n_lon, stream.reshape(rows * cols, width), gains, table, conv, w_qkv, w_out, w_up, w_down
        )
        return result.reshape(rows, cols, width)
    result = pl.pallas_call(
        functools.partial(kernel, n_lat, n_lon),
        out_shape=pltpu.VMEM((rows * cols, width), BF16),
        in_specs=[anywhere] * 8,
        out_specs=vmem,
        scratch_shapes=[
            pltpu.VMEM(gains.shape, F32),
            pltpu.VMEM(table.shape, F32),
            pltpu.VMEM(conv.shape, F32),
            pltpu.VMEM(w_qkv.shape, BF16),
            pltpu.VMEM(w_out.shape, BF16),
            pltpu.VMEM(w_up.shape, BF16),
            pltpu.VMEM(w_down.shape, BF16),
            pltpu.VMEM((384, 2 * width), BF16),
            pltpu.VMEM((96, 2 * width), BF16),
            pltpu.VMEM((96, 2 * width), BF16),
            pltpu.VMEM((layers, 384, width), BF16),
            pltpu.VMEM((layers, 96, width), BF16),
            pltpu.VMEM((layers, 96, width), BF16),
            pltpu.VMEM((layers, 128, width), BF16),
            pltpu.VMEM((288, hid), F32),
            pltpu.VMEM((256, hid), F32),
            pltpu.VMEM((WINDOW, layers * heads, 128), F32),
            pltpu.VMEM((WINDOW, layers * heads, 256), F32),
            pltpu.VMEM((layers, 3, 320, 256), F32),
            pltpu.VMEM((layers, 2, 128, 256), F32),
            pltpu.VMEM((384, width), BF16),
            pltpu.SemaphoreType.DMA((4,)),
            pltpu.SemaphoreType.DMA((layers, 4)),
            pltpu.SemaphoreType.DMA((layers, 8)),
            pltpu.SemaphoreType.DMA((layers, 8)),
        ],
        compiler_params=pltpu.CompilerParams(
            collective_id=0, has_side_effects=True, vmem_limit_bytes=58 * 1024 * 1024
        ),
    )(
        stream.reshape(rows * cols, width),
        gains,
        table,
        conv,
        w_qkv,
        w_out,
        w_up,
        w_down,
    )
    return result.reshape(rows, cols, width)


def solution(mesh):
    sizes = dict(mesh.shape)
    in_specs = (P("lat", "lon", None), P(), P(), P(), P(), P(), P(), P())
    return jax.shard_map(
        functools.partial(on_device, sizes["lat"], sizes["lon"]),
        mesh=mesh,
        in_specs=in_specs,
        out_specs=P("lat", "lon", None),
        check_vma=False,
    )
```

```python
import functools

import jax
import jax.numpy as jnp
from jax import lax
from jax.experimental import pallas as pl
from jax.experimental.pallas import tpu as pltpu
from jax.sharding import PartitionSpec as P

WINDOW = 7
REACH = 3
GROUP = 4
F32 = jnp.float32
BF16 = jnp.bfloat16

LEFT, RIGHT, TOP, BOTTOM, TOP_L, TOP_R, BOT_L, BOT_R = range(8)
STEPS = ((0, 1), (0, -1), (1, 0), (-1, 0), (1, 1), (1, -1), (-1, 1), (-1, -1))


def iota(shape, dim):
    return lax.broadcasted_iota(jnp.int32, shape, dim)


def hot(cond):
    return jnp.where(cond, 1.0, 0.0).astype(BF16)


def dot(a, b):
    return jnp.dot(a, b, preferred_element_type=F32)


def normed(wide, gain):
    scale = lax.rsqrt(jnp.mean(wide * wide, axis=-1, keepdims=True) + 1e-06)
    return (wide * scale * gain).astype(BF16)


def kernel(
    n_lat, n_lon, x_hbm, gains_hbm, table_hbm, conv_hbm, wqkv_hbm, wout_hbm, wup_hbm, wdown_hbm,
    out_ref, gains_ref, table, conv_ref, wqkv, wout, wup, wdown, kvb, near_l, near_r, xb, left, right, edge, lpad, pre, rows, spread,
    bias, row_bias, attn, in_sem, w_sem, send_sem, recv_sem,
):
    layers = wqkv.shape[0]
    tokens, width = x_hbm.shape
    cols = 16
    heads = table.shape[2]
    hid = wup.shape[2]
    lat = lax.axis_index("lat")
    lon = lax.axis_index("lon")
    has_up = lat > 0
    has_down = lat < n_lat - 1
    total_rows = n_lat * (tokens // cols)
    first_row = lat * (tokens // cols)

    loads = {}
    firsts = (("x", x_hbm, xb.at[0, pl.ds(64, 256)]), ("gains", gains_hbm, gains_ref), ("table", table_hbm, table), ("conv", conv_hbm, conv_ref))
    for k, (name, src, dst) in enumerate(firsts):
        loads[name] = pltpu.make_async_copy(src, dst, in_sem.at[k])
    loads["x"].start()
    loads["gains"].start()
    for n in range(layers):
        pairs = ((wqkv_hbm, wqkv), (wout_hbm, wout), (wup_hbm, wup), (wdown_hbm, wdown))
        for k, (src, dst) in enumerate(pairs):
            loads[n, k] = pltpu.make_async_copy(src.at[n], dst.at[n], w_sem.at[n, k])
            loads[n, k].start()
            if n == 0 and k == 0:
                loads["table"].start()
                loads["conv"].start()

    def target(step):
        return {"lat": lat + step[0], "lon": lax.rem(lon + step[1] + n_lon, n_lon)}

    def when_to(step, go):
        if step[0] == 0:
            go()
        else:
            pl.when(has_down if step[0] > 0 else has_up)(go)

    def when_from(step, go):
        when_to((-step[0], -step[1]), go)

    barrier = pltpu.get_barrier_semaphore()
    for step in STEPS:
        when_to(
            step,
            lambda step=step: pl.semaphore_signal(
                barrier, inc=1, device_id=target(step), device_id_type=pl.DeviceIdType.MESH
            ),
        )

    def remote(n, slot):
        own, lo, ro, ed = xb.at[n], left.at[n], right.at[n], edge.at[n]
        src, dst = (
            (ed.at[pl.ds(64, 64)], lo.at[pl.ds(16, 64)]),
            (ed.at[pl.ds(0, 64)], ro.at[pl.ds(16, 64)]),
            (own.at[pl.ds(256, 64)], own.at[pl.ds(0, 64)]),
            (own.at[pl.ds(64, 64)], own.at[pl.ds(320, 64)]),
            (ed.at[pl.ds(112, 16)], lo.at[pl.ds(0, 16)]),
            (ed.at[pl.ds(48, 16)], ro.at[pl.ds(0, 16)]),
            (ed.at[pl.ds(64, 16)], lo.at[pl.ds(80, 16)]),
            (ed.at[pl.ds(0, 16)], ro.at[pl.ds(80, 16)]),
        )[slot]
        return pltpu.make_async_remote_copy(
            src_ref=src,
            dst_ref=dst,
            send_sem=send_sem.at[n, slot],
            recv_sem=recv_sem.at[n, slot],
            device_id=target(STEPS[slot]),
            device_id_type=pl.DeviceIdType.MESH,
        )

    def send(n):
        for slot, step in enumerate(STEPS):
            when_to(step, lambda slot=slot: remote(n, slot).start())

    def receive(n):
        for slot, step in enumerate(STEPS):
            when_from(step, lambda slot=slot: remote(n, slot).wait_recv())

    @pl.when(jnp.logical_not(has_up))
    def _():
        for n in range(layers):
            xb[n, 0:64] = jnp.zeros((64, width), BF16)
            left[n, 0:16] = jnp.zeros((16, width), BF16)
            right[n, 0:16] = jnp.zeros((16, width), BF16)
        attn[320:352] = jnp.zeros((32, width), BF16)

    @pl.when(jnp.logical_not(has_down))
    def _():
        for n in range(layers):
            xb[n, 320:384] = jnp.zeros((64, width), BF16)
            left[n, 80:96] = jnp.zeros((16, width), BF16)
            right[n, 80:96] = jnp.zeros((16, width), BF16)
        attn[352:384] = jnp.zeros((32, width), BF16)

    lpad[0:16] = jnp.zeros((16, hid), F32)
    lpad[272:288] = jnp.zeros((16, hid), F32)

    m, t = iota((128, tokens), 0), iota((128, tokens), 1)
    pick_kv = hot(t == ((m & 63) >> 2) * cols + (m & 3) + jnp.where(m >= 64, cols - 4, 0))
    m, t = iota((128, 320), 0), iota((128, 320), 1)
    e = m & 31
    side = 4 * (4 * (m >> 4) + (m & 3) + 4)
    flank = jnp.where((m & 15) < 4, 128 + side + 3, jnp.where((m & 15) < 8, 224 + side, -1))
    above = jnp.where(e < 16, 48 + e, jnp.where(e == 16, 143, jnp.where(e == 17, 236, -1)))
    below = jnp.where(e < 16, 64 + e, jnp.where(e == 16, 211, jnp.where(e == 17, 304, -1)))
    pick_ring = hot(t == jnp.where(m < 64, flank, jnp.where(m < 96, above, below)))
    m, t = iota((32, 64), 0), iota((32, 64), 1)
    pick_side = hot(t == ((m & 15) >> 2) * 16 + (m & 3) + jnp.where(m < 16, 0, 4))
    t, k = iota((tokens, 64), 0), iota((tokens, 64), 1)
    place = hot(((k & 15) == (t >> 4)) & ((t & 15) == jnp.where(k < 32, 0, cols - 1)))
    head_of = iota((1, width), 1) >> 6
    head_hot = [hot(head_of == h) for h in range(heads)]

    def prepare(pick):
        for at in (0, 128):
            for b in range(WINDOW):
                spread[b, :, at : at + 128] = jnp.take_along_axis(
                    rows[b], pick[:, at : at + 128], axis=1
                )

    def chosen(row, offset):
        value = jnp.broadcast_to(spread[0, row : row + 1, :], offset.shape)
        for b in range(1, WINDOW):
            value = jnp.where(offset == b - REACH, spread[b, row : row + 1, :], value)
        return value

    def build_bias():
        for n in range(layers):
            for b in range(WINDOW):
                rows[b, heads * n : heads * (n + 1), 0 : 2 * WINDOW - 1] = table[n, b]
        x = iota((16, 256), 1)
        j = iota((16, 256), 0)
        own = x < 160
        on_left = x < 208
        y = jnp.where(on_left, x - 160, x - 208)
        p = jnp.where(own, x >> 4, (y >> 2) - 1)
        c = jnp.where(own, x & 15, jnp.where(on_left, (y & 3) - 4, (y & 3) + cols))
        col_ok = (c - j >= -REACH) & (c - j <= REACH)
        for i in range(GROUP):
            oks = []
            for group in (0, 1, 3):
                g = first_row + GROUP * group + i
                start = jnp.clip(g - REACH, 0, total_rows - WINDOW)
                r = first_row + GROUP * group - REACH + p
                oks.append(col_ok & (r >= start) & (r < start + WINDOW))
            prepare(jnp.clip(p[0:8] - i + REACH, 0, 2 * WINDOW - 2))
            for n in range(layers):
                for h in range(heads):
                    value = chosen(n * heads + h, c - j)
                    at = h * 80 + i * 16
                    for var in range(3):
                        bias[n, var, at : at + 16, :] = jnp.where(oks[var], value, -1000000000.0)
        e = iota((16, 256), 0)
        i, j = e & 3, jnp.where(e < 4, -1, cols)
        px, cx = p, c
        col_ok = (cx - j >= -REACH) & (cx - j <= REACH)
        oks = []
        for group in (0, 1, 3):
            g = first_row + GROUP * group + i
            start = jnp.clip(g - REACH, 0, total_rows - WINDOW)
            r = first_row + GROUP * group - REACH + px
            oks.append(col_ok & (r >= start) & (r < start + WINDOW))
        pick = jnp.clip(px - i + REACH, 0, 2 * WINDOW - 2)[0:8]
        for n in range(layers):
            for h in range(heads):
                value = jnp.zeros((8, 256), F32)
                for b in range(WINDOW):
                    source = jnp.broadcast_to(rows[b, n * heads + h : n * heads + h + 1, :], (8, 128))
                    got = [
                        jnp.take_along_axis(source, pick[:, at : at + 128], axis=1)
                        for at in (0, 128)
                    ]
                    value = jnp.where(
                        (cx - j)[0:8] == b - REACH, jnp.concatenate(got, axis=1), value
                    )
                at = h * 80 + 64
                for var in range(3):
                    bias[n, var, at : at + 8, :] = jnp.where(oks[var][0:8], value, -1000000000.0)
                    bias[n, var, at + 8 : at + 16, :] = jnp.zeros((8, 256), F32)
        x, e = iota((32, 256), 1), iota((32, 256), 0)
        j = jnp.where(e < 16, e, jnp.where(e == 16, -1, cols))
        own, on_left = x < 160, x < 208
        y = jnp.where(on_left, x - 160, x - 208)
        c = jnp.where(own, x & 15, jnp.where(on_left, (y & 3) - 4, (y & 3) + cols))
        for k, (here, first_own, first_near) in enumerate(((-1, -4, -4), (16, 10, 8))):
            away = jnp.where(own, first_own + (x >> 4), first_near + (y >> 2)) - here
            ok = (c - j >= -REACH) & (c - j <= REACH) & (away >= -REACH) & (away <= REACH)
            prepare(jnp.clip(away[0:8] + WINDOW - 1, 0, 2 * WINDOW - 2))
            for n in range(layers):
                for h in range(heads):
                    value = chosen(n * heads + h, c - j)
                    row_bias[n, k, h * 32 : h * 32 + 32, :] = jnp.where(ok, value, -1000000000.0)

    def attend(q, near, held, count):
        stacked = jnp.concatenate([q * head_hot[h] for h in range(heads)], axis=0)
        scores = lax.dot_general(
            stacked, near[:, :width], (((1,), (1,)), ((), ())), preferred_element_type=F32
        )
        scores = scores + held
        raised = jnp.exp(scores - jnp.max(scores, axis=-1, keepdims=True))
        weights = (raised * (1.0 / jnp.sum(raised, axis=-1, keepdims=True))).astype(BF16)
        mixed = dot(weights, near[:, width:])
        total = jnp.where(head_of == 0, mixed[0:count], 0.0)
        for h in range(1, heads):
            total = jnp.where(head_of == h, mixed[count * h : count * (h + 1)], total)
        return total.astype(BF16)

    def near_keys(own, side):
        parts = [kvb[own : own + 160, :], near_l[side : side + 48, :], near_r[side : side + 48, :]]
        return jnp.concatenate(parts, axis=0)

    scale = (width // heads) ** (-0.5)
    loads["x"].wait()
    for n in range(layers):
        current = xb[n, 64:320]
        edge[n] = dot(pick_kv, current).astype(BF16)
        if n == 0:
            count = 2 + jnp.where(has_up, 3, 0) + jnp.where(has_down, 3, 0)
            pl.semaphore_wait(barrier, count)
        send(n)
        if n == 0:
            loads["gains"].wait()
        gain = gains_ref[n, 0:1, :]
        wide = current.astype(F32)
        norm = normed(wide, gain)
        loads[n, 0].wait()
        kvb[64:320] = dot(norm, wqkv[n, :, width:]).astype(BF16)
        query = (dot(norm, wqkv[n, :, :width]).astype(BF16) * scale).astype(BF16)
        if n == 0:
            loads["table"].wait()
            build_bias()
            loads["conv"].wait()
        receive(n)
        around = jnp.concatenate([xb[n, 0:64], xb[n, 320:384], left[n], right[n]], axis=0)
        ring = dot(pick_ring, around)
        near = dot(normed(around.astype(F32), gain), wqkv[n, :, width:]).astype(BF16)
        kvb[0:64] = near[0:64]
        kvb[320:384] = near[64:128]
        near_l[...] = near[128:224]
        near_r[...] = near[224:320]
        ring_query = (dot(normed(ring, gain), wqkv[n, :, :width]).astype(BF16) * scale).astype(BF16)
        for group in range(4):
            at = 64 * group
            more = slice(16 * group, 16 * group + 16)
            q = jnp.concatenate([query[at : at + 64], ring_query[more]], axis=0)
            held = bias[n, (0, 1, 1, 2)[group]]
            got = attend(q, near_keys(at + 16, 16 * group), held, 80)
            attn[at : at + 64, :] = got[0:64]
            attn[256 + 16 * group : 272 + 16 * group, :] = got[64:80]

        @pl.when(has_up)
        def _():
            attn[320:352] = attend(ring_query[64:96], near_keys(0, 0), row_bias[n, 0], 32)

        @pl.when(has_down)
        def _():
            attn[352:384] = attend(ring_query[96:128], near_keys(224, 48), row_bias[n, 1], 32)

        loads[n, 1].wait()
        after = jnp.concatenate([wide, ring], axis=0) + dot(attn[...], wout[n])
        norm = normed(after, gains_ref[n, 1:2, :])
        after = after[0:tokens]
        loads[n, 2].wait()
        lift = dot(norm, wup[n]).astype(BF16)
        sides = dot(pick_side, lift[256:320])
        rims = lift[320:384].astype(F32)
        lpad[16:272] = lift[0:tokens].astype(F32)
        col = iota((tokens, 128), 0) & 15
        for ch in range(hid // 128):
            at = slice(128 * ch, 128 * ch + 128)
            above, here, below = lpad[0:256, at], lpad[16:272, at], lpad[32:288, at]

            def column(b):
                return (
                    conv_ref[0, b, n : n + 1, at] * above
                    + conv_ref[1, b, n : n + 1, at] * here
                    + conv_ref[2, b, n : n + 1, at] * below
                )

            pre[:, at] = (
                column(1)
                + jnp.where(col > 0, pltpu.roll(column(0), 1, 0), 0.0)
                + jnp.where(col < cols - 1, pltpu.roll(column(2), tokens - 1, 0), 0.0)
            )
        line = iota((16, hid), 0)

        def tap(a, b):
            return conv_ref[a, b, n : n + 1, :]

        def row_part(a, rim):
            middle = rim[0:16]
            back = jnp.where(line == 0, rim[16:17], pltpu.roll(middle, 1, 0))
            ahead = jnp.where(line == 15, rim[17:18], pltpu.roll(middle, 15, 0))
            return tap(a, 0) * back + tap(a, 1) * middle + tap(a, 2) * ahead

        def col_part(b, values):
            up = jnp.where(line == 0, 0.0, pltpu.roll(values, 1, 0))
            down = jnp.where(line == 15, 0.0, pltpu.roll(values, 15, 0))
            return tap(0, b) * up + tap(1, b) * values + tap(2, b) * down

        pieces = []
        for part in (col_part(0, sides[0:16]), col_part(2, sides[16:32])):
            high = part.astype(BF16)
            pieces += [high, (part - high.astype(F32)).astype(BF16)]
        pre[0:16] += row_part(0, rims[0:32])
        pre[240:256] += row_part(2, rims[32:64])
        whole = pre[...] + dot(place, jnp.concatenate(pieces, axis=0))
        hidden = jax.nn.gelu(whole, approximate=True).astype(BF16)
        loads[n, 3].wait()
        result = (after + dot(hidden, wdown[n])).astype(BF16)
        if n == layers - 1:
            out_ref[...] = result
        else:
            xb[n + 1, 64:320] = result

    for n in range(layers):
        for slot, step in enumerate(STEPS):
            when_to(step, lambda slot=slot: remote(n, slot).wait_send())


PITCH = 24
HALO = 8


def halved(a, b):
    half = a.shape[0] // 32 * 16
    return jnp.concatenate([dot(a[:half], b), dot(a[half:], b)], axis=0)


def wide_kernel(
    n_lat, n_lon, x_hbm, gains_hbm, table_hbm, conv_hbm, wqkv_hbm, wout_hbm, wup_hbm, wdown_hbm,
    out_ref, gains_ref, table, conv_ref, wqkv, wout, wup, wdown, raw, stage, edge, xf, kvb, qf, attn, af, nf, lifted, lifted_b, hidden, rows,
    bias, place, result, in_sem, w_sem, send_sem, recv_sem, here_sem,
):
    layers = wqkv.shape[0]
    tokens, width = x_hbm.shape
    cols = 16
    heads = table.shape[2]
    hid = wup.shape[2]
    chunks = hid // 128
    lat = lax.axis_index("lat")
    lon = lax.axis_index("lon")
    odd = lax.rem(lon, 2)
    near = lon + 1 - 2 * odd
    far = lax.rem(lon - 1 + 2 * odd + n_lon, n_lon)

    loads = {}
    firsts = (("x", x_hbm, raw), ("gains", gains_hbm, gains_ref), ("table", table_hbm, table), ("conv", conv_hbm, conv_ref))
    for k, (name, src, dst) in enumerate(firsts):
        loads[name] = pltpu.make_async_copy(src, dst, in_sem.at[k])
        loads[name].start()
    for n in range(layers):
        pairs = ((wqkv_hbm, wqkv), (wout_hbm, wout), (wup_hbm, wup), (wdown_hbm, wdown))
        for k, (src, dst) in enumerate(pairs):
            loads[n, k] = pltpu.make_async_copy(src.at[n], dst.at[n], w_sem.at[n, k])
            loads[n, k].start()

    barrier = pltpu.get_barrier_semaphore()
    partners = ((lat, near), (1 - lat, near), (1 - lat, lon), (lat, far), (1 - lat, far))
    first, last = lon == 0, lon == n_lon - 1

    def greet(semaphore, row, col):
        pl.semaphore_signal(
            semaphore, inc=1, device_id={"lat": row, "lon": col}, device_id_type=pl.DeviceIdType.MESH
        )

    for row, col in partners[:3]:
        greet(barrier, row, col)

    eager = first | ((odd == 1) & jnp.logical_not(last))

    @pl.when(eager)
    def _():
        for row, col in partners[3:]:
            greet(barrier, row, col)

    def greet_back():
        for row, col in partners[3:]:
            greet(here_sem, row, col)

    @pl.when(last)
    def _():
        pl.semaphore_wait(barrier, len(partners))
        greet_back()

    remotes = []
    pieces = (
        (edge.at[pl.ds(0, 128)], stage.at[pl.ds(0, 128)]),
        (edge.at[pl.ds(128, 64)], stage.at[pl.ds(128, 64)]),
        (edge.at[pl.ds(384, 128)], stage.at[pl.ds(192, 128)]),
        (edge.at[pl.ds(192, 128)], stage.at[pl.ds(320, 128)]),
        (edge.at[pl.ds(320, 64)], stage.at[pl.ds(448, 64)]),
    )
    for slot, (src, dst) in enumerate(pieces):
        remotes.append(
            pltpu.make_async_remote_copy(
                src_ref=src,
                dst_ref=dst,
                send_sem=send_sem.at[slot],
                recv_sem=recv_sem.at[slot],
                device_id={"lat": partners[slot][0], "lon": partners[slot][1]},
                device_id_type=pl.DeviceIdType.MESH,
            )
        )

    def flip(value, by):
        return value + by * (cols - 1 - 2 * value)

    def choose(count, shift, column):
        m, t = iota((count, 1), 0), iota((count, tokens), 1)
        i = m & ((1 << shift) - 1)
        v = i if shift == 4 else cols - 1 - i
        return hot(t == flip(v, lat) * cols + flip(column(m >> shift), odd))

    picks = (
        choose(128, 4, lambda k: 15 - k),
        choose(64, 3, lambda k: 15 - k),
        choose(128, 4, lambda k: 7 - k),
        choose(64, 3, lambda k: 7 - k),
        choose(128, 3, lambda k: k),
    )
    picks = jnp.concatenate(picks, axis=0)
    pick_own = choose(256, 4, lambda k: k)
    loads["x"].wait()
    edge[...] = halved(picks, raw[...]).astype(BF16)
    @pl.when(jnp.logical_not(last))
    def _():
        pl.semaphore_wait(barrier, len(partners) - jnp.where(eager, 2, 0))

    for remote in remotes[:3]:
        remote.start()

    @pl.when(jnp.logical_not(eager | last))
    def _():
        greet_back()

    @pl.when(last)
    def _():
        for remote in remotes[3:]:
            remote.start()

    def answer():
        @pl.when(first)
        def _():
            pl.semaphore_wait(here_sem, 2)
            for remote in remotes[3:]:
                remote.start()

    kvb[0, 768:832] = jnp.zeros((64, 2 * width), BF16)
    kvb[1, 672:832] = jnp.zeros((160, 2 * width), BF16)

    m, t = iota((256, 256), 0), iota((256, 256), 1)
    u, v = flip(m & 15, odd), flip(m >> 4, lat)
    for k in range(2):
        place[k] = hot(t == (u - 8 * k) * PITCH + v)

    loads["table"].wait()
    for n in range(layers):
        for b in range(WINDOW):
            rows[heads * n : heads * (n + 1), 16 * b : 16 * b + 2 * WINDOW - 1] = table[n, b]
    lane, v = iota((PITCH, 256), 1), iota((PITCH, 256), 0)
    start = jnp.maximum(v - REACH, 0)
    for n in range(layers):
        if n == 0:
            double = (lane * 1366) >> 16
            rest = lane - 2 * PITCH * double
            key_u = 2 * double + jnp.where(rest < 32, rest >> 4, (rest - 32) >> 3)
            key_v = jnp.where(rest < 32, rest & 15, 16 + (rest & 7))
        else:
            key_u = (lane * 2731) >> 16
            key_v = lane - PITCH * key_u
        row_ok = (key_v >= start) & (key_v < start + WINDOW)
        away = jnp.clip((key_v - v) * (1 - 2 * lat) + WINDOW - 1, 0, 2 * WINDOW - 2)
        for q in range(GROUP):
            off = key_u - REACH - q
            ok = row_ok & (off >= -REACH) & (off <= REACH)
            at = jnp.clip(off * (1 - 2 * odd) + REACH, 0, WINDOW - 1) * 16 + away
            for h in range(heads):
                line = jnp.broadcast_to(rows[n * heads + h : n * heads + h + 1, :], (PITCH, 128))
                got = [jnp.take_along_axis(line, at[:, s : s + 128], axis=1) for s in (0, 128)]
                value = jnp.where(ok, jnp.concatenate(got, axis=1) * 1.4426950408889634, -1000000000.0)
                bias[n, h, PITCH * q : PITCH * (q + 1), :] = value

    head_of = iota((1, width), 1) >> 6
    head_hot = [hot(head_of == h) for h in range(heads)]
    low_half = (iota((1, width), 1) & 127) < 64
    log2e = 1.4426950408889634
    scale = (width // heads) ** (-0.5) * log2e

    def multiply(n, wide):
        norm = normed(wide, gains_ref[n, 0:1, :])
        product = halved if wide.shape[0] > 256 else dot
        return product(norm, wqkv[n, :, width:]).astype(BF16), product(norm, wqkv[n, :, :width])

    def project(n, first, count, q_from, q_count):
        kv, query = multiply(n, xf[n, PITCH * first : PITCH * (first + count), :])
        kvb[n, PITCH * first : PITCH * (first + count), :] = kv
        at = PITCH * (q_from + 3 - first)
        qf[PITCH * q_from : PITCH * (q_from + q_count), :] = query[at : at + PITCH * q_count]

    def spread(wide, kv, query, at, shift, first, count):
        high = 1 << shift
        low = 0 if shift == 4 else 16
        for k in range(count):
            here = slice(at + high * k, at + high * (k + 1))
            to = PITCH * (first + k) + low
            xf[0, to : to + high, :] = wide[here]
            j = first + k - 3
            if 0 <= j < 26:
                qf[PITCH * j + low : PITCH * j + low + high, :] = query[here]
        for p in range(count // 2):
            to = PITCH * (first + 2 * p) + 2 * low
            kvb[0, to : to + 2 * high, :] = kv[at + 2 * high * p : at + 2 * high * (p + 1)]

    def attend(n, tiles):
        def score(j, w):
            count = PITCH * w
            q = (qf[PITCH * j : PITCH * (j + w), :] * scale).astype(BF16)
            keys = kvb[n, PITCH * j : PITCH * j + 256, 0:width]
            stacked = jnp.concatenate([q * head_hot[h] for h in range(heads)], axis=0)
            return lax.dot_general(stacked, keys, (((1,), (1,)), ((), ())), preferred_element_type=F32)

        def soften(scores, w):
            count = PITCH * w
            weights = []
            for h in range(heads):
                held = scores[count * h : count * (h + 1)] + bias[n, h, 0:count, :]
                weights.append(jnp.exp2((held - jnp.max(held, axis=-1, keepdims=True)).astype(BF16)))
            return weights

        def gather_values(weights, j, w):
            count = PITCH * w
            for pair in range(heads // 2):
                at = width + 128 * pair
                own = kvb[n, PITCH * j : PITCH * j + 256, at : at + 128]
                values = jnp.concatenate([own, jnp.ones(own.shape, BF16)], axis=1)
                both = jnp.concatenate(weights[2 * pair : 2 * pair + 2], axis=0)
                mixed = dot(both, values)
                mixed = jnp.where(low_half, mixed[0:count], mixed[count : 2 * count])
                total = mixed[:, 0:128] * (1.0 / mixed[:, 128:256])
                attn[PITCH * j : PITCH * (j + w), 128 * pair : 128 * (pair + 1)] = total.astype(BF16)

        ahead = [score(*tile) for tile in tiles[:2]]
        for k, (j, w) in enumerate(tiles):
            weights = soften(ahead[k], w)
            if k + 2 < len(tiles):
                ahead.append(score(*tiles[k + 2]))
            gather_values(weights, j, w)

    def tap(n, a, b, ch):
        return conv_ref[a + lat * (2 - 2 * a), b + odd * (2 - 2 * b), n : n + 1, 128 * ch : 128 * (ch + 1)]

    def feed(n, j0, count, tiles, o0, outs, then=None):
        attend(n, tiles)
        size = PITCH * count
        here = slice(PITCH * j0, PITCH * j0 + size)
        wide = xf[n, PITCH * (j0 + 3) : PITCH * (j0 + 3) + size, :]
        after = wide + (halved if size > 256 else dot)(attn[here], wout[n])
        af[here] = after
        scaled = lax.rsqrt(jnp.mean(after * after, axis=-1, keepdims=True) + 1e-06)
        line = iota((size, 1), 0)
        line = line - PITCH * ((line * 2731) >> 16)
        scaled = jnp.where(line == PITCH - 1, 0.0, scaled)
        norm = after * scaled * gains_ref[n, 1:2, :]
        for k in range(2):
            nf[k, 8 + PITCH * j0 : 8 + PITCH * j0 + size, :] = norm[:, 128 * k : 128 * (k + 1)]
        high = PITCH if n == 0 else 16
        more = 1 if n == 0 and j0 == 0 else 0
        moved = []
        for a in range(3):
            halves = []
            for k in range(2):
                if n == 0:
                    at = 8 + PITCH * j0 + a - 1
                    halves.append(nf[k, at : at + size + PITCH * more, :].astype(BF16))
                else:
                    spots = [8 + PITCH * j + a - 1 for j in range(j0, j0 + count)]
                    halves.append(jnp.concatenate([nf[k, at : at + 16, :] for at in spots], axis=0).astype(BF16))
            moved.append(jnp.concatenate(halves, axis=1))
        tall = moved[0].shape[0]
        moved = jnp.concatenate(moved, axis=0)
        for double in range(chunks // 2):
            product = dot(moved, wup[n, :, 256 * double : 256 * (double + 1)])
            for a in range(3):
                both = product[tall * a : tall * (a + 1)]
                for ch in (2 * double, 2 * double + 1):
                    lift = both[:, 128 * (ch % 2) : 128 * (ch % 2 + 1)]
                    if n == 0:
                        lift = lift.reshape(count + more, PITCH, 128)
                        base = lift[0:count, 0:16].reshape(16 * count, 128).astype(BF16)
                        over = lift[:, 16:PITCH]
                        pairs = jnp.concatenate([over[:-1], over[1:]], axis=1).reshape(-1, 128)
                        lifted_b[a, ch, 16 * j0 : 16 * (j0 + count + more - 1), :] = pairs.astype(BF16)
                    else:
                        base = lift.astype(BF16)
                    lifted[a, ch, 16 * j0 : 16 * (j0 + count), :] = base
        if then is not None:
            then()
        for ch in range(chunks):
            taps = [[tap(n, a, b, ch).astype(BF16) for b in range(3)] for a in range(3)]

            def convolved(source, j, wide):
                total = None
                for a in range(3):
                    for b in range(3):
                        at = 16 * (j + b - 1)
                        term = taps[a][b] * source[a, ch, at : at + 16 * wide, :]
                        total = term if total is None else total + term
                half = 0.5 * total
                inner = total * (0.7978845608028654 + 0.035677408136300125 * (total * total))
                return half + half * jnp.tanh(inner)

            for part in range(0, outs, 2):
                main = convolved(lifted, o0 + part, 2)
                if n == 0:
                    rest = convolved(lifted_b, o0 + part, 1).astype(F32)
                    main = main.astype(F32)
                    main = jnp.concatenate([main[0:16], rest[0:8], main[16:32], rest[8:16]], axis=0).astype(BF16)
                hidden[high * part : high * (part + 2), 128 * ch : 128 * (ch + 1)] = main
        down = (halved if high * outs > 256 else dot)(hidden[0 : high * outs], wdown[n])
        if n == 0:
            xf[1, PITCH * (o0 + 3) : PITCH * (o0 + 3 + outs), :] = af[PITCH * o0 : PITCH * (o0 + outs)] + down
        else:
            for k in range(outs):
                at = PITCH * (o0 + k)
                out = af[at : at + 16] + down[16 * k : 16 * (k + 1)]
                af[at : at + 16] = out

    loads["gains"].wait()
    loads[0, 0].wait()
    wide = dot(pick_own, raw[...])
    kv, query = multiply(0, wide)
    spread(wide, kv, query, 0, 4, 8, 16)
    remotes[2].wait_recv()
    wide = stage[192:320].astype(F32)
    kv, query = multiply(0, wide)
    spread(wide, kv, query, 0, 3, 8, 16)
    attend(0, ((8, 4), (12, 4)))
    for k in (0, 1):
        remotes[k].wait_recv()

    @pl.when(eager & jnp.logical_not(first))
    def _():
        pl.semaphore_wait(here_sem, 2)

    @pl.when(jnp.logical_not(first | last))
    def _():
        for remote in remotes[3:]:
            remote.start()

    wide = stage[0:192].astype(F32)
    kv, query = multiply(0, wide)
    spread(wide, kv, query, 0, 4, 24, 8)
    spread(wide, kv, query, 128, 3, 24, 8)
    loads["conv"].wait()
    for k in range(1, 4):
        loads[0, k].wait()
    feed(0, 8, 18, ((16, 4), (20, 4), (24, 2)), 9, 16, answer)
    for k in range(4):
        loads[1, k].wait()
    project(1, 12, 16, 9, 13)
    feed(1, 12, 10, ((12, 4), (16, 4), (20, 2)), 13, 8)
    result[...] = dot(place[1, :, 0:192], af[PITCH * 13 : PITCH * 21].astype(BF16))
    for k in (3, 4):
        remotes[k].wait_recv()
    wide = stage[320:512].astype(F32)
    kv, query = multiply(0, wide)
    spread(wide, kv, query, 0, 4, 0, 8)
    spread(wide, kv, query, 128, 3, 0, 8)
    feed(0, 0, 8, ((0, 4), (4, 4)), 1, 8)
    project(1, 4, 8, 4, 5)
    feed(1, 4, 8, ((4, 4), (8, 4)), 5, 8)
    out_ref[...] = (result[...] + dot(place[0, :, 0:192], af[PITCH * 5 : PITCH * 13].astype(BF16))).astype(BF16)
    for remote in remotes:
        remote.wait_send()


def wide_call(n_lat, n_lon, stream, gains, table, conv, w_qkv, w_out, w_up, w_down):
    layers = w_qkv.shape[0]
    width = stream.shape[1]
    hid = w_up.shape[2]
    vmem = pl.BlockSpec(memory_space=pltpu.VMEM)
    anywhere = pl.BlockSpec(memory_space=pltpu.HBM)
    heads = table.shape[2]
    return pl.pallas_call(
        functools.partial(wide_kernel, n_lat, n_lon),
        out_shape=pltpu.VMEM(stream.shape, BF16),
        in_specs=[anywhere] * 8,
        out_specs=vmem,
        scratch_shapes=[
            pltpu.VMEM(gains.shape, F32),
            pltpu.VMEM(table.shape, F32),
            pltpu.VMEM(conv.shape, F32),
            pltpu.VMEM(w_qkv.shape, BF16),
            pltpu.VMEM(w_out.shape, BF16),
            pltpu.VMEM(w_up.shape, BF16),
            pltpu.VMEM(w_down.shape, BF16),
            pltpu.VMEM((256, width), BF16),
            pltpu.VMEM((512, width), BF16),
            pltpu.VMEM((512, width), BF16),
            pltpu.VMEM((layers, 32 * PITCH, width), F32),
            pltpu.VMEM((layers, 832, 2 * width), BF16),
            pltpu.VMEM((26 * PITCH, width), F32),
            pltpu.VMEM((26 * PITCH, width), BF16),
            pltpu.VMEM((26 * PITCH, width), F32),
            pltpu.VMEM((2, 26 * PITCH + 16, 128), F32),
            pltpu.VMEM((3, hid // 128, 26 * 16, 128), BF16),
            pltpu.VMEM((3, hid // 128, 26 * 16, 128), BF16),
            pltpu.VMEM((16 * PITCH, hid), BF16),
            pltpu.VMEM((layers * heads, 128), F32),
            pltpu.VMEM((layers, heads, GROUP * PITCH, 256), F32),
            pltpu.VMEM((2, 256, 256), BF16),
            pltpu.VMEM((256, width), F32),
            pltpu.SemaphoreType.DMA((4,)),
            pltpu.SemaphoreType.DMA((layers, 4)),
            pltpu.SemaphoreType.DMA((5,)),
            pltpu.SemaphoreType.DMA((5,)),
            pltpu.SemaphoreType.REGULAR,
        ],
        compiler_params=pltpu.CompilerParams(
            collective_id=0, has_side_effects=True, vmem_limit_bytes=58 * 1024 * 1024
        ),
    )(stream, gains, table, conv, w_qkv, w_out, w_up, w_down)


def on_device(n_lat, n_lon, stream, gains, w_qkv, table, w_out, w_up, conv, w_down):
    rows, cols, width = stream.shape
    layers, heads = table.shape[:2]
    table = table.transpose(0, 3, 1, 2)
    conv = conv.transpose(1, 2, 0, 3)
    hid = w_up.shape[2]
    vmem = pl.BlockSpec(memory_space=pltpu.VMEM)
    anywhere = pl.BlockSpec(memory_space=pltpu.HBM)
    if n_lat == 2 and n_lon % 2 == 0 and n_lon > 2:
        result = wide_call(
            n_lat, n_lon, stream.reshape(rows * cols, width), gains, table, conv, w_qkv, w_out, w_up, w_down
        )
        return result.reshape(rows, cols, width)
    result = pl.pallas_call(
        functools.partial(kernel, n_lat, n_lon),
        out_shape=pltpu.VMEM((rows * cols, width), BF16),
        in_specs=[anywhere] * 8,
        out_specs=vmem,
        scratch_shapes=[
            pltpu.VMEM(gains.shape, F32),
            pltpu.VMEM(table.shape, F32),
            pltpu.VMEM(conv.shape, F32),
            pltpu.VMEM(w_qkv.shape, BF16),
            pltpu.VMEM(w_out.shape, BF16),
            pltpu.VMEM(w_up.shape, BF16),
            pltpu.VMEM(w_down.shape, BF16),
            pltpu.VMEM((384, 2 * width), BF16),
            pltpu.VMEM((96, 2 * width), BF16),
            pltpu.VMEM((96, 2 * width), BF16),
            pltpu.VMEM((layers, 384, width), BF16),
            pltpu.VMEM((layers, 96, width), BF16),
            pltpu.VMEM((layers, 96, width), BF16),
            pltpu.VMEM((layers, 128, width), BF16),
            pltpu.VMEM((288, hid), F32),
            pltpu.VMEM((256, hid), F32),
            pltpu.VMEM((WINDOW, layers * heads, 128), F32),
            pltpu.VMEM((WINDOW, layers * heads, 256), F32),
            pltpu.VMEM((layers, 3, 320, 256), F32),
            pltpu.VMEM((layers, 2, 128, 256), F32),
            pltpu.VMEM((384, width), BF16),
            pltpu.SemaphoreType.DMA((4,)),
            pltpu.SemaphoreType.DMA((layers, 4)),
            pltpu.SemaphoreType.DMA((layers, 8)),
            pltpu.SemaphoreType.DMA((layers, 8)),
        ],
        compiler_params=pltpu.CompilerParams(
            collective_id=0, has_side_effects=True, vmem_limit_bytes=58 * 1024 * 1024
        ),
    )(
        stream.reshape(rows * cols, width),
        gains,
        table,
        conv,
        w_qkv,
        w_out,
        w_up,
        w_down,
    )
    return result.reshape(rows, cols, width)


def solution(mesh):
    sizes = dict(mesh.shape)
    in_specs = (P("lat", "lon", None), P(), P(), P(), P(), P(), P(), P())
    return jax.shard_map(
        functools.partial(on_device, sizes["lat"], sizes["lon"]),
        mesh=mesh,
        in_specs=in_specs,
        out_specs=P("lat", "lon", None),
        check_vma=False,
    )
```

```python
import functools

import jax
import jax.numpy as jnp
from jax import lax
from jax.experimental import pallas as pl
from jax.experimental.pallas import tpu as pltpu
from jax.sharding import PartitionSpec as P

WINDOW = 7
REACH = 3
GROUP = 4
F32 = jnp.float32
BF16 = jnp.bfloat16

LEFT, RIGHT, TOP, BOTTOM, TOP_L, TOP_R, BOT_L, BOT_R = range(8)
STEPS = ((0, 1), (0, -1), (1, 0), (-1, 0), (1, 1), (1, -1), (-1, 1), (-1, -1))


def iota(shape, dim):
    return lax.broadcasted_iota(jnp.int32, shape, dim)


def hot(cond):
    return jnp.where(cond, 1.0, 0.0).astype(BF16)


def dot(a, b):
    return jnp.dot(a, b, preferred_element_type=F32)


def normed(wide, gain):
    scale = lax.rsqrt(jnp.mean(wide * wide, axis=-1, keepdims=True) + 1e-06)
    return (wide * scale * gain).astype(BF16)


def kernel(
    n_lat, n_lon, x_hbm, gains_hbm, table_hbm, conv_hbm, wqkv_hbm, wout_hbm, wup_hbm, wdown_hbm,
    out_ref, gains_ref, table, conv_ref, wqkv, wout, wup, wdown, kvb, near_l, near_r, xb, left, right, edge, lpad, pre, rows, spread,
    bias, row_bias, attn, in_sem, w_sem, send_sem, recv_sem,
):
    layers = wqkv.shape[0]
    tokens, width = x_hbm.shape
    cols = 16
    heads = table.shape[2]
    hid = wup.shape[2]
    lat = lax.axis_index("lat")
    lon = lax.axis_index("lon")
    has_up = lat > 0
    has_down = lat < n_lat - 1
    total_rows = n_lat * (tokens // cols)
    first_row = lat * (tokens // cols)

    loads = {}
    firsts = (("x", x_hbm, xb.at[0, pl.ds(64, 256)]), ("gains", gains_hbm, gains_ref), ("table", table_hbm, table), ("conv", conv_hbm, conv_ref))
    for k, (name, src, dst) in enumerate(firsts):
        loads[name] = pltpu.make_async_copy(src, dst, in_sem.at[k])
    loads["x"].start()
    loads["gains"].start()
    for n in range(layers):
        pairs = ((wqkv_hbm, wqkv), (wout_hbm, wout), (wup_hbm, wup), (wdown_hbm, wdown))
        for k, (src, dst) in enumerate(pairs):
            loads[n, k] = pltpu.make_async_copy(src.at[n], dst.at[n], w_sem.at[n, k])
            loads[n, k].start()
            if n == 0 and k == 0:
                loads["table"].start()
                loads["conv"].start()

    def target(step):
        return {"lat": lat + step[0], "lon": lax.rem(lon + step[1] + n_lon, n_lon)}

    def when_to(step, go):
        if step[0] == 0:
            go()
        else:
            pl.when(has_down if step[0] > 0 else has_up)(go)

    def when_from(step, go):
        when_to((-step[0], -step[1]), go)

    barrier = pltpu.get_barrier_semaphore()
    for step in STEPS:
        when_to(
            step,
            lambda step=step: pl.semaphore_signal(
                barrier, inc=1, device_id=target(step), device_id_type=pl.DeviceIdType.MESH
            ),
        )

    def remote(n, slot):
        own, lo, ro, ed = xb.at[n], left.at[n], right.at[n], edge.at[n]
        src, dst = (
            (ed.at[pl.ds(64, 64)], lo.at[pl.ds(16, 64)]),
            (ed.at[pl.ds(0, 64)], ro.at[pl.ds(16, 64)]),
            (own.at[pl.ds(256, 64)], own.at[pl.ds(0, 64)]),
            (own.at[pl.ds(64, 64)], own.at[pl.ds(320, 64)]),
            (ed.at[pl.ds(112, 16)], lo.at[pl.ds(0, 16)]),
            (ed.at[pl.ds(48, 16)], ro.at[pl.ds(0, 16)]),
            (ed.at[pl.ds(64, 16)], lo.at[pl.ds(80, 16)]),
            (ed.at[pl.ds(0, 16)], ro.at[pl.ds(80, 16)]),
        )[slot]
        return pltpu.make_async_remote_copy(
            src_ref=src,
            dst_ref=dst,
            send_sem=send_sem.at[n, slot],
            recv_sem=recv_sem.at[n, slot],
            device_id=target(STEPS[slot]),
            device_id_type=pl.DeviceIdType.MESH,
        )

    def send(n):
        for slot, step in enumerate(STEPS):
            when_to(step, lambda slot=slot: remote(n, slot).start())

    def receive(n):
        for slot, step in enumerate(STEPS):
            when_from(step, lambda slot=slot: remote(n, slot).wait_recv())

    @pl.when(jnp.logical_not(has_up))
    def _():
        for n in range(layers):
            xb[n, 0:64] = jnp.zeros((64, width), BF16)
            left[n, 0:16] = jnp.zeros((16, width), BF16)
            right[n, 0:16] = jnp.zeros((16, width), BF16)
        attn[320:352] = jnp.zeros((32, width), BF16)

    @pl.when(jnp.logical_not(has_down))
    def _():
        for n in range(layers):
            xb[n, 320:384] = jnp.zeros((64, width), BF16)
            left[n, 80:96] = jnp.zeros((16, width), BF16)
            right[n, 80:96] = jnp.zeros((16, width), BF16)
        attn[352:384] = jnp.zeros((32, width), BF16)

    lpad[0:16] = jnp.zeros((16, hid), F32)
    lpad[272:288] = jnp.zeros((16, hid), F32)

    m, t = iota((128, tokens), 0), iota((128, tokens), 1)
    pick_kv = hot(t == ((m & 63) >> 2) * cols + (m & 3) + jnp.where(m >= 64, cols - 4, 0))
    m, t = iota((128, 320), 0), iota((128, 320), 1)
    e = m & 31
    side = 4 * (4 * (m >> 4) + (m & 3) + 4)
    flank = jnp.where((m & 15) < 4, 128 + side + 3, jnp.where((m & 15) < 8, 224 + side, -1))
    above = jnp.where(e < 16, 48 + e, jnp.where(e == 16, 143, jnp.where(e == 17, 236, -1)))
    below = jnp.where(e < 16, 64 + e, jnp.where(e == 16, 211, jnp.where(e == 17, 304, -1)))
    pick_ring = hot(t == jnp.where(m < 64, flank, jnp.where(m < 96, above, below)))
    m, t = iota((32, 64), 0), iota((32, 64), 1)
    pick_side = hot(t == ((m & 15) >> 2) * 16 + (m & 3) + jnp.where(m < 16, 0, 4))
    t, k = iota((tokens, 64), 0), iota((tokens, 64), 1)
    place = hot(((k & 15) == (t >> 4)) & ((t & 15) == jnp.where(k < 32, 0, cols - 1)))
    head_of = iota((1, width), 1) >> 6
    head_hot = [hot(head_of == h) for h in range(heads)]

    def prepare(pick):
        for at in (0, 128):
            for b in range(WINDOW):
                spread[b, :, at : at + 128] = jnp.take_along_axis(
                    rows[b], pick[:, at : at + 128], axis=1
                )

    def chosen(row, offset):
        value = jnp.broadcast_to(spread[0, row : row + 1, :], offset.shape)
        for b in range(1, WINDOW):
            value = jnp.where(offset == b - REACH, spread[b, row : row + 1, :], value)
        return value

    def build_bias():
        for n in range(layers):
            for b in range(WINDOW):
                rows[b, heads * n : heads * (n + 1), 0 : 2 * WINDOW - 1] = table[n, b]
        x = iota((16, 256), 1)
        j = iota((16, 256), 0)
        own = x < 160
        on_left = x < 208
        y = jnp.where(on_left, x - 160, x - 208)
        p = jnp.where(own, x >> 4, (y >> 2) - 1)
        c = jnp.where(own, x & 15, jnp.where(on_left, (y & 3) - 4, (y & 3) + cols))
        col_ok = (c - j >= -REACH) & (c - j <= REACH)
        for i in range(GROUP):
            oks = []
            for group in (0, 1, 3):
                g = first_row + GROUP * group + i
                start = jnp.clip(g - REACH, 0, total_rows - WINDOW)
                r = first_row + GROUP * group - REACH + p
                oks.append(col_ok & (r >= start) & (r < start + WINDOW))
            prepare(jnp.clip(p[0:8] - i + REACH, 0, 2 * WINDOW - 2))
            for n in range(layers):
                for h in range(heads):
                    value = chosen(n * heads + h, c - j)
                    at = h * 80 + i * 16
                    for var in range(3):
                        bias[n, var, at : at + 16, :] = jnp.where(oks[var], value, -1000000000.0)
        e = iota((16, 256), 0)
        i, j = e & 3, jnp.where(e < 4, -1, cols)
        px, cx = p, c
        col_ok = (cx - j >= -REACH) & (cx - j <= REACH)
        oks = []
        for group in (0, 1, 3):
            g = first_row + GROUP * group + i
            start = jnp.clip(g - REACH, 0, total_rows - WINDOW)
            r = first_row + GROUP * group - REACH + px
            oks.append(col_ok & (r >= start) & (r < start + WINDOW))
        pick = jnp.clip(px - i + REACH, 0, 2 * WINDOW - 2)[0:8]
        for n in range(layers):
            for h in range(heads):
                value = jnp.zeros((8, 256), F32)
                for b in range(WINDOW):
                    source = jnp.broadcast_to(rows[b, n * heads + h : n * heads + h + 1, :], (8, 128))
                    got = [
                        jnp.take_along_axis(source, pick[:, at : at + 128], axis=1)
                        for at in (0, 128)
                    ]
                    value = jnp.where(
                        (cx - j)[0:8] == b - REACH, jnp.concatenate(got, axis=1), value
                    )
                at = h * 80 + 64
                for var in range(3):
                    bias[n, var, at : at + 8, :] = jnp.where(oks[var][0:8], value, -1000000000.0)
                    bias[n, var, at + 8 : at + 16, :] = jnp.zeros((8, 256), F32)
        x, e = iota((32, 256), 1), iota((32, 256), 0)
        j = jnp.where(e < 16, e, jnp.where(e == 16, -1, cols))
        own, on_left = x < 160, x < 208
        y = jnp.where(on_left, x - 160, x - 208)
        c = jnp.where(own, x & 15, jnp.where(on_left, (y & 3) - 4, (y & 3) + cols))
        for k, (here, first_own, first_near) in enumerate(((-1, -4, -4), (16, 10, 8))):
            away = jnp.where(own, first_own + (x >> 4), first_near + (y >> 2)) - here
            ok = (c - j >= -REACH) & (c - j <= REACH) & (away >= -REACH) & (away <= REACH)
            prepare(jnp.clip(away[0:8] + WINDOW - 1, 0, 2 * WINDOW - 2))
            for n in range(layers):
                for h in range(heads):
                    value = chosen(n * heads + h, c - j)
                    row_bias[n, k, h * 32 : h * 32 + 32, :] = jnp.where(ok, value, -1000000000.0)

    def attend(q, near, held, count):
        stacked = jnp.concatenate([q * head_hot[h] for h in range(heads)], axis=0)
        scores = lax.dot_general(
            stacked, near[:, :width], (((1,), (1,)), ((), ())), preferred_element_type=F32
        )
        scores = scores + held
        raised = jnp.exp(scores - jnp.max(scores, axis=-1, keepdims=True))
        weights = (raised * (1.0 / jnp.sum(raised, axis=-1, keepdims=True))).astype(BF16)
        mixed = dot(weights, near[:, width:])
        total = jnp.where(head_of == 0, mixed[0:count], 0.0)
        for h in range(1, heads):
            total = jnp.where(head_of == h, mixed[count * h : count * (h + 1)], total)
        return total.astype(BF16)

    def near_keys(own, side):
        parts = [kvb[own : own + 160, :], near_l[side : side + 48, :], near_r[side : side + 48, :]]
        return jnp.concatenate(parts, axis=0)

    scale = (width // heads) ** (-0.5)
    loads["x"].wait()
    for n in range(layers):
        current = xb[n, 64:320]
        edge[n] = dot(pick_kv, current).astype(BF16)
        if n == 0:
            count = 2 + jnp.where(has_up, 3, 0) + jnp.where(has_down, 3, 0)
            pl.semaphore_wait(barrier, count)
        send(n)
        if n == 0:
            loads["gains"].wait()
        gain = gains_ref[n, 0:1, :]
        wide = current.astype(F32)
        norm = normed(wide, gain)
        loads[n, 0].wait()
        kvb[64:320] = dot(norm, wqkv[n, :, width:]).astype(BF16)
        query = (dot(norm, wqkv[n, :, :width]).astype(BF16) * scale).astype(BF16)
        if n == 0:
            loads["table"].wait()
            build_bias()
            loads["conv"].wait()
        receive(n)
        around = jnp.concatenate([xb[n, 0:64], xb[n, 320:384], left[n], right[n]], axis=0)
        ring = dot(pick_ring, around)
        near = dot(normed(around.astype(F32), gain), wqkv[n, :, width:]).astype(BF16)
        kvb[0:64] = near[0:64]
        kvb[320:384] = near[64:128]
        near_l[...] = near[128:224]
        near_r[...] = near[224:320]
        ring_query = (dot(normed(ring, gain), wqkv[n, :, :width]).astype(BF16) * scale).astype(BF16)
        for group in range(4):
            at = 64 * group
            more = slice(16 * group, 16 * group + 16)
            q = jnp.concatenate([query[at : at + 64], ring_query[more]], axis=0)
            held = bias[n, (0, 1, 1, 2)[group]]
            got = attend(q, near_keys(at + 16, 16 * group), held, 80)
            attn[at : at + 64, :] = got[0:64]
            attn[256 + 16 * group : 272 + 16 * group, :] = got[64:80]

        @pl.when(has_up)
        def _():
            attn[320:352] = attend(ring_query[64:96], near_keys(0, 0), row_bias[n, 0], 32)

        @pl.when(has_down)
        def _():
            attn[352:384] = attend(ring_query[96:128], near_keys(224, 48), row_bias[n, 1], 32)

        loads[n, 1].wait()
        after = jnp.concatenate([wide, ring], axis=0) + dot(attn[...], wout[n])
        norm = normed(after, gains_ref[n, 1:2, :])
        after = after[0:tokens]
        loads[n, 2].wait()
        lift = dot(norm, wup[n]).astype(BF16)
        sides = dot(pick_side, lift[256:320])
        rims = lift[320:384].astype(F32)
        lpad[16:272] = lift[0:tokens].astype(F32)
        col = iota((tokens, 128), 0) & 15
        for ch in range(hid // 128):
            at = slice(128 * ch, 128 * ch + 128)
            above, here, below = lpad[0:256, at], lpad[16:272, at], lpad[32:288, at]

            def column(b):
                return (
                    conv_ref[0, b, n : n + 1, at] * above
                    + conv_ref[1, b, n : n + 1, at] * here
                    + conv_ref[2, b, n : n + 1, at] * below
                )

            pre[:, at] = (
                column(1)
                + jnp.where(col > 0, pltpu.roll(column(0), 1, 0), 0.0)
                + jnp.where(col < cols - 1, pltpu.roll(column(2), tokens - 1, 0), 0.0)
            )
        line = iota((16, hid), 0)

        def tap(a, b):
            return conv_ref[a, b, n : n + 1, :]

        def row_part(a, rim):
            middle = rim[0:16]
            back = jnp.where(line == 0, rim[16:17], pltpu.roll(middle, 1, 0))
            ahead = jnp.where(line == 15, rim[17:18], pltpu.roll(middle, 15, 0))
            return tap(a, 0) * back + tap(a, 1) * middle + tap(a, 2) * ahead

        def col_part(b, values):
            up = jnp.where(line == 0, 0.0, pltpu.roll(values, 1, 0))
            down = jnp.where(line == 15, 0.0, pltpu.roll(values, 15, 0))
            return tap(0, b) * up + tap(1, b) * values + tap(2, b) * down

        pieces = []
        for part in (col_part(0, sides[0:16]), col_part(2, sides[16:32])):
            high = part.astype(BF16)
            pieces += [high, (part - high.astype(F32)).astype(BF16)]
        pre[0:16] += row_part(0, rims[0:32])
        pre[240:256] += row_part(2, rims[32:64])
        whole = pre[...] + dot(place, jnp.concatenate(pieces, axis=0))
        hidden = jax.nn.gelu(whole, approximate=True).astype(BF16)
        loads[n, 3].wait()
        result = (after + dot(hidden, wdown[n])).astype(BF16)
        if n == layers - 1:
            out_ref[...] = result
        else:
            xb[n + 1, 64:320] = result

    for n in range(layers):
        for slot, step in enumerate(STEPS):
            when_to(step, lambda slot=slot: remote(n, slot).wait_send())


PITCH = 24
HALO = 8


def halved(a, b):
    half = a.shape[0] // 32 * 16
    return jnp.concatenate([dot(a[:half], b), dot(a[half:], b)], axis=0)


def wide_kernel(
    n_lat, n_lon, x_hbm, gains_hbm, table_hbm, conv_hbm, wqkv_hbm, wout_hbm, wup_hbm, wdown_hbm,
    out_ref, gains_ref, table, conv_ref, wqkv, wout, wup, wdown, raw, stage, edge, xf, kvb, qf, af, nf, lifted_0, lifted_1, lifted_2, over_0, over_1, over_2, hidden_0, hidden_1, hidden_2, rows,
    bias, place, result, in_sem, w_sem, send_sem, recv_sem, here_sem,
):
    layers = wqkv.shape[0]
    tokens, width = x_hbm.shape
    lifted, over_rows, hidden = (lifted_0, lifted_1, lifted_2), (over_0, over_1, over_2), (hidden_0, hidden_1, hidden_2)
    cols = 16
    heads = table.shape[2]
    hid = wup.shape[2]
    chunks = hid // 128
    lat = lax.axis_index("lat")
    lon = lax.axis_index("lon")
    odd = lax.rem(lon, 2)
    near = lon + 1 - 2 * odd
    far = lax.rem(lon - 1 + 2 * odd + n_lon, n_lon)

    loads = {}
    firsts = (("x", x_hbm, raw), ("gains", gains_hbm, gains_ref), ("table", table_hbm, table), ("conv", conv_hbm, conv_ref))
    for k, (name, src, dst) in enumerate(firsts):
        loads[name] = pltpu.make_async_copy(src, dst, in_sem.at[k])
        loads[name].start()
    for n in range(layers):
        pairs = ((wqkv_hbm, wqkv), (wout_hbm, wout), (wup_hbm, wup), (wdown_hbm, wdown))
        for k, (src, dst) in enumerate(pairs):
            loads[n, k] = pltpu.make_async_copy(src.at[n], dst.at[n], w_sem.at[n, k])
            loads[n, k].start()

    barrier = pltpu.get_barrier_semaphore()
    partners = ((lat, near), (1 - lat, near), (1 - lat, lon), (lat, far), (1 - lat, far))
    first, last = lon == 0, lon == n_lon - 1

    def greet(semaphore, row, col):
        pl.semaphore_signal(
            semaphore, inc=1, device_id={"lat": row, "lon": col}, device_id_type=pl.DeviceIdType.MESH
        )

    for row, col in partners[:3]:
        greet(barrier, row, col)

    eager = first | ((odd == 1) & jnp.logical_not(last))

    @pl.when(eager)
    def _():
        for row, col in partners[3:]:
            greet(barrier, row, col)

    def greet_back():
        for row, col in partners[3:]:
            greet(here_sem, row, col)

    @pl.when(last)
    def _():
        pl.semaphore_wait(barrier, len(partners))
        greet_back()

    remotes = []
    pieces = (
        (edge.at[pl.ds(0, 128)], stage.at[pl.ds(0, 128)]),
        (edge.at[pl.ds(128, 64)], stage.at[pl.ds(128, 64)]),
        (edge.at[pl.ds(384, 128)], stage.at[pl.ds(192, 128)]),
        (edge.at[pl.ds(192, 128)], stage.at[pl.ds(320, 128)]),
        (edge.at[pl.ds(320, 64)], stage.at[pl.ds(448, 64)]),
    )
    for slot, (src, dst) in enumerate(pieces):
        remotes.append(
            pltpu.make_async_remote_copy(
                src_ref=src,
                dst_ref=dst,
                send_sem=send_sem.at[slot],
                recv_sem=recv_sem.at[slot],
                device_id={"lat": partners[slot][0], "lon": partners[slot][1]},
                device_id_type=pl.DeviceIdType.MESH,
            )
        )

    def flip(value, by):
        return value + by * (cols - 1 - 2 * value)

    def choose(count, shift, column):
        m, t = iota((count, 1), 0), iota((count, tokens), 1)
        i = m & ((1 << shift) - 1)
        v = i if shift == 4 else cols - 1 - i
        return hot(t == flip(v, lat) * cols + flip(column(m >> shift), odd))

    picks = (
        choose(128, 4, lambda k: 15 - k),
        choose(64, 3, lambda k: 15 - k),
        choose(128, 4, lambda k: 7 - k),
        choose(64, 3, lambda k: 7 - k),
        choose(128, 3, lambda k: k),
    )
    picks = jnp.concatenate(picks, axis=0)
    pick_own = choose(256, 4, lambda k: k)
    loads["x"].wait()
    edge[...] = halved(picks, raw[...]).astype(BF16)
    @pl.when(jnp.logical_not(last))
    def _():
        pl.semaphore_wait(barrier, len(partners) - jnp.where(eager, 2, 0))

    @pl.when(last)
    def _():
        for remote in remotes[3:]:
            remote.start()

    for remote in remotes[:3]:
        remote.start()

    @pl.when(jnp.logical_not(eager | last))
    def _():
        greet_back()

    def answer():
        @pl.when(first)
        def _():
            pl.semaphore_wait(here_sem, 2)
            for remote in remotes[3:]:
                remote.start()

    kvb[0, 768:832] = jnp.zeros((64, 2 * width), BF16)
    kvb[1, 672:832] = jnp.zeros((160, 2 * width), BF16)

    m, t = iota((256, 256), 0), iota((256, 256), 1)
    u, v = flip(m & 15, odd), flip(m >> 4, lat)
    for k in range(2):
        place[k] = hot(t == (u - 8 * k) * PITCH + v)

    loads["table"].wait()
    for n in range(layers):
        for b in range(WINDOW):
            rows[heads * n : heads * (n + 1), 16 * b : 16 * b + 2 * WINDOW - 1] = table[n, b]
    lane, v = iota((PITCH, 256), 1), iota((PITCH, 256), 0)
    start = jnp.maximum(v - REACH, 0)
    for n in range(layers):
        if n == 0:
            double = (lane * 1366) >> 16
            rest = lane - 2 * PITCH * double
            key_u = 2 * double + jnp.where(rest < 32, rest >> 4, (rest - 32) >> 3)
            key_v = jnp.where(rest < 32, rest & 15, 16 + (rest & 7))
        else:
            key_u = (lane * 2731) >> 16
            key_v = lane - PITCH * key_u
        row_ok = (key_v >= start) & (key_v < start + WINDOW)
        away = jnp.clip((key_v - v) * (1 - 2 * lat) + WINDOW - 1, 0, 2 * WINDOW - 2)
        for q in range(GROUP):
            off = key_u - REACH - q
            ok = row_ok & (off >= -REACH) & (off <= REACH)
            at = jnp.clip(off * (1 - 2 * odd) + REACH, 0, WINDOW - 1) * 16 + away
            for h in range(heads):
                line = jnp.broadcast_to(rows[n * heads + h : n * heads + h + 1, :], (PITCH, 128))
                got = [jnp.take_along_axis(line, at[:, s : s + 128], axis=1) for s in (0, 128)]
                value = jnp.where(ok, jnp.concatenate(got, axis=1) * 1.4426950408889634, -1000000000.0)
                bias[n, h, PITCH * q : PITCH * (q + 1), :] = value

    head_of = iota((1, width), 1) >> 6
    head_hot = [hot(head_of == h) for h in range(heads)]
    low_half = (iota((1, width), 1) & 127) < 64
    log2e = 1.4426950408889634
    scale = (width // heads) ** (-0.5) * log2e

    def multiply(n, wide):
        norm = normed(wide, gains_ref[n, 0:1, :])
        product = halved if wide.shape[0] > 256 else dot
        return product(norm, wqkv[n, :, width:]).astype(BF16), product(norm, wqkv[n, :, :width])

    def project(n, first, count, q_from, q_count):
        kv, query = multiply(n, xf[n, PITCH * first : PITCH * (first + count), :])
        kvb[n, PITCH * first : PITCH * (first + count), :] = kv
        at = PITCH * (q_from + 3 - first)
        qf[PITCH * q_from : PITCH * (q_from + q_count), :] = query[at : at + PITCH * q_count]

    def spread(wide, kv, query, at, shift, first, count):
        high = 1 << shift
        low = 0 if shift == 4 else 16
        for k in range(count):
            here = slice(at + high * k, at + high * (k + 1))
            to = PITCH * (first + k) + low
            xf[0, to : to + high, :] = wide[here]
            j = first + k - 3
            if 0 <= j < 26:
                qf[PITCH * j + low : PITCH * j + low + high, :] = query[here]
        for p in range(count // 2):
            to = PITCH * (first + 2 * p) + 2 * low
            kvb[0, to : to + 2 * high, :] = kv[at + 2 * high * p : at + 2 * high * (p + 1)]

    def attend(n, tiles, finish):
        def score(j, w):
            count = PITCH * w
            q = (qf[PITCH * j : PITCH * (j + w), :] * scale).astype(BF16)
            keys = kvb[n, PITCH * j : PITCH * j + 256, 0:width]
            stacked = jnp.concatenate([q * head_hot[h] for h in range(heads)], axis=0)
            return lax.dot_general(stacked, keys, (((1,), (1,)), ((), ())), preferred_element_type=F32)

        def soften(scores, w):
            count = PITCH * w
            weights = []
            for h in range(heads):
                held = scores[count * h : count * (h + 1)] + bias[n, h, 0:count, :]
                weights.append(jnp.exp2((held - jnp.max(held, axis=-1, keepdims=True)).astype(BF16)))
            return weights

        def gather_values(weights, j, w):
            count = PITCH * w
            totals = []
            for pair in range(heads // 2):
                at = width + 128 * pair
                own = kvb[n, PITCH * j : PITCH * j + 256, at : at + 128]
                values = jnp.concatenate([own, jnp.ones(own.shape, BF16)], axis=1)
                both = jnp.concatenate(weights[2 * pair : 2 * pair + 2], axis=0)
                mixed = dot(both, values)
                mixed = jnp.where(low_half, mixed[0:count], mixed[count : 2 * count])
                total = mixed[:, 0:128] * (1.0 / mixed[:, 128:256])
                totals.append(total.astype(BF16))
            return jnp.concatenate(totals, axis=1)

        ahead = [score(*tile) for tile in tiles[:2]]
        attended = []
        for k, (j, w) in enumerate(tiles):
            weights = soften(ahead[k], w)
            if k + 2 < len(tiles):
                ahead.append(score(*tiles[k + 2]))
            attended.append(gather_values(weights, j, w))
            if k > 0:
                finish(*tiles[k - 1], attended[k - 1])
        finish(*tiles[-1], attended[-1])

    def tap(n, a, b, ch):
        return conv_ref[a + lat * (2 - 2 * a), b + odd * (2 - 2 * b), n : n + 1, 128 * ch : 128 * (ch + 1)]

    def feed(n, tiles, l0, lifts, o0, outs):
        def finish(j, w, attended):
            size = PITCH * w
            here = slice(PITCH * j, PITCH * j + size)
            after = xf[n, PITCH * (j + 3) : PITCH * (j + 3) + size, :] + dot(attended, wout[n])
            af[here] = after
            scaled = lax.rsqrt(jnp.mean(after * after, axis=-1, keepdims=True) + 1e-06)
            line = iota((size, 1), 0)
            line = line - PITCH * ((line * 2731) >> 16)
            scaled = jnp.where(line == PITCH - 1, 0.0, scaled)
            norm = after * scaled * gains_ref[n, 1:2, :]
            for k in range(2):
                nf[k, 8 + PITCH * j : 8 + PITCH * j + size, :] = norm[:, 128 * k : 128 * (k + 1)]

        attend(n, tiles, finish)
        high = PITCH if n == 0 else 16
        moved = []
        for a in range(3):
            halves = []
            for k in range(2):
                if n == 0:
                    at = 8 + PITCH * l0 + a - 1
                    halves.append(nf[k, at : at + PITCH * lifts, :].astype(BF16))
                else:
                    spots = [8 + PITCH * j + a - 1 for j in range(l0, l0 + lifts)]
                    halves.append(jnp.concatenate([nf[k, at : at + 16, :] for at in spots], axis=0).astype(BF16))
            moved.append(jnp.concatenate(halves, axis=1))
        tall = moved[0].shape[0]
        moved = jnp.concatenate(moved, axis=0)

        def lift_up(double):
            product = dot(moved, wup[n, :, 256 * double : 256 * (double + 1)])
            for a in range(3):
                both = product[tall * a : tall * (a + 1)]
                for ch in range(2):
                    lift = both[:, 128 * ch : 128 * (ch + 1)]
                    if n == 0:
                        lift = lift.reshape(lifts, PITCH, 128)
                        base = lift[:, 0:16].reshape(16 * lifts, 128).astype(BF16)
                        over = lift[:, 16:PITCH]
                        pairs = jnp.concatenate([over[:-1], over[1:]], axis=1).reshape(-1, 128)
                        over_rows[double][a, ch, 16 * l0 : 16 * (l0 + lifts - 1), :] = pairs.astype(BF16)
                    else:
                        base = lift.astype(BF16)
                    lifted[double][a, ch, 16 * l0 : 16 * (l0 + lifts), :] = base

        def convolve(ch):
            taps = [[(0.5 * tap(n, a, b, ch)).astype(BF16) for b in range(3)] for a in range(3)]

            def convolved(source, j, wide):
                total = None
                for a in range(3):
                    for b in range(3):
                        at = 16 * (j + b - 1)
                        term = taps[a][b] * source[a, ch % 2, at : at + 16 * wide, :]
                        total = term if total is None else total + term
                inner = total * (1.5957691216057308 + 0.285419265090401 * (total * total))
                return total + total * jnp.tanh(inner)

            for part in range(0, outs, 2):
                main = convolved(lifted[ch // 2], o0 + part, 2)
                if n == 0:
                    rest = convolved(over_rows[ch // 2], o0 + part, 1).astype(F32)
                    main = main.astype(F32)
                    main = jnp.concatenate([main[0:16], rest[0:8], main[16:32], rest[8:16]], axis=0).astype(BF16)
                side = slice(128 * (ch % 2), 128 * (ch % 2 + 1))
                hidden[ch // 2][high * part : high * (part + 2), side] = main

        product = halved if high * outs > 256 else dot
        down = None
        lift_up(0)
        for double in range(chunks // 2):
            if double + 1 < chunks // 2:
                lift_up(double + 1)
            convolve(2 * double)
            convolve(2 * double + 1)
            units = slice(256 * double, 256 * (double + 1))
            part = product(hidden[double][0 : high * outs], wdown[n, units, :])
            down = part if down is None else down + part
        if n == 0:
            xf[1, PITCH * (o0 + 3) : PITCH * (o0 + 3 + outs), :] = af[PITCH * o0 : PITCH * (o0 + outs)] + down
        else:
            for k in range(outs):
                at = PITCH * (o0 + k)
                out = af[at : at + 16] + down[16 * k : 16 * (k + 1)]
                af[at : at + 16] = out

    loads["gains"].wait()
    loads[0, 0].wait()
    wide = dot(pick_own, raw[...])
    kv, query = multiply(0, wide)
    spread(wide, kv, query, 0, 4, 8, 16)
    remotes[2].wait_recv()
    wide = stage[192:320].astype(F32)
    kv, query = multiply(0, wide)
    spread(wide, kv, query, 0, 3, 8, 16)
    loads["conv"].wait()
    for k in range(1, 4):
        loads[0, k].wait()
    feed(0, ((8, 4), (12, 4)), 8, 8, 9, 6)
    for k in (0, 1):
        remotes[k].wait_recv()

    @pl.when(eager & jnp.logical_not(first))
    def _():
        pl.semaphore_wait(here_sem, 2)

    @pl.when(jnp.logical_not(first | last))
    def _():
        for remote in remotes[3:]:
            remote.start()

    wide = stage[0:192].astype(F32)
    kv, query = multiply(0, wide)
    spread(wide, kv, query, 0, 4, 24, 8)
    spread(wide, kv, query, 128, 3, 24, 8)
    feed(0, ((16, 4), (20, 4), (24, 2)), 15, 11, 15, 10)
    for k in range(4):
        loads[1, k].wait()
    project(1, 12, 16, 9, 13)
    answer()
    feed(1, ((12, 4), (16, 4), (20, 2)), 12, 10, 13, 8)
    result[...] = dot(place[1, :, 0:192], af[PITCH * 13 : PITCH * 21].astype(BF16))
    for k in (3, 4):
        remotes[k].wait_recv()
    wide = stage[320:512].astype(F32)
    kv, query = multiply(0, wide)
    spread(wide, kv, query, 0, 4, 0, 8)
    spread(wide, kv, query, 128, 3, 0, 8)
    feed(0, ((0, 4), (4, 4)), 0, 9, 1, 8)
    project(1, 4, 8, 4, 5)
    feed(1, ((4, 4), (8, 4)), 4, 8, 5, 8)
    out_ref[...] = (result[...] + dot(place[0, :, 0:192], af[PITCH * 5 : PITCH * 13].astype(BF16))).astype(BF16)
    for remote in remotes:
        remote.wait_send()


def wide_call(n_lat, n_lon, stream, gains, table, conv, w_qkv, w_out, w_up, w_down):
    layers = w_qkv.shape[0]
    width = stream.shape[1]
    hid = w_up.shape[2]
    vmem = pl.BlockSpec(memory_space=pltpu.VMEM)
    anywhere = pl.BlockSpec(memory_space=pltpu.HBM)
    heads = table.shape[2]
    return pl.pallas_call(
        functools.partial(wide_kernel, n_lat, n_lon),
        out_shape=pltpu.VMEM(stream.shape, BF16),
        in_specs=[anywhere] * 8,
        out_specs=vmem,
        scratch_shapes=[
            pltpu.VMEM(gains.shape, F32),
            pltpu.VMEM(table.shape, F32),
            pltpu.VMEM(conv.shape, F32),
            pltpu.VMEM(w_qkv.shape, BF16),
            pltpu.VMEM(w_out.shape, BF16),
            pltpu.VMEM(w_up.shape, BF16),
            pltpu.VMEM(w_down.shape, BF16),
            pltpu.VMEM((256, width), BF16),
            pltpu.VMEM((512, width), BF16),
            pltpu.VMEM((512, width), BF16),
            pltpu.VMEM((layers, 32 * PITCH, width), F32),
            pltpu.VMEM((layers, 832, 2 * width), BF16),
            pltpu.VMEM((26 * PITCH, width), F32),
            pltpu.VMEM((26 * PITCH, width), F32),
            pltpu.VMEM((2, 26 * PITCH + 16, 128), F32),
            *[pltpu.VMEM((3, 2, 26 * 16, 128), BF16)] * (hid // 128),
            *[pltpu.VMEM((16 * PITCH, 256), BF16)] * (hid // 256),
            pltpu.VMEM((layers * heads, 128), F32),
            pltpu.VMEM((layers, heads, GROUP * PITCH, 256), F32),
            pltpu.VMEM((2, 256, 256), BF16),
            pltpu.VMEM((256, width), F32),
            pltpu.SemaphoreType.DMA((4,)),
            pltpu.SemaphoreType.DMA((layers, 4)),
            pltpu.SemaphoreType.DMA((5,)),
            pltpu.SemaphoreType.DMA((5,)),
            pltpu.SemaphoreType.REGULAR,
        ],
        compiler_params=pltpu.CompilerParams(
            collective_id=0, has_side_effects=True, vmem_limit_bytes=58 * 1024 * 1024
        ),
    )(stream, gains, table, conv, w_qkv, w_out, w_up, w_down)


def on_device(n_lat, n_lon, stream, gains, w_qkv, table, w_out, w_up, conv, w_down):
    rows, cols, width = stream.shape
    layers, heads = table.shape[:2]
    table = table.transpose(0, 3, 1, 2)
    conv = conv.transpose(1, 2, 0, 3)
    hid = w_up.shape[2]
    vmem = pl.BlockSpec(memory_space=pltpu.VMEM)
    anywhere = pl.BlockSpec(memory_space=pltpu.HBM)
    if n_lat == 2 and n_lon % 2 == 0 and n_lon > 2:
        result = wide_call(
            n_lat, n_lon, stream.reshape(rows * cols, width), gains, table, conv, w_qkv, w_out, w_up, w_down
        )
        return result.reshape(rows, cols, width)
    result = pl.pallas_call(
        functools.partial(kernel, n_lat, n_lon),
        out_shape=pltpu.VMEM((rows * cols, width), BF16),
        in_specs=[anywhere] * 8,
        out_specs=vmem,
        scratch_shapes=[
            pltpu.VMEM(gains.shape, F32),
            pltpu.VMEM(table.shape, F32),
            pltpu.VMEM(conv.shape, F32),
            pltpu.VMEM(w_qkv.shape, BF16),
            pltpu.VMEM(w_out.shape, BF16),
            pltpu.VMEM(w_up.shape, BF16),
            pltpu.VMEM(w_down.shape, BF16),
            pltpu.VMEM((384, 2 * width), BF16),
            pltpu.VMEM((96, 2 * width), BF16),
            pltpu.VMEM((96, 2 * width), BF16),
            pltpu.VMEM((layers, 384, width), BF16),
            pltpu.VMEM((layers, 96, width), BF16),
            pltpu.VMEM((layers, 96, width), BF16),
            pltpu.VMEM((layers, 128, width), BF16),
            pltpu.VMEM((288, hid), F32),
            pltpu.VMEM((256, hid), F32),
            pltpu.VMEM((WINDOW, layers * heads, 128), F32),
            pltpu.VMEM((WINDOW, layers * heads, 256), F32),
            pltpu.VMEM((layers, 3, 320, 256), F32),
            pltpu.VMEM((layers, 2, 128, 256), F32),
            pltpu.VMEM((384, width), BF16),
            pltpu.SemaphoreType.DMA((4,)),
            pltpu.SemaphoreType.DMA((layers, 4)),
            pltpu.SemaphoreType.DMA((layers, 8)),
            pltpu.SemaphoreType.DMA((layers, 8)),
        ],
        compiler_params=pltpu.CompilerParams(
            collective_id=0, has_side_effects=True, vmem_limit_bytes=58 * 1024 * 1024
        ),
    )(
        stream.reshape(rows * cols, width),
        gains,
        table,
        conv,
        w_qkv,
        w_out,
        w_up,
        w_down,
    )
    return result.reshape(rows, cols, width)


def solution(mesh):
    sizes = dict(mesh.shape)
    in_specs = (P("lat", "lon", None), P(), P(), P(), P(), P(), P(), P())
    return jax.shard_map(
        functools.partial(on_device, sizes["lat"], sizes["lon"]),
        mesh=mesh,
        in_specs=in_specs,
        out_specs=P("lat", "lon", None),
        check_vma=False,
    )
```

```python
import functools

import jax
import jax.numpy as jnp
from jax import lax
from jax.experimental import pallas as pl
from jax.experimental.pallas import tpu as pltpu
from jax.sharding import PartitionSpec as P

WINDOW = 7
REACH = 3
GROUP = 4
F32 = jnp.float32
BF16 = jnp.bfloat16

LEFT, RIGHT, TOP, BOTTOM, TOP_L, TOP_R, BOT_L, BOT_R = range(8)
STEPS = ((0, 1), (0, -1), (1, 0), (-1, 0), (1, 1), (1, -1), (-1, 1), (-1, -1))


def iota(shape, dim):
    return lax.broadcasted_iota(jnp.int32, shape, dim)


def hot(cond):
    return jnp.where(cond, 1.0, 0.0).astype(BF16)


def dot(a, b):
    return jnp.dot(a, b, preferred_element_type=F32)


def normed(wide, gain):
    scale = lax.rsqrt(jnp.mean(wide * wide, axis=-1, keepdims=True) + 1e-06)
    return (wide * scale * gain).astype(BF16)


def kernel(
    n_lat, n_lon, x_hbm, gains_hbm, table_hbm, conv_hbm, wqkv_hbm, wout_hbm, wup_hbm, wdown_hbm,
    out_ref, gains_ref, table, conv_ref, wqkv, wout, wup, wdown, kvb, near_l, near_r, xb, left, right, edge, lpad, pre, rows, spread,
    bias, row_bias, attn, in_sem, w_sem, send_sem, recv_sem,
):
    layers = wqkv.shape[0]
    tokens, width = x_hbm.shape
    cols = 16
    heads = table.shape[2]
    hid = wup.shape[2]
    lat = lax.axis_index("lat")
    lon = lax.axis_index("lon")
    has_up = lat > 0
    has_down = lat < n_lat - 1
    total_rows = n_lat * (tokens // cols)
    first_row = lat * (tokens // cols)

    loads = {}
    firsts = (("x", x_hbm, xb.at[0, pl.ds(64, 256)]), ("gains", gains_hbm, gains_ref), ("table", table_hbm, table), ("conv", conv_hbm, conv_ref))
    for k, (name, src, dst) in enumerate(firsts):
        loads[name] = pltpu.make_async_copy(src, dst, in_sem.at[k])
    loads["x"].start()
    loads["gains"].start()
    for n in range(layers):
        pairs = ((wqkv_hbm, wqkv), (wout_hbm, wout), (wup_hbm, wup), (wdown_hbm, wdown))
        for k, (src, dst) in enumerate(pairs):
            loads[n, k] = pltpu.make_async_copy(src.at[n], dst.at[n], w_sem.at[n, k])
            loads[n, k].start()
            if n == 0 and k == 0:
                loads["table"].start()
                loads["conv"].start()

    def target(step):
        return {"lat": lat + step[0], "lon": lax.rem(lon + step[1] + n_lon, n_lon)}

    def when_to(step, go):
        if step[0] == 0:
            go()
        else:
            pl.when(has_down if step[0] > 0 else has_up)(go)

    def when_from(step, go):
        when_to((-step[0], -step[1]), go)

    barrier = pltpu.get_barrier_semaphore()
    for step in STEPS:
        when_to(
            step,
            lambda step=step: pl.semaphore_signal(
                barrier, inc=1, device_id=target(step), device_id_type=pl.DeviceIdType.MESH
            ),
        )

    def remote(n, slot):
        own, lo, ro, ed = xb.at[n], left.at[n], right.at[n], edge.at[n]
        src, dst = (
            (ed.at[pl.ds(64, 64)], lo.at[pl.ds(16, 64)]),
            (ed.at[pl.ds(0, 64)], ro.at[pl.ds(16, 64)]),
            (own.at[pl.ds(256, 64)], own.at[pl.ds(0, 64)]),
            (own.at[pl.ds(64, 64)], own.at[pl.ds(320, 64)]),
            (ed.at[pl.ds(112, 16)], lo.at[pl.ds(0, 16)]),
            (ed.at[pl.ds(48, 16)], ro.at[pl.ds(0, 16)]),
            (ed.at[pl.ds(64, 16)], lo.at[pl.ds(80, 16)]),
            (ed.at[pl.ds(0, 16)], ro.at[pl.ds(80, 16)]),
        )[slot]
        return pltpu.make_async_remote_copy(
            src_ref=src,
            dst_ref=dst,
            send_sem=send_sem.at[n, slot],
            recv_sem=recv_sem.at[n, slot],
            device_id=target(STEPS[slot]),
            device_id_type=pl.DeviceIdType.MESH,
        )

    def send(n):
        for slot, step in enumerate(STEPS):
            when_to(step, lambda slot=slot: remote(n, slot).start())

    def receive(n):
        for slot, step in enumerate(STEPS):
            when_from(step, lambda slot=slot: remote(n, slot).wait_recv())

    @pl.when(jnp.logical_not(has_up))
    def _():
        for n in range(layers):
            xb[n, 0:64] = jnp.zeros((64, width), BF16)
            left[n, 0:16] = jnp.zeros((16, width), BF16)
            right[n, 0:16] = jnp.zeros((16, width), BF16)
        attn[320:352] = jnp.zeros((32, width), BF16)

    @pl.when(jnp.logical_not(has_down))
    def _():
        for n in range(layers):
            xb[n, 320:384] = jnp.zeros((64, width), BF16)
            left[n, 80:96] = jnp.zeros((16, width), BF16)
            right[n, 80:96] = jnp.zeros((16, width), BF16)
        attn[352:384] = jnp.zeros((32, width), BF16)

    lpad[0:16] = jnp.zeros((16, hid), F32)
    lpad[272:288] = jnp.zeros((16, hid), F32)

    m, t = iota((128, tokens), 0), iota((128, tokens), 1)
    pick_kv = hot(t == ((m & 63) >> 2) * cols + (m & 3) + jnp.where(m >= 64, cols - 4, 0))
    m, t = iota((128, 320), 0), iota((128, 320), 1)
    e = m & 31
    side = 4 * (4 * (m >> 4) + (m & 3) + 4)
    flank = jnp.where((m & 15) < 4, 128 + side + 3, jnp.where((m & 15) < 8, 224 + side, -1))
    above = jnp.where(e < 16, 48 + e, jnp.where(e == 16, 143, jnp.where(e == 17, 236, -1)))
    below = jnp.where(e < 16, 64 + e, jnp.where(e == 16, 211, jnp.where(e == 17, 304, -1)))
    pick_ring = hot(t == jnp.where(m < 64, flank, jnp.where(m < 96, above, below)))
    m, t = iota((32, 64), 0), iota((32, 64), 1)
    pick_side = hot(t == ((m & 15) >> 2) * 16 + (m & 3) + jnp.where(m < 16, 0, 4))
    t, k = iota((tokens, 64), 0), iota((tokens, 64), 1)
    place = hot(((k & 15) == (t >> 4)) & ((t & 15) == jnp.where(k < 32, 0, cols - 1)))
    head_of = iota((1, width), 1) >> 6
    head_hot = [hot(head_of == h) for h in range(heads)]

    def prepare(pick):
        for at in (0, 128):
            for b in range(WINDOW):
                spread[b, :, at : at + 128] = jnp.take_along_axis(
                    rows[b], pick[:, at : at + 128], axis=1
                )

    def chosen(row, offset):
        value = jnp.broadcast_to(spread[0, row : row + 1, :], offset.shape)
        for b in range(1, WINDOW):
            value = jnp.where(offset == b - REACH, spread[b, row : row + 1, :], value)
        return value

    def build_bias():
        for n in range(layers):
            for b in range(WINDOW):
                rows[b, heads * n : heads * (n + 1), 0 : 2 * WINDOW - 1] = table[n, b]
        x = iota((16, 256), 1)
        j = iota((16, 256), 0)
        own = x < 160
        on_left = x < 208
        y = jnp.where(on_left, x - 160, x - 208)
        p = jnp.where(own, x >> 4, (y >> 2) - 1)
        c = jnp.where(own, x & 15, jnp.where(on_left, (y & 3) - 4, (y & 3) + cols))
        col_ok = (c - j >= -REACH) & (c - j <= REACH)
        for i in range(GROUP):
            oks = []
            for group in (0, 1, 3):
                g = first_row + GROUP * group + i
                start = jnp.clip(g - REACH, 0, total_rows - WINDOW)
                r = first_row + GROUP * group - REACH + p
                oks.append(col_ok & (r >= start) & (r < start + WINDOW))
            prepare(jnp.clip(p[0:8] - i + REACH, 0, 2 * WINDOW - 2))
            for n in range(layers):
                for h in range(heads):
                    value = chosen(n * heads + h, c - j)
                    at = h * 80 + i * 16
                    for var in range(3):
                        bias[n, var, at : at + 16, :] = jnp.where(oks[var], value, -1000000000.0)
        e = iota((16, 256), 0)
        i, j = e & 3, jnp.where(e < 4, -1, cols)
        px, cx = p, c
        col_ok = (cx - j >= -REACH) & (cx - j <= REACH)
        oks = []
        for group in (0, 1, 3):
            g = first_row + GROUP * group + i
            start = jnp.clip(g - REACH, 0, total_rows - WINDOW)
            r = first_row + GROUP * group - REACH + px
            oks.append(col_ok & (r >= start) & (r < start + WINDOW))
        pick = jnp.clip(px - i + REACH, 0, 2 * WINDOW - 2)[0:8]
        for n in range(layers):
            for h in range(heads):
                value = jnp.zeros((8, 256), F32)
                for b in range(WINDOW):
                    source = jnp.broadcast_to(rows[b, n * heads + h : n * heads + h + 1, :], (8, 128))
                    got = [
                        jnp.take_along_axis(source, pick[:, at : at + 128], axis=1)
                        for at in (0, 128)
                    ]
                    value = jnp.where(
                        (cx - j)[0:8] == b - REACH, jnp.concatenate(got, axis=1), value
                    )
                at = h * 80 + 64
                for var in range(3):
                    bias[n, var, at : at + 8, :] = jnp.where(oks[var][0:8], value, -1000000000.0)
                    bias[n, var, at + 8 : at + 16, :] = jnp.zeros((8, 256), F32)
        x, e = iota((32, 256), 1), iota((32, 256), 0)
        j = jnp.where(e < 16, e, jnp.where(e == 16, -1, cols))
        own, on_left = x < 160, x < 208
        y = jnp.where(on_left, x - 160, x - 208)
        c = jnp.where(own, x & 15, jnp.where(on_left, (y & 3) - 4, (y & 3) + cols))
        for k, (here, first_own, first_near) in enumerate(((-1, -4, -4), (16, 10, 8))):
            away = jnp.where(own, first_own + (x >> 4), first_near + (y >> 2)) - here
            ok = (c - j >= -REACH) & (c - j <= REACH) & (away >= -REACH) & (away <= REACH)
            prepare(jnp.clip(away[0:8] + WINDOW - 1, 0, 2 * WINDOW - 2))
            for n in range(layers):
                for h in range(heads):
                    value = chosen(n * heads + h, c - j)
                    row_bias[n, k, h * 32 : h * 32 + 32, :] = jnp.where(ok, value, -1000000000.0)

    def attend(q, near, held, count):
        stacked = jnp.concatenate([q * head_hot[h] for h in range(heads)], axis=0)
        scores = lax.dot_general(
            stacked, near[:, :width], (((1,), (1,)), ((), ())), preferred_element_type=F32
        )
        scores = scores + held
        raised = jnp.exp(scores - jnp.max(scores, axis=-1, keepdims=True))
        weights = (raised * (1.0 / jnp.sum(raised, axis=-1, keepdims=True))).astype(BF16)
        mixed = dot(weights, near[:, width:])
        total = jnp.where(head_of == 0, mixed[0:count], 0.0)
        for h in range(1, heads):
            total = jnp.where(head_of == h, mixed[count * h : count * (h + 1)], total)
        return total.astype(BF16)

    def near_keys(own, side):
        parts = [kvb[own : own + 160, :], near_l[side : side + 48, :], near_r[side : side + 48, :]]
        return jnp.concatenate(parts, axis=0)

    scale = (width // heads) ** (-0.5)
    loads["x"].wait()
    for n in range(layers):
        current = xb[n, 64:320]
        edge[n] = dot(pick_kv, current).astype(BF16)
        if n == 0:
            count = 2 + jnp.where(has_up, 3, 0) + jnp.where(has_down, 3, 0)
            pl.semaphore_wait(barrier, count)
        send(n)
        if n == 0:
            loads["gains"].wait()
        gain = gains_ref[n, 0:1, :]
        wide = current.astype(F32)
        norm = normed(wide, gain)
        loads[n, 0].wait()
        kvb[64:320] = dot(norm, wqkv[n, :, width:]).astype(BF16)
        query = (dot(norm, wqkv[n, :, :width]).astype(BF16) * scale).astype(BF16)
        if n == 0:
            loads["table"].wait()
            build_bias()
            loads["conv"].wait()
        receive(n)
        around = jnp.concatenate([xb[n, 0:64], xb[n, 320:384], left[n], right[n]], axis=0)
        ring = dot(pick_ring, around)
        near = dot(normed(around.astype(F32), gain), wqkv[n, :, width:]).astype(BF16)
        kvb[0:64] = near[0:64]
        kvb[320:384] = near[64:128]
        near_l[...] = near[128:224]
        near_r[...] = near[224:320]
        ring_query = (dot(normed(ring, gain), wqkv[n, :, :width]).astype(BF16) * scale).astype(BF16)
        for group in range(4):
            at = 64 * group
            more = slice(16 * group, 16 * group + 16)
            q = jnp.concatenate([query[at : at + 64], ring_query[more]], axis=0)
            held = bias[n, (0, 1, 1, 2)[group]]
            got = attend(q, near_keys(at + 16, 16 * group), held, 80)
            attn[at : at + 64, :] = got[0:64]
            attn[256 + 16 * group : 272 + 16 * group, :] = got[64:80]

        @pl.when(has_up)
        def _():
            attn[320:352] = attend(ring_query[64:96], near_keys(0, 0), row_bias[n, 0], 32)

        @pl.when(has_down)
        def _():
            attn[352:384] = attend(ring_query[96:128], near_keys(224, 48), row_bias[n, 1], 32)

        loads[n, 1].wait()
        after = jnp.concatenate([wide, ring], axis=0) + dot(attn[...], wout[n])
        norm = normed(after, gains_ref[n, 1:2, :])
        after = after[0:tokens]
        loads[n, 2].wait()
        lift = dot(norm, wup[n]).astype(BF16)
        sides = dot(pick_side, lift[256:320])
        rims = lift[320:384].astype(F32)
        lpad[16:272] = lift[0:tokens].astype(F32)
        col = iota((tokens, 128), 0) & 15
        for ch in range(hid // 128):
            at = slice(128 * ch, 128 * ch + 128)
            above, here, below = lpad[0:256, at], lpad[16:272, at], lpad[32:288, at]

            def column(b):
                return (
                    conv_ref[0, b, n : n + 1, at] * above
                    + conv_ref[1, b, n : n + 1, at] * here
                    + conv_ref[2, b, n : n + 1, at] * below
                )

            pre[:, at] = (
                column(1)
                + jnp.where(col > 0, pltpu.roll(column(0), 1, 0), 0.0)
                + jnp.where(col < cols - 1, pltpu.roll(column(2), tokens - 1, 0), 0.0)
            )
        line = iota((16, hid), 0)

        def tap(a, b):
            return conv_ref[a, b, n : n + 1, :]

        def row_part(a, rim):
            middle = rim[0:16]
            back = jnp.where(line == 0, rim[16:17], pltpu.roll(middle, 1, 0))
            ahead = jnp.where(line == 15, rim[17:18], pltpu.roll(middle, 15, 0))
            return tap(a, 0) * back + tap(a, 1) * middle + tap(a, 2) * ahead

        def col_part(b, values):
            up = jnp.where(line == 0, 0.0, pltpu.roll(values, 1, 0))
            down = jnp.where(line == 15, 0.0, pltpu.roll(values, 15, 0))
            return tap(0, b) * up + tap(1, b) * values + tap(2, b) * down

        pieces = []
        for part in (col_part(0, sides[0:16]), col_part(2, sides[16:32])):
            high = part.astype(BF16)
            pieces += [high, (part - high.astype(F32)).astype(BF16)]
        pre[0:16] += row_part(0, rims[0:32])
        pre[240:256] += row_part(2, rims[32:64])
        whole = pre[...] + dot(place, jnp.concatenate(pieces, axis=0))
        hidden = jax.nn.gelu(whole, approximate=True).astype(BF16)
        loads[n, 3].wait()
        result = (after + dot(hidden, wdown[n])).astype(BF16)
        if n == layers - 1:
            out_ref[...] = result
        else:
            xb[n + 1, 64:320] = result

    for n in range(layers):
        for slot, step in enumerate(STEPS):
            when_to(step, lambda slot=slot: remote(n, slot).wait_send())


PITCH = 24
HALO = 8


def halved(a, b):
    half = a.shape[0] // 32 * 16
    return jnp.concatenate([dot(a[:half], b), dot(a[half:], b)], axis=0)


def wide_kernel(
    n_lat, n_lon, x_hbm, gains_hbm, table_hbm, conv_hbm, wqkv_hbm, wout_hbm, wup_hbm, wdown_hbm,
    out_ref, gains_ref, table, conv_ref, wqkv, wout, wup, wdown, raw, stage, edge, xf, kvb, qf, af, nf, lifted_0, lifted_1, lifted_2, over_0, over_1, over_2, hidden_0, hidden_1, hidden_2, rows,
    bias, place, result, in_sem, w_sem, send_sem, recv_sem, here_sem,
):
    layers = wqkv.shape[0]
    tokens, width = x_hbm.shape
    lifted, over_rows, hidden = (lifted_0, lifted_1, lifted_2), (over_0, over_1, over_2), (hidden_0, hidden_1, hidden_2)
    cols = 16
    heads = table.shape[2]
    hid = wup.shape[2]
    chunks = hid // 128
    lat = lax.axis_index("lat")
    lon = lax.axis_index("lon")
    odd = lax.rem(lon, 2)
    near = lon + 1 - 2 * odd
    far = lax.rem(lon - 1 + 2 * odd + n_lon, n_lon)

    loads = {}
    firsts = (
        ("x", x_hbm.at[pl.ds(0, 128)], raw.at[pl.ds(0, 128)]),
        ("x2", x_hbm.at[pl.ds(128, 128)], raw.at[pl.ds(128, 128)]),
        ("gains", gains_hbm, gains_ref),
        ("table", table_hbm, table),
        ("conv", conv_hbm, conv_ref),
    )
    for k, (name, src, dst) in enumerate(firsts):
        loads[name] = pltpu.make_async_copy(src, dst, in_sem.at[k])
    for n in range(layers):
        pairs = ((wqkv_hbm, wqkv), (wout_hbm, wout), (wup_hbm, wup), (wdown_hbm, wdown))
        for k, (src, dst) in enumerate(pairs):
            loads[n, k] = pltpu.make_async_copy(src.at[n], dst.at[n], w_sem.at[n, k])
    loads["x"].start()
    loads["x2"].start()

    barrier = pltpu.get_barrier_semaphore()
    partners = ((lat, near), (1 - lat, near), (1 - lat, lon), (lat, far), (1 - lat, far))
    first, last = lon == 0, lon == n_lon - 1

    def greet(semaphore, row, col):
        pl.semaphore_signal(
            semaphore, inc=1, device_id={"lat": row, "lon": col}, device_id_type=pl.DeviceIdType.MESH
        )

    for row, col in partners[:3]:
        greet(barrier, row, col)

    eager = first | ((odd == 1) & jnp.logical_not(last))

    @pl.when(eager)
    def _():
        for row, col in partners[3:]:
            greet(barrier, row, col)

    def greet_back():
        for row, col in partners[3:]:
            greet(here_sem, row, col)

    @pl.when(last)
    def _():
        pl.semaphore_wait(barrier, len(partners))
        greet_back()

    remotes = []
    pieces = (
        (edge.at[pl.ds(0, 128)], stage.at[pl.ds(0, 128)]),
        (edge.at[pl.ds(128, 64)], stage.at[pl.ds(128, 64)]),
        (edge.at[pl.ds(384, 128)], stage.at[pl.ds(192, 128)]),
        (edge.at[pl.ds(192, 128)], stage.at[pl.ds(320, 128)]),
        (edge.at[pl.ds(320, 64)], stage.at[pl.ds(448, 64)]),
    )
    for slot, (src, dst) in enumerate(pieces):
        remotes.append(
            pltpu.make_async_remote_copy(
                src_ref=src,
                dst_ref=dst,
                send_sem=send_sem.at[slot],
                recv_sem=recv_sem.at[slot],
                device_id={"lat": partners[slot][0], "lon": partners[slot][1]},
                device_id_type=pl.DeviceIdType.MESH,
            )
        )

    def flip(value, by):
        return value + by * (cols - 1 - 2 * value)

    def choose(count, shift, column):
        m, t = iota((count, 1), 0), iota((count, tokens), 1)
        i = m & ((1 << shift) - 1)
        v = i if shift == 4 else cols - 1 - i
        return hot(t == flip(v, lat) * cols + flip(column(m >> shift), odd))

    picks = (
        choose(128, 4, lambda k: 15 - k),
        choose(64, 3, lambda k: 15 - k),
        choose(128, 4, lambda k: 7 - k),
        choose(64, 3, lambda k: 7 - k),
        choose(128, 3, lambda k: k),
    )
    picks = jnp.concatenate(picks, axis=0)
    pick_own = choose(256, 4, lambda k: k)
    loads["x"].wait()
    loads["x2"].wait()
    for name in ("table", "gains", (0, 0), "conv", (0, 1), (0, 2), (0, 3), (1, 0), (1, 1), (1, 2), (1, 3)):
        loads[name].start()
    edge[...] = halved(picks, raw[...]).astype(BF16)
    @pl.when(jnp.logical_not(last))
    def _():
        pl.semaphore_wait(barrier, len(partners) - jnp.where(eager, 2, 0))

    @pl.when(last)
    def _():
        for remote in remotes[3:]:
            remote.start()

    for remote in remotes[:3]:
        remote.start()

    @pl.when(jnp.logical_not(eager | last))
    def _():
        greet_back()

    def answer():
        @pl.when(first)
        def _():
            pl.semaphore_wait(here_sem, 2)
            for remote in remotes[3:]:
                remote.start()

    kvb[0, 768:832] = jnp.zeros((64, 2 * width), BF16)
    kvb[1, 672:832] = jnp.zeros((160, 2 * width), BF16)

    m, t = iota((256, 256), 0), iota((256, 256), 1)
    u, v = flip(m & 15, odd), flip(m >> 4, lat)
    for k in range(2):
        place[k] = hot(t == (u - 8 * k) * PITCH + v)

    loads["table"].wait()
    for n in range(layers):
        for b in range(WINDOW):
            rows[heads * n : heads * (n + 1), 16 * b : 16 * b + 2 * WINDOW - 1] = table[n, b]
    lane, v = iota((PITCH, 256), 1), iota((PITCH, 256), 0)
    start = jnp.maximum(v - REACH, 0)
    for n in range(layers):
        if n == 0:
            double = (lane * 1366) >> 16
            rest = lane - 2 * PITCH * double
            key_u = 2 * double + jnp.where(rest < 32, rest >> 4, (rest - 32) >> 3)
            key_v = jnp.where(rest < 32, rest & 15, 16 + (rest & 7))
        else:
            key_u = (lane * 2731) >> 16
            key_v = lane - PITCH * key_u
        row_ok = (key_v >= start) & (key_v < start + WINDOW)
        away = jnp.clip((key_v - v) * (1 - 2 * lat) + WINDOW - 1, 0, 2 * WINDOW - 2)
        for q in range(GROUP):
            off = key_u - REACH - q
            ok = row_ok & (off >= -REACH) & (off <= REACH)
            at = jnp.clip(off * (1 - 2 * odd) + REACH, 0, WINDOW - 1) * 16 + away
            for h in range(heads):
                line = jnp.broadcast_to(rows[n * heads + h : n * heads + h + 1, :], (PITCH, 128))
                got = [jnp.take_along_axis(line, at[:, s : s + 128], axis=1) for s in (0, 128)]
                value = jnp.where(ok, jnp.concatenate(got, axis=1) * 1.4426950408889634, -1000000000.0)
                bias[n, h, PITCH * q : PITCH * (q + 1), :] = value

    head_of = iota((1, width), 1) >> 6
    head_hot = [hot(head_of == h) for h in range(heads)]
    low_half = (iota((1, width), 1) & 127) < 64
    log2e = 1.4426950408889634
    scale = (width // heads) ** (-0.5) * log2e

    def multiply(n, wide):
        norm = normed(wide, gains_ref[n, 0:1, :])
        product = halved if wide.shape[0] > 256 else dot
        return product(norm, wqkv[n, :, width:]).astype(BF16), product(norm, wqkv[n, :, :width])

    def project(n, first, count, q_from, q_count):
        kv, query = multiply(n, xf[n, PITCH * first : PITCH * (first + count), :])
        kvb[n, PITCH * first : PITCH * (first + count), :] = kv
        at = PITCH * (q_from + 3 - first)
        qf[PITCH * q_from : PITCH * (q_from + q_count), :] = query[at : at + PITCH * q_count]

    def spread(wide, kv, query, at, shift, first, count):
        high = 1 << shift
        low = 0 if shift == 4 else 16
        for k in range(count):
            here = slice(at + high * k, at + high * (k + 1))
            to = PITCH * (first + k) + low
            xf[0, to : to + high, :] = wide[here]
            j = first + k - 3
            if 0 <= j < 26:
                qf[PITCH * j + low : PITCH * j + low + high, :] = query[here]
        for p in range(count // 2):
            to = PITCH * (first + 2 * p) + 2 * low
            kvb[0, to : to + 2 * high, :] = kv[at + 2 * high * p : at + 2 * high * (p + 1)]

    def attend(n, tiles, finish):
        def score(j, w):
            count = PITCH * w
            q = (qf[PITCH * j : PITCH * (j + w), :] * scale).astype(BF16)
            keys = kvb[n, PITCH * j : PITCH * j + 256, 0:width]
            stacked = jnp.concatenate([q * head_hot[h] for h in range(heads)], axis=0)
            return lax.dot_general(stacked, keys, (((1,), (1,)), ((), ())), preferred_element_type=F32)

        def soften(scores, w):
            count = PITCH * w
            weights = []
            for h in range(heads):
                held = scores[count * h : count * (h + 1)] + bias[n, h, 0:count, :]
                weights.append(jnp.exp2((held - jnp.max(held, axis=-1, keepdims=True)).astype(BF16)))
            return weights

        def gather_values(weights, j, w):
            count = PITCH * w
            totals = []
            for pair in range(heads // 2):
                at = width + 128 * pair
                own = kvb[n, PITCH * j : PITCH * j + 256, at : at + 128]
                values = jnp.concatenate([own, jnp.ones(own.shape, BF16)], axis=1)
                both = jnp.concatenate(weights[2 * pair : 2 * pair + 2], axis=0)
                mixed = dot(both, values)
                mixed = jnp.where(low_half, mixed[0:count], mixed[count : 2 * count])
                total = mixed[:, 0:128] * (1.0 / mixed[:, 128:256])
                totals.append(total.astype(BF16))
            return jnp.concatenate(totals, axis=1)

        ahead = [score(*tile) for tile in tiles[:2]]
        attended = []
        for k, (j, w) in enumerate(tiles):
            weights = soften(ahead[k], w)
            if k + 2 < len(tiles):
                ahead.append(score(*tiles[k + 2]))
            attended.append(gather_values(weights, j, w))
            if k > 0:
                finish(*tiles[k - 1], attended[k - 1])
        finish(*tiles[-1], attended[-1])

    def tap(n, a, b, ch):
        return conv_ref[a + lat * (2 - 2 * a), b + odd * (2 - 2 * b), n : n + 1, 128 * ch : 128 * (ch + 1)]

    def feed(n, tiles, l0, lifts, o0, outs):
        def finish(j, w, attended):
            size = PITCH * w
            here = slice(PITCH * j, PITCH * j + size)
            after = xf[n, PITCH * (j + 3) : PITCH * (j + 3) + size, :] + dot(attended, wout[n])
            af[here] = after
            scaled = lax.rsqrt(jnp.mean(after * after, axis=-1, keepdims=True) + 1e-06)
            line = iota((size, 1), 0)
            line = line - PITCH * ((line * 2731) >> 16)
            scaled = jnp.where(line == PITCH - 1, 0.0, scaled)
            norm = after * scaled * gains_ref[n, 1:2, :]
            for k in range(2):
                nf[k, 8 + PITCH * j : 8 + PITCH * j + size, :] = norm[:, 128 * k : 128 * (k + 1)]

        attend(n, tiles, finish)
        high = PITCH if n == 0 else 16
        moved = []
        for a in range(3):
            halves = []
            for k in range(2):
                if n == 0:
                    at = 8 + PITCH * l0 + a - 1
                    halves.append(nf[k, at : at + PITCH * lifts, :].astype(BF16))
                else:
                    spots = [8 + PITCH * j + a - 1 for j in range(l0, l0 + lifts)]
                    halves.append(jnp.concatenate([nf[k, at : at + 16, :] for at in spots], axis=0).astype(BF16))
            moved.append(jnp.concatenate(halves, axis=1))
        tall = moved[0].shape[0]
        moved = jnp.concatenate(moved, axis=0)

        def lift_up(double):
            product = dot(moved, wup[n, :, 256 * double : 256 * (double + 1)])
            for a in range(3):
                both = product[tall * a : tall * (a + 1)]
                for ch in range(2):
                    lift = both[:, 128 * ch : 128 * (ch + 1)]
                    if n == 0:
                        lift = lift.reshape(lifts, PITCH, 128)
                        base = lift[:, 0:16].reshape(16 * lifts, 128).astype(BF16)
                        over = lift[:, 16:PITCH]
                        pairs = jnp.concatenate([over[:-1], over[1:]], axis=1).reshape(-1, 128)
                        over_rows[double][a, ch, 16 * l0 : 16 * (l0 + lifts - 1), :] = pairs.astype(BF16)
                    else:
                        base = lift.astype(BF16)
                    lifted[double][a, ch, 16 * l0 : 16 * (l0 + lifts), :] = base

        def convolve(ch):
            taps = [[(0.5 * tap(n, a, b, ch)).astype(BF16) for b in range(3)] for a in range(3)]

            def convolved(source, j, wide):
                total = None
                for a in range(3):
                    for b in range(3):
                        at = 16 * (j + b - 1)
                        term = taps[a][b] * source[a, ch % 2, at : at + 16 * wide, :]
                        total = term if total is None else total + term
                inner = total * (1.5957691216057308 + 0.285419265090401 * (total * total))
                return total + total * jnp.tanh(inner)

            for part in range(0, outs, 2):
                main = convolved(lifted[ch // 2], o0 + part, 2)
                if n == 0:
                    rest = convolved(over_rows[ch // 2], o0 + part, 1).astype(F32)
                    main = main.astype(F32)
                    main = jnp.concatenate([main[0:16], rest[0:8], main[16:32], rest[8:16]], axis=0).astype(BF16)
                side = slice(128 * (ch % 2), 128 * (ch % 2 + 1))
                hidden[ch // 2][high * part : high * (part + 2), side] = main

        product = halved if high * outs > 256 else dot
        down = None
        lift_up(0)
        for double in range(chunks // 2):
            if double + 1 < chunks // 2:
                lift_up(double + 1)
            convolve(2 * double)
            convolve(2 * double + 1)
            units = slice(256 * double, 256 * (double + 1))
            part = product(hidden[double][0 : high * outs], wdown[n, units, :])
            down = part if down is None else down + part
        if n == 0:
            xf[1, PITCH * (o0 + 3) : PITCH * (o0 + 3 + outs), :] = af[PITCH * o0 : PITCH * (o0 + outs)] + down
        else:
            for k in range(outs):
                at = PITCH * (o0 + k)
                out = af[at : at + 16] + down[16 * k : 16 * (k + 1)]
                af[at : at + 16] = out

    loads["gains"].wait()
    loads[0, 0].wait()
    wide = dot(pick_own, raw[...])
    kv, query = multiply(0, wide)
    spread(wide, kv, query, 0, 4, 8, 16)
    remotes[2].wait_recv()
    wide = stage[192:320].astype(F32)
    kv, query = multiply(0, wide)
    spread(wide, kv, query, 0, 3, 8, 16)
    loads["conv"].wait()
    for k in range(1, 4):
        loads[0, k].wait()
    feed(0, ((8, 4), (12, 4)), 8, 8, 9, 6)
    for k in (0, 1):
        remotes[k].wait_recv()

    @pl.when(eager & jnp.logical_not(first))
    def _():
        pl.semaphore_wait(here_sem, 2)

    @pl.when(jnp.logical_not(first | last))
    def _():
        for remote in remotes[3:]:
            remote.start()

    wide = stage[0:192].astype(F32)
    kv, query = multiply(0, wide)
    spread(wide, kv, query, 0, 4, 24, 8)
    spread(wide, kv, query, 128, 3, 24, 8)
    feed(0, ((16, 4), (20, 4), (24, 2)), 15, 11, 15, 10)
    for k in range(4):
        loads[1, k].wait()
    project(1, 12, 16, 9, 13)
    answer()
    feed(1, ((12, 4), (16, 4), (20, 2)), 12, 10, 13, 8)
    result[...] = dot(place[1, :, 0:192], af[PITCH * 13 : PITCH * 21].astype(BF16))
    for k in (3, 4):
        remotes[k].wait_recv()
    wide = stage[320:512].astype(F32)
    kv, query = multiply(0, wide)
    spread(wide, kv, query, 0, 4, 0, 8)
    spread(wide, kv, query, 128, 3, 0, 8)
    feed(0, ((0, 4), (4, 4)), 0, 9, 1, 8)
    project(1, 4, 8, 4, 5)
    feed(1, ((4, 4), (8, 4)), 4, 8, 5, 8)
    out_ref[...] = (result[...] + dot(place[0, :, 0:192], af[PITCH * 5 : PITCH * 13].astype(BF16))).astype(BF16)
    for remote in remotes:
        remote.wait_send()


def wide_call(n_lat, n_lon, stream, gains, table, conv, w_qkv, w_out, w_up, w_down):
    layers = w_qkv.shape[0]
    width = stream.shape[1]
    hid = w_up.shape[2]
    vmem = pl.BlockSpec(memory_space=pltpu.VMEM)
    anywhere = pl.BlockSpec(memory_space=pltpu.HBM)
    heads = table.shape[2]
    return pl.pallas_call(
        functools.partial(wide_kernel, n_lat, n_lon),
        out_shape=pltpu.VMEM(stream.shape, BF16),
        in_specs=[anywhere] * 8,
        out_specs=vmem,
        scratch_shapes=[
            pltpu.VMEM(gains.shape, F32),
            pltpu.VMEM(table.shape, F32),
            pltpu.VMEM(conv.shape, F32),
            pltpu.VMEM(w_qkv.shape, BF16),
            pltpu.VMEM(w_out.shape, BF16),
            pltpu.VMEM(w_up.shape, BF16),
            pltpu.VMEM(w_down.shape, BF16),
            pltpu.VMEM((256, width), BF16),
            pltpu.VMEM((512, width), BF16),
            pltpu.VMEM((512, width), BF16),
            pltpu.VMEM((layers, 32 * PITCH, width), F32),
            pltpu.VMEM((layers, 832, 2 * width), BF16),
            pltpu.VMEM((26 * PITCH, width), F32),
            pltpu.VMEM((26 * PITCH, width), F32),
            pltpu.VMEM((2, 26 * PITCH + 16, 128), F32),
            *[pltpu.VMEM((3, 2, 26 * 16, 128), BF16)] * (hid // 128),
            *[pltpu.VMEM((16 * PITCH, 256), BF16)] * (hid // 256),
            pltpu.VMEM((layers * heads, 128), F32),
            pltpu.VMEM((layers, heads, GROUP * PITCH, 256), F32),
            pltpu.VMEM((2, 256, 256), BF16),
            pltpu.VMEM((256, width), F32),
            pltpu.SemaphoreType.DMA((5,)),
            pltpu.SemaphoreType.DMA((layers, 4)),
            pltpu.SemaphoreType.DMA((5,)),
            pltpu.SemaphoreType.DMA((5,)),
            pltpu.SemaphoreType.REGULAR,
        ],
        compiler_params=pltpu.CompilerParams(
            collective_id=0, has_side_effects=True, vmem_limit_bytes=58 * 1024 * 1024
        ),
    )(stream, gains, table, conv, w_qkv, w_out, w_up, w_down)


def on_device(n_lat, n_lon, stream, gains, w_qkv, table, w_out, w_up, conv, w_down):
    rows, cols, width = stream.shape
    layers, heads = table.shape[:2]
    table = table.transpose(0, 3, 1, 2)
    conv = conv.transpose(1, 2, 0, 3)
    hid = w_up.shape[2]
    vmem = pl.BlockSpec(memory_space=pltpu.VMEM)
    anywhere = pl.BlockSpec(memory_space=pltpu.HBM)
    if n_lat == 2 and n_lon % 2 == 0 and n_lon > 2:
        result = wide_call(
            n_lat, n_lon, stream.reshape(rows * cols, width), gains, table, conv, w_qkv, w_out, w_up, w_down
        )
        return result.reshape(rows, cols, width)
    result = pl.pallas_call(
        functools.partial(kernel, n_lat, n_lon),
        out_shape=pltpu.VMEM((rows * cols, width), BF16),
        in_specs=[anywhere] * 8,
        out_specs=vmem,
        scratch_shapes=[
            pltpu.VMEM(gains.shape, F32),
            pltpu.VMEM(table.shape, F32),
            pltpu.VMEM(conv.shape, F32),
            pltpu.VMEM(w_qkv.shape, BF16),
            pltpu.VMEM(w_out.shape, BF16),
            pltpu.VMEM(w_up.shape, BF16),
            pltpu.VMEM(w_down.shape, BF16),
            pltpu.VMEM((384, 2 * width), BF16),
            pltpu.VMEM((96, 2 * width), BF16),
            pltpu.VMEM((96, 2 * width), BF16),
            pltpu.VMEM((layers, 384, width), BF16),
            pltpu.VMEM((layers, 96, width), BF16),
            pltpu.VMEM((layers, 96, width), BF16),
            pltpu.VMEM((layers, 128, width), BF16),
            pltpu.VMEM((288, hid), F32),
            pltpu.VMEM((256, hid), F32),
            pltpu.VMEM((WINDOW, layers * heads, 128), F32),
            pltpu.VMEM((WINDOW, layers * heads, 256), F32),
            pltpu.VMEM((layers, 3, 320, 256), F32),
            pltpu.VMEM((layers, 2, 128, 256), F32),
            pltpu.VMEM((384, width), BF16),
            pltpu.SemaphoreType.DMA((4,)),
            pltpu.SemaphoreType.DMA((layers, 4)),
            pltpu.SemaphoreType.DMA((layers, 8)),
            pltpu.SemaphoreType.DMA((layers, 8)),
        ],
        compiler_params=pltpu.CompilerParams(
            collective_id=0, has_side_effects=True, vmem_limit_bytes=58 * 1024 * 1024
        ),
    )(
        stream.reshape(rows * cols, width),
        gains,
        table,
        conv,
        w_qkv,
        w_out,
        w_up,
        w_down,
    )
    return result.reshape(rows, cols, width)


def solution(mesh):
    sizes = dict(mesh.shape)
    in_specs = (P("lat", "lon", None), P(), P(), P(), P(), P(), P(), P())
    return jax.shard_map(
        functools.partial(on_device, sizes["lat"], sizes["lon"]),
        mesh=mesh,
        in_specs=in_specs,
        out_specs=P("lat", "lon", None),
        check_vma=False,
    )
```

```python
import functools

import jax
import jax.numpy as jnp
from jax import lax
from jax.experimental import pallas as pl
from jax.experimental.pallas import tpu as pltpu
from jax.sharding import PartitionSpec as P

WINDOW = 7
REACH = 3
GROUP = 4
F32 = jnp.float32
BF16 = jnp.bfloat16

LEFT, RIGHT, TOP, BOTTOM, TOP_L, TOP_R, BOT_L, BOT_R = range(8)
STEPS = ((0, 1), (0, -1), (1, 0), (-1, 0), (1, 1), (1, -1), (-1, 1), (-1, -1))


def iota(shape, dim):
    return lax.broadcasted_iota(jnp.int32, shape, dim)


def hot(cond):
    return jnp.where(cond, 1.0, 0.0).astype(BF16)


def dot(a, b):
    return jnp.dot(a, b, preferred_element_type=F32)


def normed(wide, gain):
    scale = lax.rsqrt(jnp.mean(wide * wide, axis=-1, keepdims=True) + 1e-06)
    return (wide * scale * gain).astype(BF16)


def kernel(
    n_lat, n_lon, x_hbm, gains_hbm, table_hbm, conv_hbm, wqkv_hbm, wout_hbm, wup_hbm, wdown_hbm,
    out_ref, gains_ref, table, conv_ref, wqkv, wout, wup, wdown, kvb, near_l, near_r, xb, left, right, edge, lpad, pre, rows, spread,
    bias, row_bias, attn, in_sem, w_sem, send_sem, recv_sem,
):
    layers = wqkv.shape[0]
    tokens, width = x_hbm.shape
    cols = 16
    heads = table.shape[2]
    hid = wup.shape[2]
    lat = lax.axis_index("lat")
    lon = lax.axis_index("lon")
    has_up = lat > 0
    has_down = lat < n_lat - 1
    total_rows = n_lat * (tokens // cols)
    first_row = lat * (tokens // cols)

    loads = {}
    firsts = (("x", x_hbm, xb.at[0, pl.ds(64, 256)]), ("gains", gains_hbm, gains_ref), ("table", table_hbm, table), ("conv", conv_hbm, conv_ref))
    for k, (name, src, dst) in enumerate(firsts):
        loads[name] = pltpu.make_async_copy(src, dst, in_sem.at[k])
    loads["x"].start()
    loads["gains"].start()
    for n in range(layers):
        pairs = ((wqkv_hbm, wqkv), (wout_hbm, wout), (wup_hbm, wup), (wdown_hbm, wdown))
        for k, (src, dst) in enumerate(pairs):
            loads[n, k] = pltpu.make_async_copy(src.at[n], dst.at[n], w_sem.at[n, k])
            loads[n, k].start()
            if n == 0 and k == 0:
                loads["table"].start()
                loads["conv"].start()

    def target(step):
        return {"lat": lat + step[0], "lon": lax.rem(lon + step[1] + n_lon, n_lon)}

    def when_to(step, go):
        if step[0] == 0:
            go()
        else:
            pl.when(has_down if step[0] > 0 else has_up)(go)

    def when_from(step, go):
        when_to((-step[0], -step[1]), go)

    barrier = pltpu.get_barrier_semaphore()
    for step in STEPS:
        when_to(
            step,
            lambda step=step: pl.semaphore_signal(
                barrier, inc=1, device_id=target(step), device_id_type=pl.DeviceIdType.MESH
            ),
        )

    def remote(n, slot):
        own, lo, ro, ed = xb.at[n], left.at[n], right.at[n], edge.at[n]
        src, dst = (
            (ed.at[pl.ds(64, 64)], lo.at[pl.ds(16, 64)]),
            (ed.at[pl.ds(0, 64)], ro.at[pl.ds(16, 64)]),
            (own.at[pl.ds(256, 64)], own.at[pl.ds(0, 64)]),
            (own.at[pl.ds(64, 64)], own.at[pl.ds(320, 64)]),
            (ed.at[pl.ds(112, 16)], lo.at[pl.ds(0, 16)]),
            (ed.at[pl.ds(48, 16)], ro.at[pl.ds(0, 16)]),
            (ed.at[pl.ds(64, 16)], lo.at[pl.ds(80, 16)]),
            (ed.at[pl.ds(0, 16)], ro.at[pl.ds(80, 16)]),
        )[slot]
        return pltpu.make_async_remote_copy(
            src_ref=src,
            dst_ref=dst,
            send_sem=send_sem.at[n, slot],
            recv_sem=recv_sem.at[n, slot],
            device_id=target(STEPS[slot]),
            device_id_type=pl.DeviceIdType.MESH,
        )

    def send(n):
        for slot, step in enumerate(STEPS):
            when_to(step, lambda slot=slot: remote(n, slot).start())

    def receive(n):
        for slot, step in enumerate(STEPS):
            when_from(step, lambda slot=slot: remote(n, slot).wait_recv())

    @pl.when(jnp.logical_not(has_up))
    def _():
        for n in range(layers):
            xb[n, 0:64] = jnp.zeros((64, width), BF16)
            left[n, 0:16] = jnp.zeros((16, width), BF16)
            right[n, 0:16] = jnp.zeros((16, width), BF16)
        attn[320:352] = jnp.zeros((32, width), BF16)

    @pl.when(jnp.logical_not(has_down))
    def _():
        for n in range(layers):
            xb[n, 320:384] = jnp.zeros((64, width), BF16)
            left[n, 80:96] = jnp.zeros((16, width), BF16)
            right[n, 80:96] = jnp.zeros((16, width), BF16)
        attn[352:384] = jnp.zeros((32, width), BF16)

    lpad[0:16] = jnp.zeros((16, hid), F32)
    lpad[272:288] = jnp.zeros((16, hid), F32)

    m, t = iota((128, tokens), 0), iota((128, tokens), 1)
    pick_kv = hot(t == ((m & 63) >> 2) * cols + (m & 3) + jnp.where(m >= 64, cols - 4, 0))
    m, t = iota((128, 320), 0), iota((128, 320), 1)
    e = m & 31
    side = 4 * (4 * (m >> 4) + (m & 3) + 4)
    flank = jnp.where((m & 15) < 4, 128 + side + 3, jnp.where((m & 15) < 8, 224 + side, -1))
    above = jnp.where(e < 16, 48 + e, jnp.where(e == 16, 143, jnp.where(e == 17, 236, -1)))
    below = jnp.where(e < 16, 64 + e, jnp.where(e == 16, 211, jnp.where(e == 17, 304, -1)))
    pick_ring = hot(t == jnp.where(m < 64, flank, jnp.where(m < 96, above, below)))
    m, t = iota((32, 64), 0), iota((32, 64), 1)
    pick_side = hot(t == ((m & 15) >> 2) * 16 + (m & 3) + jnp.where(m < 16, 0, 4))
    t, k = iota((tokens, 64), 0), iota((tokens, 64), 1)
    place = hot(((k & 15) == (t >> 4)) & ((t & 15) == jnp.where(k < 32, 0, cols - 1)))
    head_of = iota((1, width), 1) >> 6
    head_hot = [hot(head_of == h) for h in range(heads)]

    def prepare(pick):
        for at in (0, 128):
            for b in range(WINDOW):
                spread[b, :, at : at + 128] = jnp.take_along_axis(
                    rows[b], pick[:, at : at + 128], axis=1
                )

    def chosen(row, offset):
        value = jnp.broadcast_to(spread[0, row : row + 1, :], offset.shape)
        for b in range(1, WINDOW):
            value = jnp.where(offset == b - REACH, spread[b, row : row + 1, :], value)
        return value

    def build_bias():
        for n in range(layers):
            for b in range(WINDOW):
                rows[b, heads * n : heads * (n + 1), 0 : 2 * WINDOW - 1] = table[n, b]
        x = iota((16, 256), 1)
        j = iota((16, 256), 0)
        own = x < 160
        on_left = x < 208
        y = jnp.where(on_left, x - 160, x - 208)
        p = jnp.where(own, x >> 4, (y >> 2) - 1)
        c = jnp.where(own, x & 15, jnp.where(on_left, (y & 3) - 4, (y & 3) + cols))
        col_ok = (c - j >= -REACH) & (c - j <= REACH)
        for i in range(GROUP):
            oks = []
            for group in (0, 1, 3):
                g = first_row + GROUP * group + i
                start = jnp.clip(g - REACH, 0, total_rows - WINDOW)
                r = first_row + GROUP * group - REACH + p
                oks.append(col_ok & (r >= start) & (r < start + WINDOW))
            prepare(jnp.clip(p[0:8] - i + REACH, 0, 2 * WINDOW - 2))
            for n in range(layers):
                for h in range(heads):
                    value = chosen(n * heads + h, c - j)
                    at = h * 80 + i * 16
                    for var in range(3):
                        bias[n, var, at : at + 16, :] = jnp.where(oks[var], value, -1000000000.0)
        e = iota((16, 256), 0)
        i, j = e & 3, jnp.where(e < 4, -1, cols)
        px, cx = p, c
        col_ok = (cx - j >= -REACH) & (cx - j <= REACH)
        oks = []
        for group in (0, 1, 3):
            g = first_row + GROUP * group + i
            start = jnp.clip(g - REACH, 0, total_rows - WINDOW)
            r = first_row + GROUP * group - REACH + px
            oks.append(col_ok & (r >= start) & (r < start + WINDOW))
        pick = jnp.clip(px - i + REACH, 0, 2 * WINDOW - 2)[0:8]
        for n in range(layers):
            for h in range(heads):
                value = jnp.zeros((8, 256), F32)
                for b in range(WINDOW):
                    source = jnp.broadcast_to(rows[b, n * heads + h : n * heads + h + 1, :], (8, 128))
                    got = [
                        jnp.take_along_axis(source, pick[:, at : at + 128], axis=1)
                        for at in (0, 128)
                    ]
                    value = jnp.where(
                        (cx - j)[0:8] == b - REACH, jnp.concatenate(got, axis=1), value
                    )
                at = h * 80 + 64
                for var in range(3):
                    bias[n, var, at : at + 8, :] = jnp.where(oks[var][0:8], value, -1000000000.0)
                    bias[n, var, at + 8 : at + 16, :] = jnp.zeros((8, 256), F32)
        x, e = iota((32, 256), 1), iota((32, 256), 0)
        j = jnp.where(e < 16, e, jnp.where(e == 16, -1, cols))
        own, on_left = x < 160, x < 208
        y = jnp.where(on_left, x - 160, x - 208)
        c = jnp.where(own, x & 15, jnp.where(on_left, (y & 3) - 4, (y & 3) + cols))
        for k, (here, first_own, first_near) in enumerate(((-1, -4, -4), (16, 10, 8))):
            away = jnp.where(own, first_own + (x >> 4), first_near + (y >> 2)) - here
            ok = (c - j >= -REACH) & (c - j <= REACH) & (away >= -REACH) & (away <= REACH)
            prepare(jnp.clip(away[0:8] + WINDOW - 1, 0, 2 * WINDOW - 2))
            for n in range(layers):
                for h in range(heads):
                    value = chosen(n * heads + h, c - j)
                    row_bias[n, k, h * 32 : h * 32 + 32, :] = jnp.where(ok, value, -1000000000.0)

    def attend(q, near, held, count):
        stacked = jnp.concatenate([q * head_hot[h] for h in range(heads)], axis=0)
        scores = lax.dot_general(
            stacked, near[:, :width], (((1,), (1,)), ((), ())), preferred_element_type=F32
        )
        scores = scores + held
        raised = jnp.exp(scores - jnp.max(scores, axis=-1, keepdims=True))
        weights = (raised * (1.0 / jnp.sum(raised, axis=-1, keepdims=True))).astype(BF16)
        mixed = dot(weights, near[:, width:])
        total = jnp.where(head_of == 0, mixed[0:count], 0.0)
        for h in range(1, heads):
            total = jnp.where(head_of == h, mixed[count * h : count * (h + 1)], total)
        return total.astype(BF16)

    def near_keys(own, side):
        parts = [kvb[own : own + 160, :], near_l[side : side + 48, :], near_r[side : side + 48, :]]
        return jnp.concatenate(parts, axis=0)

    scale = (width // heads) ** (-0.5)
    loads["x"].wait()
    for n in range(layers):
        current = xb[n, 64:320]
        edge[n] = dot(pick_kv, current).astype(BF16)
        if n == 0:
            count = 2 + jnp.where(has_up, 3, 0) + jnp.where(has_down, 3, 0)
            pl.semaphore_wait(barrier, count)
        send(n)
        if n == 0:
            loads["gains"].wait()
        gain = gains_ref[n, 0:1, :]
        wide = current.astype(F32)
        norm = normed(wide, gain)
        loads[n, 0].wait()
        kvb[64:320] = dot(norm, wqkv[n, :, width:]).astype(BF16)
        query = (dot(norm, wqkv[n, :, :width]).astype(BF16) * scale).astype(BF16)
        if n == 0:
            loads["table"].wait()
            build_bias()
            loads["conv"].wait()
        receive(n)
        around = jnp.concatenate([xb[n, 0:64], xb[n, 320:384], left[n], right[n]], axis=0)
        ring = dot(pick_ring, around)
        near = dot(normed(around.astype(F32), gain), wqkv[n, :, width:]).astype(BF16)
        kvb[0:64] = near[0:64]
        kvb[320:384] = near[64:128]
        near_l[...] = near[128:224]
        near_r[...] = near[224:320]
        ring_query = (dot(normed(ring, gain), wqkv[n, :, :width]).astype(BF16) * scale).astype(BF16)
        for group in range(4):
            at = 64 * group
            more = slice(16 * group, 16 * group + 16)
            q = jnp.concatenate([query[at : at + 64], ring_query[more]], axis=0)
            held = bias[n, (0, 1, 1, 2)[group]]
            got = attend(q, near_keys(at + 16, 16 * group), held, 80)
            attn[at : at + 64, :] = got[0:64]
            attn[256 + 16 * group : 272 + 16 * group, :] = got[64:80]

        @pl.when(has_up)
        def _():
            attn[320:352] = attend(ring_query[64:96], near_keys(0, 0), row_bias[n, 0], 32)

        @pl.when(has_down)
        def _():
            attn[352:384] = attend(ring_query[96:128], near_keys(224, 48), row_bias[n, 1], 32)

        loads[n, 1].wait()
        after = jnp.concatenate([wide, ring], axis=0) + dot(attn[...], wout[n])
        norm = normed(after, gains_ref[n, 1:2, :])
        after = after[0:tokens]
        loads[n, 2].wait()
        lift = dot(norm, wup[n]).astype(BF16)
        sides = dot(pick_side, lift[256:320])
        rims = lift[320:384].astype(F32)
        lpad[16:272] = lift[0:tokens].astype(F32)
        col = iota((tokens, 128), 0) & 15
        for ch in range(hid // 128):
            at = slice(128 * ch, 128 * ch + 128)
            above, here, below = lpad[0:256, at], lpad[16:272, at], lpad[32:288, at]

            def column(b):
                return (
                    conv_ref[0, b, n : n + 1, at] * above
                    + conv_ref[1, b, n : n + 1, at] * here
                    + conv_ref[2, b, n : n + 1, at] * below
                )

            pre[:, at] = (
                column(1)
                + jnp.where(col > 0, pltpu.roll(column(0), 1, 0), 0.0)
                + jnp.where(col < cols - 1, pltpu.roll(column(2), tokens - 1, 0), 0.0)
            )
        line = iota((16, hid), 0)

        def tap(a, b):
            return conv_ref[a, b, n : n + 1, :]

        def row_part(a, rim):
            middle = rim[0:16]
            back = jnp.where(line == 0, rim[16:17], pltpu.roll(middle, 1, 0))
            ahead = jnp.where(line == 15, rim[17:18], pltpu.roll(middle, 15, 0))
            return tap(a, 0) * back + tap(a, 1) * middle + tap(a, 2) * ahead

        def col_part(b, values):
            up = jnp.where(line == 0, 0.0, pltpu.roll(values, 1, 0))
            down = jnp.where(line == 15, 0.0, pltpu.roll(values, 15, 0))
            return tap(0, b) * up + tap(1, b) * values + tap(2, b) * down

        pieces = []
        for part in (col_part(0, sides[0:16]), col_part(2, sides[16:32])):
            high = part.astype(BF16)
            pieces += [high, (part - high.astype(F32)).astype(BF16)]
        pre[0:16] += row_part(0, rims[0:32])
        pre[240:256] += row_part(2, rims[32:64])
        whole = pre[...] + dot(place, jnp.concatenate(pieces, axis=0))
        hidden = jax.nn.gelu(whole, approximate=True).astype(BF16)
        loads[n, 3].wait()
        result = (after + dot(hidden, wdown[n])).astype(BF16)
        if n == layers - 1:
            out_ref[...] = result
        else:
            xb[n + 1, 64:320] = result

    for n in range(layers):
        for slot, step in enumerate(STEPS):
            when_to(step, lambda slot=slot: remote(n, slot).wait_send())


PITCH = 24
HALO = 8


def halved(a, b):
    half = a.shape[0] // 32 * 16
    return jnp.concatenate([dot(a[:half], b), dot(a[half:], b)], axis=0)


def wide_kernel(
    n_lat, n_lon, x_hbm, gains_hbm, table_hbm, conv_hbm, wqkv_hbm, wout_hbm, wup_hbm, wdown_hbm,
    out_ref, gains_ref, table, conv_ref, wqkv, wout, wup, wdown, raw, stage, edge, xf, kvb, qf, af, nf, lifted_0, lifted_1, lifted_2, over_0, over_1, over_2, hidden_0, hidden_1, hidden_2, rows,
    bias, place, result, in_sem, w_sem, send_sem, recv_sem, here_sem,
):
    layers = wqkv.shape[0]
    tokens, width = x_hbm.shape
    lifted, over_rows, hidden = (lifted_0, lifted_1, lifted_2), (over_0, over_1, over_2), (hidden_0, hidden_1, hidden_2)
    cols = 16
    heads = table.shape[2]
    hid = wup.shape[2]
    chunks = hid // 128
    lat = lax.axis_index("lat")
    lon = lax.axis_index("lon")
    odd = lax.rem(lon, 2)
    near = lon + 1 - 2 * odd
    far = lax.rem(lon - 1 + 2 * odd + n_lon, n_lon)

    loads = {}
    firsts = (
        ("x", x_hbm.at[pl.ds(0, 128)], raw.at[pl.ds(0, 128)]),
        ("x2", x_hbm.at[pl.ds(128, 128)], raw.at[pl.ds(128, 128)]),
        ("gains", gains_hbm, gains_ref),
        ("table", table_hbm, table),
        ("conv", conv_hbm, conv_ref),
    )
    for k, (name, src, dst) in enumerate(firsts):
        loads[name] = pltpu.make_async_copy(src, dst, in_sem.at[k])
    for n in range(layers):
        pairs = ((wqkv_hbm, wqkv), (wout_hbm, wout), (wup_hbm, wup), (wdown_hbm, wdown))
        for k, (src, dst) in enumerate(pairs):
            loads[n, k] = pltpu.make_async_copy(src.at[n], dst.at[n], w_sem.at[n, k])
    loads["x"].start()
    loads["x2"].start()

    barrier = pltpu.get_barrier_semaphore()
    partners = ((lat, near), (1 - lat, near), (1 - lat, lon), (lat, far), (1 - lat, far))
    first, last = lon == 0, lon == n_lon - 1

    def greet(semaphore, row, col):
        pl.semaphore_signal(
            semaphore, inc=1, device_id={"lat": row, "lon": col}, device_id_type=pl.DeviceIdType.MESH
        )

    for row, col in partners[:3]:
        greet(barrier, row, col)

    eager = first | ((odd == 1) & jnp.logical_not(last))

    @pl.when(eager)
    def _():
        for row, col in partners[3:]:
            greet(barrier, row, col)

    def greet_back():
        for row, col in partners[3:]:
            greet(here_sem, row, col)

    @pl.when(last)
    def _():
        pl.semaphore_wait(barrier, len(partners))
        greet_back()

    remotes = []
    pieces = (
        (edge.at[pl.ds(0, 128)], stage.at[pl.ds(0, 128)]),
        (edge.at[pl.ds(128, 64)], stage.at[pl.ds(128, 64)]),
        (edge.at[pl.ds(384, 128)], stage.at[pl.ds(192, 128)]),
        (edge.at[pl.ds(192, 128)], stage.at[pl.ds(320, 128)]),
        (edge.at[pl.ds(320, 64)], stage.at[pl.ds(448, 64)]),
    )
    for slot, (src, dst) in enumerate(pieces):
        remotes.append(
            pltpu.make_async_remote_copy(
                src_ref=src,
                dst_ref=dst,
                send_sem=send_sem.at[slot],
                recv_sem=recv_sem.at[slot],
                device_id={"lat": partners[slot][0], "lon": partners[slot][1]},
                device_id_type=pl.DeviceIdType.MESH,
            )
        )

    def flip(value, by):
        return value + by * (cols - 1 - 2 * value)

    def choose(count, shift, column):
        m, t = iota((count, 1), 0), iota((count, tokens), 1)
        i = m & ((1 << shift) - 1)
        v = i if shift == 4 else cols - 1 - i
        return hot(t == flip(v, lat) * cols + flip(column(m >> shift), odd))

    picks = (
        choose(128, 4, lambda k: 15 - k),
        choose(64, 3, lambda k: 15 - k),
        choose(128, 4, lambda k: 7 - k),
        choose(64, 3, lambda k: 7 - k),
        choose(128, 3, lambda k: k),
    )
    pick_own = choose(256, 4, lambda k: k)
    loads["x"].wait()
    loads["x2"].wait()

    def far_edge():
        edge[192:384] = dot(jnp.concatenate(picks[2:4], axis=0), raw[...]).astype(BF16)

    @pl.when(last)
    def _():
        far_edge()
        for remote in remotes[3:]:
            remote.start()

    edge[0:192] = dot(jnp.concatenate(picks[0:2], axis=0), raw[...]).astype(BF16)
    edge[384:512] = dot(picks[4], raw[...]).astype(BF16)
    for name in ("table", "gains", (0, 0), "conv", (0, 1), (0, 2), (0, 3), (1, 0), (1, 1), (1, 2), (1, 3)):
        loads[name].start()
    @pl.when(jnp.logical_not(last))
    def _():
        pl.semaphore_wait(barrier, len(partners) - jnp.where(eager, 2, 0))

    for remote in remotes[:3]:
        remote.start()

    @pl.when(jnp.logical_not(eager | last))
    def _():
        greet_back()

    @pl.when(jnp.logical_not(last))
    def _():
        far_edge()

    def answer():
        @pl.when(first)
        def _():
            pl.semaphore_wait(here_sem, 2)
            for remote in remotes[3:]:
                remote.start()

    kvb[0, 768:832] = jnp.zeros((64, 2 * width), BF16)
    kvb[1, 672:832] = jnp.zeros((160, 2 * width), BF16)

    m, t = iota((256, 256), 0), iota((256, 256), 1)
    u, v = flip(m & 15, odd), flip(m >> 4, lat)
    for k in range(2):
        place[k] = hot(t == (u - 8 * k) * PITCH + v)

    loads["table"].wait()
    for n in range(layers):
        for b in range(WINDOW):
            rows[heads * n : heads * (n + 1), 16 * b : 16 * b + 2 * WINDOW - 1] = table[n, b]
    lane, v = iota((PITCH, 256), 1), iota((PITCH, 256), 0)
    start = jnp.maximum(v - REACH, 0)
    for n in range(layers):
        if n == 0:
            double = (lane * 1366) >> 16
            rest = lane - 2 * PITCH * double
            key_u = 2 * double + jnp.where(rest < 32, rest >> 4, (rest - 32) >> 3)
            key_v = jnp.where(rest < 32, rest & 15, 16 + (rest & 7))
        else:
            key_u = (lane * 2731) >> 16
            key_v = lane - PITCH * key_u
        row_ok = (key_v >= start) & (key_v < start + WINDOW)
        away = jnp.clip((key_v - v) * (1 - 2 * lat) + WINDOW - 1, 0, 2 * WINDOW - 2)
        for q in range(GROUP):
            off = key_u - REACH - q
            ok = row_ok & (off >= -REACH) & (off <= REACH)
            at = jnp.clip(off * (1 - 2 * odd) + REACH, 0, WINDOW - 1) * 16 + away
            for h in range(heads):
                line = jnp.broadcast_to(rows[n * heads + h : n * heads + h + 1, :], (PITCH, 128))
                got = [jnp.take_along_axis(line, at[:, s : s + 128], axis=1) for s in (0, 128)]
                value = jnp.where(ok, jnp.concatenate(got, axis=1) * 1.4426950408889634, -1000000000.0)
                bias[n, h, PITCH * q : PITCH * (q + 1), :] = value

    head_of = iota((1, width), 1) >> 6
    head_hot = [hot(head_of == h) for h in range(heads)]
    low_half = (iota((1, width), 1) & 127) < 64
    log2e = 1.4426950408889634
    scale = (width // heads) ** (-0.5) * log2e

    def multiply(n, wide):
        norm = normed(wide, gains_ref[n, 0:1, :])
        product = halved if wide.shape[0] > 256 else dot
        return product(norm, wqkv[n, :, width:]).astype(BF16), product(norm, wqkv[n, :, :width])

    def project(n, first, count, q_from, q_count):
        kv, query = multiply(n, xf[n, PITCH * first : PITCH * (first + count), :])
        kvb[n, PITCH * first : PITCH * (first + count), :] = kv
        at = PITCH * (q_from + 3 - first)
        qf[PITCH * q_from : PITCH * (q_from + q_count), :] = query[at : at + PITCH * q_count]

    def spread(wide, kv, query, at, shift, first, count):
        high = 1 << shift
        low = 0 if shift == 4 else 16
        for k in range(count):
            here = slice(at + high * k, at + high * (k + 1))
            to = PITCH * (first + k) + low
            xf[0, to : to + high, :] = wide[here]
            j = first + k - 3
            if 0 <= j < 26:
                qf[PITCH * j + low : PITCH * j + low + high, :] = query[here]
        for p in range(count // 2):
            to = PITCH * (first + 2 * p) + 2 * low
            kvb[0, to : to + 2 * high, :] = kv[at + 2 * high * p : at + 2 * high * (p + 1)]

    def attend(n, tiles, finish):
        def score(j, w):
            count = PITCH * w
            q = (qf[PITCH * j : PITCH * (j + w), :] * scale).astype(BF16)
            keys = kvb[n, PITCH * j : PITCH * j + 256, 0:width]
            stacked = jnp.concatenate([q * head_hot[h] for h in range(heads)], axis=0)
            return lax.dot_general(stacked, keys, (((1,), (1,)), ((), ())), preferred_element_type=F32)

        def soften(scores, w):
            count = PITCH * w
            weights = []
            for h in range(heads):
                held = scores[count * h : count * (h + 1)] + bias[n, h, 0:count, :]
                weights.append(jnp.exp2((held - jnp.max(held, axis=-1, keepdims=True)).astype(BF16)))
            return weights

        def gather_values(weights, j, w):
            count = PITCH * w
            totals = []
            for pair in range(heads // 2):
                at = width + 128 * pair
                own = kvb[n, PITCH * j : PITCH * j + 256, at : at + 128]
                values = jnp.concatenate([own, jnp.ones(own.shape, BF16)], axis=1)
                both = jnp.concatenate(weights[2 * pair : 2 * pair + 2], axis=0)
                mixed = dot(both, values)
                mixed = jnp.where(low_half, mixed[0:count], mixed[count : 2 * count])
                total = mixed[:, 0:128] * (1.0 / mixed[:, 128:256])
                totals.append(total.astype(BF16))
            return jnp.concatenate(totals, axis=1)

        ahead = [score(*tile) for tile in tiles[:2]]
        attended = []
        for k, (j, w) in enumerate(tiles):
            weights = soften(ahead[k], w)
            if k + 2 < len(tiles):
                ahead.append(score(*tiles[k + 2]))
            attended.append(gather_values(weights, j, w))
            if k > 0:
                finish(*tiles[k - 1], attended[k - 1])
        finish(*tiles[-1], attended[-1])

    def tap(n, a, b, ch):
        return conv_ref[a + lat * (2 - 2 * a), b + odd * (2 - 2 * b), n : n + 1, 128 * ch : 128 * (ch + 1)]

    def feed(n, tiles, l0, lifts, o0, outs):
        def finish(j, w, attended):
            size = PITCH * w
            here = slice(PITCH * j, PITCH * j + size)
            after = xf[n, PITCH * (j + 3) : PITCH * (j + 3) + size, :] + dot(attended, wout[n])
            af[here] = after
            scaled = lax.rsqrt(jnp.mean(after * after, axis=-1, keepdims=True) + 1e-06)
            line = iota((size, 1), 0)
            line = line - PITCH * ((line * 2731) >> 16)
            scaled = jnp.where(line == PITCH - 1, 0.0, scaled)
            norm = after * scaled * gains_ref[n, 1:2, :]
            for k in range(2):
                nf[k, 8 + PITCH * j : 8 + PITCH * j + size, :] = norm[:, 128 * k : 128 * (k + 1)]

        attend(n, tiles, finish)
        high = PITCH if n == 0 else 16
        moved = []
        for a in range(3):
            halves = []
            for k in range(2):
                if n == 0:
                    at = 8 + PITCH * l0 + a - 1
                    halves.append(nf[k, at : at + PITCH * lifts, :].astype(BF16))
                else:
                    spots = [8 + PITCH * j + a - 1 for j in range(l0, l0 + lifts)]
                    halves.append(jnp.concatenate([nf[k, at : at + 16, :] for at in spots], axis=0).astype(BF16))
            moved.append(jnp.concatenate(halves, axis=1))
        tall = moved[0].shape[0]
        moved = jnp.concatenate(moved, axis=0)

        def lift_up(double):
            product = dot(moved, wup[n, :, 256 * double : 256 * (double + 1)])
            for a in range(3):
                both = product[tall * a : tall * (a + 1)]
                for ch in range(2):
                    lift = both[:, 128 * ch : 128 * (ch + 1)]
                    if n == 0:
                        lift = lift.reshape(lifts, PITCH, 128)
                        base = lift[:, 0:16].reshape(16 * lifts, 128).astype(BF16)
                        over = lift[:, 16:PITCH]
                        pairs = jnp.concatenate([over[:-1], over[1:]], axis=1).reshape(-1, 128)
                        over_rows[double][a, ch, 16 * l0 : 16 * (l0 + lifts - 1), :] = pairs.astype(BF16)
                    else:
                        base = lift.astype(BF16)
                    lifted[double][a, ch, 16 * l0 : 16 * (l0 + lifts), :] = base

        def convolve(ch):
            taps = [[(0.5 * tap(n, a, b, ch)).astype(BF16) for b in range(3)] for a in range(3)]

            def convolved(source, j, wide):
                total = None
                for a in range(3):
                    for b in range(3):
                        at = 16 * (j + b - 1)
                        term = taps[a][b] * source[a, ch % 2, at : at + 16 * wide, :]
                        total = term if total is None else total + term
                inner = total * (1.5957691216057308 + 0.285419265090401 * (total * total))
                return total + total * jnp.tanh(inner)

            for part in range(0, outs, 2):
                main = convolved(lifted[ch // 2], o0 + part, 2)
                if n == 0:
                    rest = convolved(over_rows[ch // 2], o0 + part, 1).astype(F32)
                    main = main.astype(F32)
                    main = jnp.concatenate([main[0:16], rest[0:8], main[16:32], rest[8:16]], axis=0).astype(BF16)
                side = slice(128 * (ch % 2), 128 * (ch % 2 + 1))
                hidden[ch // 2][high * part : high * (part + 2), side] = main

        product = halved if high * outs > 256 else dot
        down = None
        lift_up(0)
        for double in range(chunks // 2):
            if double + 1 < chunks // 2:
                lift_up(double + 1)
            convolve(2 * double)
            convolve(2 * double + 1)
            units = slice(256 * double, 256 * (double + 1))
            part = product(hidden[double][0 : high * outs], wdown[n, units, :])
            down = part if down is None else down + part
        if n == 0:
            xf[1, PITCH * (o0 + 3) : PITCH * (o0 + 3 + outs), :] = af[PITCH * o0 : PITCH * (o0 + outs)] + down
        else:
            for k in range(outs):
                at = PITCH * (o0 + k)
                out = af[at : at + 16] + down[16 * k : 16 * (k + 1)]
                af[at : at + 16] = out

    loads["gains"].wait()
    loads[0, 0].wait()
    wide = dot(pick_own, raw[...])
    kv, query = multiply(0, wide)
    spread(wide, kv, query, 0, 4, 8, 16)
    remotes[2].wait_recv()
    wide = stage[192:320].astype(F32)
    kv, query = multiply(0, wide)
    spread(wide, kv, query, 0, 3, 8, 16)
    loads["conv"].wait()
    for k in range(1, 4):
        loads[0, k].wait()
    feed(0, ((8, 4), (12, 4)), 8, 8, 9, 6)
    for k in (0, 1):
        remotes[k].wait_recv()

    @pl.when(eager & jnp.logical_not(first))
    def _():
        pl.semaphore_wait(here_sem, 2)

    @pl.when(jnp.logical_not(first | last))
    def _():
        for remote in remotes[3:]:
            remote.start()

    wide = stage[0:192].astype(F32)
    kv, query = multiply(0, wide)
    spread(wide, kv, query, 0, 4, 24, 8)
    spread(wide, kv, query, 128, 3, 24, 8)
    feed(0, ((16, 4), (20, 4), (24, 2)), 15, 11, 15, 10)
    for k in range(4):
        loads[1, k].wait()
    answer()
    project(1, 12, 16, 9, 13)
    feed(1, ((12, 4), (16, 4), (20, 2)), 12, 10, 13, 8)
    result[...] = dot(place[1, :, 0:192], af[PITCH * 13 : PITCH * 21].astype(BF16))
    for k in (3, 4):
        remotes[k].wait_recv()
    wide = stage[320:512].astype(F32)
    kv, query = multiply(0, wide)
    spread(wide, kv, query, 0, 4, 0, 8)
    spread(wide, kv, query, 128, 3, 0, 8)
    feed(0, ((0, 4), (4, 4)), 0, 9, 1, 8)
    project(1, 4, 8, 4, 5)
    feed(1, ((4, 4), (8, 4)), 4, 8, 5, 8)
    out_ref[...] = (result[...] + dot(place[0, :, 0:192], af[PITCH * 5 : PITCH * 13].astype(BF16))).astype(BF16)
    for remote in remotes:
        remote.wait_send()


def wide_call(n_lat, n_lon, stream, gains, table, conv, w_qkv, w_out, w_up, w_down):
    layers = w_qkv.shape[0]
    width = stream.shape[1]
    hid = w_up.shape[2]
    vmem = pl.BlockSpec(memory_space=pltpu.VMEM)
    anywhere = pl.BlockSpec(memory_space=pltpu.HBM)
    heads = table.shape[2]
    return pl.pallas_call(
        functools.partial(wide_kernel, n_lat, n_lon),
        out_shape=pltpu.VMEM(stream.shape, BF16),
        in_specs=[anywhere] * 8,
        out_specs=vmem,
        scratch_shapes=[
            pltpu.VMEM(gains.shape, F32),
            pltpu.VMEM(table.shape, F32),
            pltpu.VMEM(conv.shape, F32),
            pltpu.VMEM(w_qkv.shape, BF16),
            pltpu.VMEM(w_out.shape, BF16),
            pltpu.VMEM(w_up.shape, BF16),
            pltpu.VMEM(w_down.shape, BF16),
            pltpu.VMEM((256, width), BF16),
            pltpu.VMEM((512, width), BF16),
            pltpu.VMEM((512, width), BF16),
            pltpu.VMEM((layers, 32 * PITCH, width), F32),
            pltpu.VMEM((layers, 832, 2 * width), BF16),
            pltpu.VMEM((26 * PITCH, width), F32),
            pltpu.VMEM((26 * PITCH, width), F32),
            pltpu.VMEM((2, 26 * PITCH + 16, 128), F32),
            *[pltpu.VMEM((3, 2, 26 * 16, 128), BF16)] * (hid // 128),
            *[pltpu.VMEM((16 * PITCH, 256), BF16)] * (hid // 256),
            pltpu.VMEM((layers * heads, 128), F32),
            pltpu.VMEM((layers, heads, GROUP * PITCH, 256), F32),
            pltpu.VMEM((2, 256, 256), BF16),
            pltpu.VMEM((256, width), F32),
            pltpu.SemaphoreType.DMA((5,)),
            pltpu.SemaphoreType.DMA((layers, 4)),
            pltpu.SemaphoreType.DMA((5,)),
            pltpu.SemaphoreType.DMA((5,)),
            pltpu.SemaphoreType.REGULAR,
        ],
        compiler_params=pltpu.CompilerParams(
            collective_id=0, has_side_effects=True, vmem_limit_bytes=58 * 1024 * 1024
        ),
    )(stream, gains, table, conv, w_qkv, w_out, w_up, w_down)


def on_device(n_lat, n_lon, stream, gains, w_qkv, table, w_out, w_up, conv, w_down):
    rows, cols, width = stream.shape
    layers, heads = table.shape[:2]
    table = table.transpose(0, 3, 1, 2)
    conv = conv.transpose(1, 2, 0, 3)
    hid = w_up.shape[2]
    vmem = pl.BlockSpec(memory_space=pltpu.VMEM)
    anywhere = pl.BlockSpec(memory_space=pltpu.HBM)
    if n_lat == 2 and n_lon % 2 == 0 and n_lon > 2:
        result = wide_call(
            n_lat, n_lon, stream.reshape(rows * cols, width), gains, table, conv, w_qkv, w_out, w_up, w_down
        )
        return result.reshape(rows, cols, width)
    result = pl.pallas_call(
        functools.partial(kernel, n_lat, n_lon),
        out_shape=pltpu.VMEM((rows * cols, width), BF16),
        in_specs=[anywhere] * 8,
        out_specs=vmem,
        scratch_shapes=[
            pltpu.VMEM(gains.shape, F32),
            pltpu.VMEM(table.shape, F32),
            pltpu.VMEM(conv.shape, F32),
            pltpu.VMEM(w_qkv.shape, BF16),
            pltpu.VMEM(w_out.shape, BF16),
            pltpu.VMEM(w_up.shape, BF16),
            pltpu.VMEM(w_down.shape, BF16),
            pltpu.VMEM((384, 2 * width), BF16),
            pltpu.VMEM((96, 2 * width), BF16),
            pltpu.VMEM((96, 2 * width), BF16),
            pltpu.VMEM((layers, 384, width), BF16),
            pltpu.VMEM((layers, 96, width), BF16),
            pltpu.VMEM((layers, 96, width), BF16),
            pltpu.VMEM((layers, 128, width), BF16),
            pltpu.VMEM((288, hid), F32),
            pltpu.VMEM((256, hid), F32),
            pltpu.VMEM((WINDOW, layers * heads, 128), F32),
            pltpu.VMEM((WINDOW, layers * heads, 256), F32),
            pltpu.VMEM((layers, 3, 320, 256), F32),
            pltpu.VMEM((layers, 2, 128, 256), F32),
            pltpu.VMEM((384, width), BF16),
            pltpu.SemaphoreType.DMA((4,)),
            pltpu.SemaphoreType.DMA((layers, 4)),
            pltpu.SemaphoreType.DMA((layers, 8)),
            pltpu.SemaphoreType.DMA((layers, 8)),
        ],
        compiler_params=pltpu.CompilerParams(
            collective_id=0, has_side_effects=True, vmem_limit_bytes=58 * 1024 * 1024
        ),
    )(
        stream.reshape(rows * cols, width),
        gains,
        table,
        conv,
        w_qkv,
        w_out,
        w_up,
        w_down,
    )
    return result.reshape(rows, cols, width)


def solution(mesh):
    sizes = dict(mesh.shape)
    in_specs = (P("lat", "lon", None), P(), P(), P(), P(), P(), P(), P())
    return jax.shard_map(
        functools.partial(on_device, sizes["lat"], sizes["lon"]),
        mesh=mesh,
        in_specs=in_specs,
        out_specs=P("lat", "lon", None),
        check_vma=False,
    )
```

```python
import functools

import jax
import jax.numpy as jnp
from jax import lax
from jax.experimental import pallas as pl
from jax.experimental.pallas import tpu as pltpu
from jax.sharding import PartitionSpec as P

WINDOW = 7
REACH = 3
GROUP = 4
F32 = jnp.float32
BF16 = jnp.bfloat16

LEFT, RIGHT, TOP, BOTTOM, TOP_L, TOP_R, BOT_L, BOT_R = range(8)
STEPS = ((0, 1), (0, -1), (1, 0), (-1, 0), (1, 1), (1, -1), (-1, 1), (-1, -1))


def iota(shape, dim):
    return lax.broadcasted_iota(jnp.int32, shape, dim)


def hot(cond):
    return jnp.where(cond, 1.0, 0.0).astype(BF16)


def dot(a, b):
    return jnp.dot(a, b, preferred_element_type=F32)


def normed(wide, gain):
    scale = lax.rsqrt(jnp.mean(wide * wide, axis=-1, keepdims=True) + 1e-06)
    return (wide * scale * gain).astype(BF16)


def kernel(
    n_lat, n_lon, x_hbm, gains_hbm, table_hbm, conv_hbm, wqkv_hbm, wout_hbm, wup_hbm, wdown_hbm,
    out_ref, gains_ref, table, conv_ref, wqkv, wout, wup, wdown, kvb, near_l, near_r, xb, left, right, edge, lpad, pre, rows, spread,
    bias, row_bias, attn, in_sem, w_sem, send_sem, recv_sem,
):
    layers = wqkv.shape[0]
    tokens, width = x_hbm.shape
    cols = 16
    heads = table.shape[2]
    hid = wup.shape[2]
    lat = lax.axis_index("lat")
    lon = lax.axis_index("lon")
    has_up = lat > 0
    has_down = lat < n_lat - 1
    total_rows = n_lat * (tokens // cols)
    first_row = lat * (tokens // cols)

    loads = {}
    firsts = (("x", x_hbm, xb.at[0, pl.ds(64, 256)]), ("gains", gains_hbm, gains_ref), ("table", table_hbm, table), ("conv", conv_hbm, conv_ref))
    for k, (name, src, dst) in enumerate(firsts):
        loads[name] = pltpu.make_async_copy(src, dst, in_sem.at[k])
    loads["x"].start()
    loads["gains"].start()
    for n in range(layers):
        pairs = ((wqkv_hbm, wqkv), (wout_hbm, wout), (wup_hbm, wup), (wdown_hbm, wdown))
        for k, (src, dst) in enumerate(pairs):
            loads[n, k] = pltpu.make_async_copy(src.at[n], dst.at[n], w_sem.at[n, k])
            loads[n, k].start()
            if n == 0 and k == 0:
                loads["table"].start()
                loads["conv"].start()

    def target(step):
        return {"lat": lat + step[0], "lon": lax.rem(lon + step[1] + n_lon, n_lon)}

    def when_to(step, go):
        if step[0] == 0:
            go()
        else:
            pl.when(has_down if step[0] > 0 else has_up)(go)

    def when_from(step, go):
        when_to((-step[0], -step[1]), go)

    barrier = pltpu.get_barrier_semaphore()
    for step in STEPS:
        when_to(
            step,
            lambda step=step: pl.semaphore_signal(
                barrier, inc=1, device_id=target(step), device_id_type=pl.DeviceIdType.MESH
            ),
        )

    def remote(n, slot):
        own, lo, ro, ed = xb.at[n], left.at[n], right.at[n], edge.at[n]
        src, dst = (
            (ed.at[pl.ds(64, 64)], lo.at[pl.ds(16, 64)]),
            (ed.at[pl.ds(0, 64)], ro.at[pl.ds(16, 64)]),
            (own.at[pl.ds(256, 64)], own.at[pl.ds(0, 64)]),
            (own.at[pl.ds(64, 64)], own.at[pl.ds(320, 64)]),
            (ed.at[pl.ds(112, 16)], lo.at[pl.ds(0, 16)]),
            (ed.at[pl.ds(48, 16)], ro.at[pl.ds(0, 16)]),
            (ed.at[pl.ds(64, 16)], lo.at[pl.ds(80, 16)]),
            (ed.at[pl.ds(0, 16)], ro.at[pl.ds(80, 16)]),
        )[slot]
        return pltpu.make_async_remote_copy(
            src_ref=src,
            dst_ref=dst,
            send_sem=send_sem.at[n, slot],
            recv_sem=recv_sem.at[n, slot],
            device_id=target(STEPS[slot]),
            device_id_type=pl.DeviceIdType.MESH,
        )

    def send(n):
        for slot, step in enumerate(STEPS):
            when_to(step, lambda slot=slot: remote(n, slot).start())

    def receive(n):
        for slot, step in enumerate(STEPS):
            when_from(step, lambda slot=slot: remote(n, slot).wait_recv())

    @pl.when(jnp.logical_not(has_up))
    def _():
        for n in range(layers):
            xb[n, 0:64] = jnp.zeros((64, width), BF16)
            left[n, 0:16] = jnp.zeros((16, width), BF16)
            right[n, 0:16] = jnp.zeros((16, width), BF16)
        attn[320:352] = jnp.zeros((32, width), BF16)

    @pl.when(jnp.logical_not(has_down))
    def _():
        for n in range(layers):
            xb[n, 320:384] = jnp.zeros((64, width), BF16)
            left[n, 80:96] = jnp.zeros((16, width), BF16)
            right[n, 80:96] = jnp.zeros((16, width), BF16)
        attn[352:384] = jnp.zeros((32, width), BF16)

    lpad[0:16] = jnp.zeros((16, hid), F32)
    lpad[272:288] = jnp.zeros((16, hid), F32)

    m, t = iota((128, tokens), 0), iota((128, tokens), 1)
    pick_kv = hot(t == ((m & 63) >> 2) * cols + (m & 3) + jnp.where(m >= 64, cols - 4, 0))
    m, t = iota((128, 320), 0), iota((128, 320), 1)
    e = m & 31
    side = 4 * (4 * (m >> 4) + (m & 3) + 4)
    flank = jnp.where((m & 15) < 4, 128 + side + 3, jnp.where((m & 15) < 8, 224 + side, -1))
    above = jnp.where(e < 16, 48 + e, jnp.where(e == 16, 143, jnp.where(e == 17, 236, -1)))
    below = jnp.where(e < 16, 64 + e, jnp.where(e == 16, 211, jnp.where(e == 17, 304, -1)))
    pick_ring = hot(t == jnp.where(m < 64, flank, jnp.where(m < 96, above, below)))
    m, t = iota((32, 64), 0), iota((32, 64), 1)
    pick_side = hot(t == ((m & 15) >> 2) * 16 + (m & 3) + jnp.where(m < 16, 0, 4))
    t, k = iota((tokens, 64), 0), iota((tokens, 64), 1)
    place = hot(((k & 15) == (t >> 4)) & ((t & 15) == jnp.where(k < 32, 0, cols - 1)))
    head_of = iota((1, width), 1) >> 6
    head_hot = [hot(head_of == h) for h in range(heads)]

    def prepare(pick):
        for at in (0, 128):
            for b in range(WINDOW):
                spread[b, :, at : at + 128] = jnp.take_along_axis(
                    rows[b], pick[:, at : at + 128], axis=1
                )

    def chosen(row, offset):
        value = jnp.broadcast_to(spread[0, row : row + 1, :], offset.shape)
        for b in range(1, WINDOW):
            value = jnp.where(offset == b - REACH, spread[b, row : row + 1, :], value)
        return value

    def build_bias():
        for n in range(layers):
            for b in range(WINDOW):
                rows[b, heads * n : heads * (n + 1), 0 : 2 * WINDOW - 1] = table[n, b]
        x = iota((16, 256), 1)
        j = iota((16, 256), 0)
        own = x < 160
        on_left = x < 208
        y = jnp.where(on_left, x - 160, x - 208)
        p = jnp.where(own, x >> 4, (y >> 2) - 1)
        c = jnp.where(own, x & 15, jnp.where(on_left, (y & 3) - 4, (y & 3) + cols))
        col_ok = (c - j >= -REACH) & (c - j <= REACH)
        for i in range(GROUP):
            oks = []
            for group in (0, 1, 3):
                g = first_row + GROUP * group + i
                start = jnp.clip(g - REACH, 0, total_rows - WINDOW)
                r = first_row + GROUP * group - REACH + p
                oks.append(col_ok & (r >= start) & (r < start + WINDOW))
            prepare(jnp.clip(p[0:8] - i + REACH, 0, 2 * WINDOW - 2))
            for n in range(layers):
                for h in range(heads):
                    value = chosen(n * heads + h, c - j)
                    at = h * 80 + i * 16
                    for var in range(3):
                        bias[n, var, at : at + 16, :] = jnp.where(oks[var], value, -1000000000.0)
        e = iota((16, 256), 0)
        i, j = e & 3, jnp.where(e < 4, -1, cols)
        px, cx = p, c
        col_ok = (cx - j >= -REACH) & (cx - j <= REACH)
        oks = []
        for group in (0, 1, 3):
            g = first_row + GROUP * group + i
            start = jnp.clip(g - REACH, 0, total_rows - WINDOW)
            r = first_row + GROUP * group - REACH + px
            oks.append(col_ok & (r >= start) & (r < start + WINDOW))
        pick = jnp.clip(px - i + REACH, 0, 2 * WINDOW - 2)[0:8]
        for n in range(layers):
            for h in range(heads):
                value = jnp.zeros((8, 256), F32)
                for b in range(WINDOW):
                    source = jnp.broadcast_to(rows[b, n * heads + h : n * heads + h + 1, :], (8, 128))
                    got = [
                        jnp.take_along_axis(source, pick[:, at : at + 128], axis=1)
                        for at in (0, 128)
                    ]
                    value = jnp.where(
                        (cx - j)[0:8] == b - REACH, jnp.concatenate(got, axis=1), value
                    )
                at = h * 80 + 64
                for var in range(3):
                    bias[n, var, at : at + 8, :] = jnp.where(oks[var][0:8], value, -1000000000.0)
                    bias[n, var, at + 8 : at + 16, :] = jnp.zeros((8, 256), F32)
        x, e = iota((32, 256), 1), iota((32, 256), 0)
        j = jnp.where(e < 16, e, jnp.where(e == 16, -1, cols))
        own, on_left = x < 160, x < 208
        y = jnp.where(on_left, x - 160, x - 208)
        c = jnp.where(own, x & 15, jnp.where(on_left, (y & 3) - 4, (y & 3) + cols))
        for k, (here, first_own, first_near) in enumerate(((-1, -4, -4), (16, 10, 8))):
            away = jnp.where(own, first_own + (x >> 4), first_near + (y >> 2)) - here
            ok = (c - j >= -REACH) & (c - j <= REACH) & (away >= -REACH) & (away <= REACH)
            prepare(jnp.clip(away[0:8] + WINDOW - 1, 0, 2 * WINDOW - 2))
            for n in range(layers):
                for h in range(heads):
                    value = chosen(n * heads + h, c - j)
                    row_bias[n, k, h * 32 : h * 32 + 32, :] = jnp.where(ok, value, -1000000000.0)

    def attend(q, near, held, count):
        stacked = jnp.concatenate([q * head_hot[h] for h in range(heads)], axis=0)
        scores = lax.dot_general(
            stacked, near[:, :width], (((1,), (1,)), ((), ())), preferred_element_type=F32
        )
        scores = scores + held
        raised = jnp.exp(scores - jnp.max(scores, axis=-1, keepdims=True))
        weights = (raised * (1.0 / jnp.sum(raised, axis=-1, keepdims=True))).astype(BF16)
        mixed = dot(weights, near[:, width:])
        total = jnp.where(head_of == 0, mixed[0:count], 0.0)
        for h in range(1, heads):
            total = jnp.where(head_of == h, mixed[count * h : count * (h + 1)], total)
        return total.astype(BF16)

    def near_keys(own, side):
        parts = [kvb[own : own + 160, :], near_l[side : side + 48, :], near_r[side : side + 48, :]]
        return jnp.concatenate(parts, axis=0)

    scale = (width // heads) ** (-0.5)
    loads["x"].wait()
    for n in range(layers):
        current = xb[n, 64:320]
        edge[n] = dot(pick_kv, current).astype(BF16)
        if n == 0:
            count = 2 + jnp.where(has_up, 3, 0) + jnp.where(has_down, 3, 0)
            pl.semaphore_wait(barrier, count)
        send(n)
        if n == 0:
            loads["gains"].wait()
        gain = gains_ref[n, 0:1, :]
        wide = current.astype(F32)
        norm = normed(wide, gain)
        loads[n, 0].wait()
        kvb[64:320] = dot(norm, wqkv[n, :, width:]).astype(BF16)
        query = (dot(norm, wqkv[n, :, :width]).astype(BF16) * scale).astype(BF16)
        if n == 0:
            loads["table"].wait()
            build_bias()
            loads["conv"].wait()
        receive(n)
        around = jnp.concatenate([xb[n, 0:64], xb[n, 320:384], left[n], right[n]], axis=0)
        ring = dot(pick_ring, around)
        near = dot(normed(around.astype(F32), gain), wqkv[n, :, width:]).astype(BF16)
        kvb[0:64] = near[0:64]
        kvb[320:384] = near[64:128]
        near_l[...] = near[128:224]
        near_r[...] = near[224:320]
        ring_query = (dot(normed(ring, gain), wqkv[n, :, :width]).astype(BF16) * scale).astype(BF16)
        for group in range(4):
            at = 64 * group
            more = slice(16 * group, 16 * group + 16)
            q = jnp.concatenate([query[at : at + 64], ring_query[more]], axis=0)
            held = bias[n, (0, 1, 1, 2)[group]]
            got = attend(q, near_keys(at + 16, 16 * group), held, 80)
            attn[at : at + 64, :] = got[0:64]
            attn[256 + 16 * group : 272 + 16 * group, :] = got[64:80]

        @pl.when(has_up)
        def _():
            attn[320:352] = attend(ring_query[64:96], near_keys(0, 0), row_bias[n, 0], 32)

        @pl.when(has_down)
        def _():
            attn[352:384] = attend(ring_query[96:128], near_keys(224, 48), row_bias[n, 1], 32)

        loads[n, 1].wait()
        after = jnp.concatenate([wide, ring], axis=0) + dot(attn[...], wout[n])
        norm = normed(after, gains_ref[n, 1:2, :])
        after = after[0:tokens]
        loads[n, 2].wait()
        lift = dot(norm, wup[n]).astype(BF16)
        sides = dot(pick_side, lift[256:320])
        rims = lift[320:384].astype(F32)
        lpad[16:272] = lift[0:tokens].astype(F32)
        col = iota((tokens, 128), 0) & 15
        for ch in range(hid // 128):
            at = slice(128 * ch, 128 * ch + 128)
            above, here, below = lpad[0:256, at], lpad[16:272, at], lpad[32:288, at]

            def column(b):
                return (
                    conv_ref[0, b, n : n + 1, at] * above
                    + conv_ref[1, b, n : n + 1, at] * here
                    + conv_ref[2, b, n : n + 1, at] * below
                )

            pre[:, at] = (
                column(1)
                + jnp.where(col > 0, pltpu.roll(column(0), 1, 0), 0.0)
                + jnp.where(col < cols - 1, pltpu.roll(column(2), tokens - 1, 0), 0.0)
            )
        line = iota((16, hid), 0)

        def tap(a, b):
            return conv_ref[a, b, n : n + 1, :]

        def row_part(a, rim):
            middle = rim[0:16]
            back = jnp.where(line == 0, rim[16:17], pltpu.roll(middle, 1, 0))
            ahead = jnp.where(line == 15, rim[17:18], pltpu.roll(middle, 15, 0))
            return tap(a, 0) * back + tap(a, 1) * middle + tap(a, 2) * ahead

        def col_part(b, values):
            up = jnp.where(line == 0, 0.0, pltpu.roll(values, 1, 0))
            down = jnp.where(line == 15, 0.0, pltpu.roll(values, 15, 0))
            return tap(0, b) * up + tap(1, b) * values + tap(2, b) * down

        pieces = []
        for part in (col_part(0, sides[0:16]), col_part(2, sides[16:32])):
            high = part.astype(BF16)
            pieces += [high, (part - high.astype(F32)).astype(BF16)]
        pre[0:16] += row_part(0, rims[0:32])
        pre[240:256] += row_part(2, rims[32:64])
        whole = pre[...] + dot(place, jnp.concatenate(pieces, axis=0))
        hidden = jax.nn.gelu(whole, approximate=True).astype(BF16)
        loads[n, 3].wait()
        result = (after + dot(hidden, wdown[n])).astype(BF16)
        if n == layers - 1:
            out_ref[...] = result
        else:
            xb[n + 1, 64:320] = result

    for n in range(layers):
        for slot, step in enumerate(STEPS):
            when_to(step, lambda slot=slot: remote(n, slot).wait_send())


PITCH = 24
HALO = 8


def halved(a, b):
    half = a.shape[0] // 32 * 16
    return jnp.concatenate([dot(a[:half], b), dot(a[half:], b)], axis=0)


def wide_kernel(
    n_lat, n_lon, x_hbm, gains_hbm, table_hbm, conv_hbm, wqkv_hbm, wout_hbm, wup_hbm, wdown_hbm,
    out_ref, gains_ref, table, conv_ref, wqkv, wout, wup, wdown, raw, stage, edge, xf, kvb, qf, af, nf, lifted_0, lifted_1, lifted_2, over_0, over_1, over_2, hidden_0, hidden_1, hidden_2, rows,
    bias, place, result, in_sem, w_sem, send_sem, recv_sem, here_sem,
):
    layers = wqkv.shape[0]
    tokens, width = x_hbm.shape
    lifted, over_rows, hidden = (lifted_0, lifted_1, lifted_2), (over_0, over_1, over_2), (hidden_0, hidden_1, hidden_2)
    cols = 16
    heads = table.shape[2]
    hid = wup.shape[2]
    chunks = hid // 128
    lat = lax.axis_index("lat")
    lon = lax.axis_index("lon")
    odd = lax.rem(lon, 2)
    near = lon + 1 - 2 * odd
    far = lax.rem(lon - 1 + 2 * odd + n_lon, n_lon)

    loads = {}
    firsts = (
        ("x", x_hbm.at[pl.ds(0, 128)], raw.at[pl.ds(0, 128)]),
        ("x2", x_hbm.at[pl.ds(128, 128)], raw.at[pl.ds(128, 128)]),
        ("gains", gains_hbm, gains_ref),
        ("table", table_hbm, table),
        ("conv", conv_hbm, conv_ref),
    )
    for k, (name, src, dst) in enumerate(firsts):
        loads[name] = pltpu.make_async_copy(src, dst, in_sem.at[k])
    for n in range(layers):
        pairs = ((wqkv_hbm, wqkv), (wout_hbm, wout), (wup_hbm, wup), (wdown_hbm, wdown))
        for k, (src, dst) in enumerate(pairs):
            loads[n, k] = pltpu.make_async_copy(src.at[n], dst.at[n], w_sem.at[n, k])
    loads["x"].start()
    loads["x2"].start()

    barrier = pltpu.get_barrier_semaphore()
    partners = ((lat, near), (1 - lat, near), (1 - lat, lon), (lat, far), (1 - lat, far))
    first, last = lon == 0, lon == n_lon - 1

    def greet(semaphore, row, col):
        pl.semaphore_signal(
            semaphore, inc=1, device_id={"lat": row, "lon": col}, device_id_type=pl.DeviceIdType.MESH
        )

    for row, col in partners[:3]:
        greet(barrier, row, col)

    eager = first | ((odd == 1) & jnp.logical_not(last))

    @pl.when(eager)
    def _():
        for row, col in partners[3:]:
            greet(barrier, row, col)

    def greet_back():
        for row, col in partners[3:]:
            greet(here_sem, row, col)

    @pl.when(last)
    def _():
        pl.semaphore_wait(barrier, len(partners))
        greet_back()

    remotes = []
    pieces = (
        (edge.at[pl.ds(0, 128)], stage.at[pl.ds(0, 128)]),
        (edge.at[pl.ds(128, 64)], stage.at[pl.ds(128, 64)]),
        (edge.at[pl.ds(384, 128)], stage.at[pl.ds(192, 128)]),
        (edge.at[pl.ds(192, 128)], stage.at[pl.ds(320, 128)]),
        (edge.at[pl.ds(320, 64)], stage.at[pl.ds(448, 64)]),
    )
    for slot, (src, dst) in enumerate(pieces):
        remotes.append(
            pltpu.make_async_remote_copy(
                src_ref=src,
                dst_ref=dst,
                send_sem=send_sem.at[slot],
                recv_sem=recv_sem.at[slot],
                device_id={"lat": partners[slot][0], "lon": partners[slot][1]},
                device_id_type=pl.DeviceIdType.MESH,
            )
        )

    def flip(value, by):
        return value + by * (cols - 1 - 2 * value)

    def choose(count, shift, column):
        m, t = iota((count, 1), 0), iota((count, tokens), 1)
        i = m & ((1 << shift) - 1)
        v = i if shift == 4 else cols - 1 - i
        return hot(t == flip(v, lat) * cols + flip(column(m >> shift), odd))

    picks = (
        choose(128, 4, lambda k: 15 - k),
        choose(64, 3, lambda k: 15 - k),
        choose(128, 4, lambda k: 7 - k),
        choose(64, 3, lambda k: 7 - k),
        choose(128, 3, lambda k: k),
    )
    picks = jnp.concatenate(picks, axis=0)
    pick_own = choose(256, 4, lambda k: k)
    loads["x"].wait()
    loads["x2"].wait()
    for name in ("table", "gains", (0, 0), "conv", (0, 1), (0, 2), (0, 3), (1, 0), (1, 1), (1, 2), (1, 3)):
        loads[name].start()
    edge[...] = halved(picks, raw[...]).astype(BF16)
    @pl.when(jnp.logical_not(last))
    def _():
        pl.semaphore_wait(barrier, len(partners) - jnp.where(eager, 2, 0))

    @pl.when(last)
    def _():
        for remote in remotes[3:]:
            remote.start()

    for remote in remotes[:3]:
        remote.start()

    @pl.when(jnp.logical_not(eager | last))
    def _():
        greet_back()

    def answer():
        @pl.when(first)
        def _():
            pl.semaphore_wait(here_sem, 2)
            for remote in remotes[3:]:
                remote.start()

    kvb[0, 768:832] = jnp.zeros((64, 2 * width), BF16)
    kvb[1, 672:832] = jnp.zeros((160, 2 * width), BF16)

    m, t = iota((256, 256), 0), iota((256, 256), 1)
    u, v = flip(m & 15, odd), flip(m >> 4, lat)
    for k in range(2):
        place[k] = hot(t == (u - 8 * k) * PITCH + v)

    loads["table"].wait()
    for n in range(layers):
        for b in range(WINDOW):
            rows[heads * n : heads * (n + 1), 16 * b : 16 * b + 2 * WINDOW - 1] = table[n, b]
    lane, v = iota((PITCH, 256), 1), iota((PITCH, 256), 0)
    start = jnp.maximum(v - REACH, 0)
    for n in range(layers):
        if n == 0:
            double = (lane * 1366) >> 16
            rest = lane - 2 * PITCH * double
            key_u = 2 * double + jnp.where(rest < 32, rest >> 4, (rest - 32) >> 3)
            key_v = jnp.where(rest < 32, rest & 15, 16 + (rest & 7))
        else:
            key_u = (lane * 2731) >> 16
            key_v = lane - PITCH * key_u
        row_ok = (key_v >= start) & (key_v < start + WINDOW)
        away = jnp.clip((key_v - v) * (1 - 2 * lat) + WINDOW - 1, 0, 2 * WINDOW - 2)
        for q in range(GROUP):
            off = key_u - REACH - q
            ok = row_ok & (off >= -REACH) & (off <= REACH)
            at = jnp.clip(off * (1 - 2 * odd) + REACH, 0, WINDOW - 1) * 16 + away
            for h in range(heads):
                line = jnp.broadcast_to(rows[n * heads + h : n * heads + h + 1, :], (PITCH, 128))
                got = [jnp.take_along_axis(line, at[:, s : s + 128], axis=1) for s in (0, 128)]
                value = jnp.where(ok, jnp.concatenate(got, axis=1) * 1.4426950408889634, -1000000000.0)
                bias[n, h, PITCH * q : PITCH * (q + 1), :] = value

    head_of = iota((1, width), 1) >> 6
    head_hot = [hot(head_of == h) for h in range(heads)]
    low_half = (iota((1, width), 1) & 127) < 64
    log2e = 1.4426950408889634
    scale = (width // heads) ** (-0.5) * log2e

    def multiply(n, wide):
        norm = normed(wide, gains_ref[n, 0:1, :])
        return dot(norm, wqkv[n, :, width:]).astype(BF16), dot(norm, wqkv[n, :, :width])

    def project(n, first, count, q_from, q_count):
        kv, query = multiply(n, xf[n, PITCH * first : PITCH * (first + count), :])
        kvb[n, PITCH * first : PITCH * (first + count), :] = kv
        at = PITCH * (q_from + 3 - first)
        qf[PITCH * q_from : PITCH * (q_from + q_count), :] = query[at : at + PITCH * q_count]

    def spread(wide, kv, query, at, shift, first, count):
        high = 1 << shift
        low = 0 if shift == 4 else 16
        for k in range(count):
            here = slice(at + high * k, at + high * (k + 1))
            to = PITCH * (first + k) + low
            xf[0, to : to + high, :] = wide[here]
            j = first + k - 3
            if 0 <= j < 26:
                qf[PITCH * j + low : PITCH * j + low + high, :] = query[here]
        for p in range(count // 2):
            to = PITCH * (first + 2 * p) + 2 * low
            kvb[0, to : to + 2 * high, :] = kv[at + 2 * high * p : at + 2 * high * (p + 1)]

    def attend(n, tiles, finish):
        def score(j, w):
            count = PITCH * w
            q = (qf[PITCH * j : PITCH * (j + w), :] * scale).astype(BF16)
            keys = kvb[n, PITCH * j : PITCH * j + 256, 0:width]
            stacked = jnp.concatenate([q * head_hot[h] for h in range(heads)], axis=0)
            return lax.dot_general(stacked, keys, (((1,), (1,)), ((), ())), preferred_element_type=F32)

        def soften(scores, w):
            count = PITCH * w
            weights = []
            for h in range(heads):
                held = scores[count * h : count * (h + 1)] + bias[n, h, 0:count, :]
                weights.append(jnp.exp2((held - jnp.max(held, axis=-1, keepdims=True)).astype(BF16)))
            return weights

        def gather_values(weights, j, w):
            count = PITCH * w
            totals = []
            for pair in range(heads // 2):
                at = width + 128 * pair
                own = kvb[n, PITCH * j : PITCH * j + 256, at : at + 128]
                values = jnp.concatenate([own, jnp.ones(own.shape, BF16)], axis=1)
                both = jnp.concatenate(weights[2 * pair : 2 * pair + 2], axis=0)
                mixed = dot(both, values)
                mixed = jnp.where(low_half, mixed[0:count], mixed[count : 2 * count])
                total = mixed[:, 0:128] * (1.0 / mixed[:, 128:256])
                totals.append(total.astype(BF16))
            return jnp.concatenate(totals, axis=1)

        ahead = [score(*tile) for tile in tiles[:2]]
        attended = []
        for k, (j, w) in enumerate(tiles):
            weights = soften(ahead[k], w)
            if k + 2 < len(tiles):
                ahead.append(score(*tiles[k + 2]))
            attended.append(gather_values(weights, j, w))
        finish(tiles[0][0], sum(w for _, w in tiles), jnp.concatenate(attended, axis=0))

    def tap(n, a, b, ch):
        return conv_ref[a + lat * (2 - 2 * a), b + odd * (2 - 2 * b), n : n + 1, 128 * ch : 128 * (ch + 1)]

    def feed(n, tiles, l0, lifts, o0, outs):
        def finish(j, w, attended):
            size = PITCH * w
            here = slice(PITCH * j, PITCH * j + size)
            after = xf[n, PITCH * (j + 3) : PITCH * (j + 3) + size, :] + dot(attended, wout[n])
            af[here] = after
            scaled = lax.rsqrt(jnp.mean(after * after, axis=-1, keepdims=True) + 1e-06)
            line = iota((size, 1), 0)
            line = line - PITCH * ((line * 2731) >> 16)
            scaled = jnp.where(line == PITCH - 1, 0.0, scaled)
            norm = after * scaled * gains_ref[n, 1:2, :]
            for k in range(2):
                nf[k, 8 + PITCH * j : 8 + PITCH * j + size, :] = norm[:, 128 * k : 128 * (k + 1)]

        attend(n, tiles, finish)
        high = PITCH if n == 0 else 16
        moved = []
        for a in range(3):
            halves = []
            for k in range(2):
                if n == 0:
                    at = 8 + PITCH * l0 + a - 1
                    halves.append(nf[k, at : at + PITCH * lifts, :].astype(BF16))
                else:
                    spots = [8 + PITCH * j + a - 1 for j in range(l0, l0 + lifts)]
                    halves.append(jnp.concatenate([nf[k, at : at + 16, :] for at in spots], axis=0).astype(BF16))
            moved.append(jnp.concatenate(halves, axis=1))
        tall = moved[0].shape[0]
        moved = jnp.concatenate(moved, axis=0)

        def lift_up(double):
            product = dot(moved, wup[n, :, 256 * double : 256 * (double + 1)])
            for a in range(3):
                both = product[tall * a : tall * (a + 1)]
                for ch in range(2):
                    lift = both[:, 128 * ch : 128 * (ch + 1)]
                    if n == 0:
                        lift = lift.reshape(lifts, PITCH, 128)
                        base = lift[:, 0:16].reshape(16 * lifts, 128).astype(BF16)
                        over = lift[:, 16:PITCH]
                        pairs = jnp.concatenate([over[:-1], over[1:]], axis=1).reshape(-1, 128)
                        over_rows[double][a, ch, 16 * l0 : 16 * (l0 + lifts - 1), :] = pairs.astype(BF16)
                    else:
                        base = lift.astype(BF16)
                    lifted[double][a, ch, 16 * l0 : 16 * (l0 + lifts), :] = base

        def convolve(ch):
            taps = [[(0.5 * tap(n, a, b, ch)).astype(BF16) for b in range(3)] for a in range(3)]

            def convolved(source, j, wide):
                total = None
                for a in range(3):
                    for b in range(3):
                        at = 16 * (j + b - 1)
                        term = taps[a][b] * source[a, ch % 2, at : at + 16 * wide, :]
                        total = term if total is None else total + term
                inner = total * (1.5957691216057308 + 0.285419265090401 * (total * total))
                return total + total * jnp.tanh(inner)

            for part in range(0, outs, 2):
                main = convolved(lifted[ch // 2], o0 + part, 2)
                if n == 0:
                    rest = convolved(over_rows[ch // 2], o0 + part, 1).astype(F32)
                    main = main.astype(F32)
                    main = jnp.concatenate([main[0:16], rest[0:8], main[16:32], rest[8:16]], axis=0).astype(BF16)
                side = slice(128 * (ch % 2), 128 * (ch % 2 + 1))
                hidden[ch // 2][high * part : high * (part + 2), side] = main

        product = halved if high * outs > 256 else dot
        down = None
        lift_up(0)
        for double in range(chunks // 2):
            if double + 1 < chunks // 2:
                lift_up(double + 1)
            convolve(2 * double)
            convolve(2 * double + 1)
            units = slice(256 * double, 256 * (double + 1))
            part = product(hidden[double][0 : high * outs], wdown[n, units, :])
            down = part if down is None else down + part
        if n == 0:
            xf[1, PITCH * (o0 + 3) : PITCH * (o0 + 3 + outs), :] = af[PITCH * o0 : PITCH * (o0 + outs)] + down
        else:
            for k in range(outs):
                at = PITCH * (o0 + k)
                out = af[at : at + 16] + down[16 * k : 16 * (k + 1)]
                af[at : at + 16] = out

    loads["gains"].wait()
    loads[0, 0].wait()
    wide = dot(pick_own, raw[...])
    kv, query = multiply(0, wide)
    spread(wide, kv, query, 0, 4, 8, 16)
    remotes[2].wait_recv()
    wide = stage[192:320].astype(F32)
    kv, query = multiply(0, wide)
    spread(wide, kv, query, 0, 3, 8, 16)
    loads["conv"].wait()
    for k in range(1, 4):
        loads[0, k].wait()
    feed(0, ((8, 4), (12, 4)), 8, 8, 9, 6)
    for k in (0, 1):
        remotes[k].wait_recv()

    @pl.when(eager & jnp.logical_not(first))
    def _():
        pl.semaphore_wait(here_sem, 2)

    @pl.when(jnp.logical_not(first | last))
    def _():
        for remote in remotes[3:]:
            remote.start()

    wide = stage[0:192].astype(F32)
    kv, query = multiply(0, wide)
    spread(wide, kv, query, 0, 4, 24, 8)
    spread(wide, kv, query, 128, 3, 24, 8)
    feed(0, ((16, 4), (20, 4), (24, 2)), 15, 11, 15, 10)
    for k in range(4):
        loads[1, k].wait()
    project(1, 12, 16, 9, 13)
    answer()
    feed(1, ((12, 4), (16, 4), (20, 2)), 12, 10, 13, 8)
    result[...] = dot(place[1, :, 0:192], af[PITCH * 13 : PITCH * 21].astype(BF16))
    for k in (3, 4):
        remotes[k].wait_recv()
    wide = stage[320:512].astype(F32)
    kv, query = multiply(0, wide)
    spread(wide, kv, query, 0, 4, 0, 8)
    spread(wide, kv, query, 128, 3, 0, 8)
    feed(0, ((0, 4), (4, 4)), 0, 9, 1, 8)
    project(1, 4, 8, 4, 5)
    feed(1, ((4, 4), (8, 4)), 4, 8, 5, 8)
    out_ref[...] = (result[...] + dot(place[0, :, 0:192], af[PITCH * 5 : PITCH * 13].astype(BF16))).astype(BF16)
    for remote in remotes:
        remote.wait_send()


def wide_call(n_lat, n_lon, stream, gains, table, conv, w_qkv, w_out, w_up, w_down):
    layers = w_qkv.shape[0]
    width = stream.shape[1]
    hid = w_up.shape[2]
    vmem = pl.BlockSpec(memory_space=pltpu.VMEM)
    anywhere = pl.BlockSpec(memory_space=pltpu.HBM)
    heads = table.shape[2]
    return pl.pallas_call(
        functools.partial(wide_kernel, n_lat, n_lon),
        out_shape=pltpu.VMEM(stream.shape, BF16),
        in_specs=[anywhere] * 8,
        out_specs=vmem,
        scratch_shapes=[
            pltpu.VMEM(gains.shape, F32),
            pltpu.VMEM(table.shape, F32),
            pltpu.VMEM(conv.shape, F32),
            pltpu.VMEM(w_qkv.shape, BF16),
            pltpu.VMEM(w_out.shape, BF16),
            pltpu.VMEM(w_up.shape, BF16),
            pltpu.VMEM(w_down.shape, BF16),
            pltpu.VMEM((256, width), BF16),
            pltpu.VMEM((512, width), BF16),
            pltpu.VMEM((512, width), BF16),
            pltpu.VMEM((layers, 32 * PITCH, width), F32),
            pltpu.VMEM((layers, 832, 2 * width), BF16),
            pltpu.VMEM((26 * PITCH, width), F32),
            pltpu.VMEM((26 * PITCH, width), F32),
            pltpu.VMEM((2, 26 * PITCH + 16, 128), F32),
            *[pltpu.VMEM((3, 2, 26 * 16, 128), BF16)] * (hid // 128),
            *[pltpu.VMEM((16 * PITCH, 256), BF16)] * (hid // 256),
            pltpu.VMEM((layers * heads, 128), F32),
            pltpu.VMEM((layers, heads, GROUP * PITCH, 256), F32),
            pltpu.VMEM((2, 256, 256), BF16),
            pltpu.VMEM((256, width), F32),
            pltpu.SemaphoreType.DMA((5,)),
            pltpu.SemaphoreType.DMA((layers, 4)),
            pltpu.SemaphoreType.DMA((5,)),
            pltpu.SemaphoreType.DMA((5,)),
            pltpu.SemaphoreType.REGULAR,
        ],
        compiler_params=pltpu.CompilerParams(
            collective_id=0, has_side_effects=True, vmem_limit_bytes=58 * 1024 * 1024
        ),
    )(stream, gains, table, conv, w_qkv, w_out, w_up, w_down)


def on_device(n_lat, n_lon, stream, gains, w_qkv, table, w_out, w_up, conv, w_down):
    rows, cols, width = stream.shape
    layers, heads = table.shape[:2]
    table = table.transpose(0, 3, 1, 2)
    conv = conv.transpose(1, 2, 0, 3)
    hid = w_up.shape[2]
    vmem = pl.BlockSpec(memory_space=pltpu.VMEM)
    anywhere = pl.BlockSpec(memory_space=pltpu.HBM)
    if n_lat == 2 and n_lon % 2 == 0 and n_lon > 2:
        result = wide_call(
            n_lat, n_lon, stream.reshape(rows * cols, width), gains, table, conv, w_qkv, w_out, w_up, w_down
        )
        return result.reshape(rows, cols, width)
    result = pl.pallas_call(
        functools.partial(kernel, n_lat, n_lon),
        out_shape=pltpu.VMEM((rows * cols, width), BF16),
        in_specs=[anywhere] * 8,
        out_specs=vmem,
        scratch_shapes=[
            pltpu.VMEM(gains.shape, F32),
            pltpu.VMEM(table.shape, F32),
            pltpu.VMEM(conv.shape, F32),
            pltpu.VMEM(w_qkv.shape, BF16),
            pltpu.VMEM(w_out.shape, BF16),
            pltpu.VMEM(w_up.shape, BF16),
            pltpu.VMEM(w_down.shape, BF16),
            pltpu.VMEM((384, 2 * width), BF16),
            pltpu.VMEM((96, 2 * width), BF16),
            pltpu.VMEM((96, 2 * width), BF16),
            pltpu.VMEM((layers, 384, width), BF16),
            pltpu.VMEM((layers, 96, width), BF16),
            pltpu.VMEM((layers, 96, width), BF16),
            pltpu.VMEM((layers, 128, width), BF16),
            pltpu.VMEM((288, hid), F32),
            pltpu.VMEM((256, hid), F32),
            pltpu.VMEM((WINDOW, layers * heads, 128), F32),
            pltpu.VMEM((WINDOW, layers * heads, 256), F32),
            pltpu.VMEM((layers, 3, 320, 256), F32),
            pltpu.VMEM((layers, 2, 128, 256), F32),
            pltpu.VMEM((384, width), BF16),
            pltpu.SemaphoreType.DMA((4,)),
            pltpu.SemaphoreType.DMA((layers, 4)),
            pltpu.SemaphoreType.DMA((layers, 8)),
            pltpu.SemaphoreType.DMA((layers, 8)),
        ],
        compiler_params=pltpu.CompilerParams(
            collective_id=0, has_side_effects=True, vmem_limit_bytes=58 * 1024 * 1024
        ),
    )(
        stream.reshape(rows * cols, width),
        gains,
        table,
        conv,
        w_qkv,
        w_out,
        w_up,
        w_down,
    )
    return result.reshape(rows, cols, width)


def solution(mesh):
    sizes = dict(mesh.shape)
    in_specs = (P("lat", "lon", None), P(), P(), P(), P(), P(), P(), P())
    return jax.shard_map(
        functools.partial(on_device, sizes["lat"], sizes["lon"]),
        mesh=mesh,
        in_specs=in_specs,
        out_specs=P("lat", "lon", None),
        check_vma=False,
    )
```
